512 devices in a mesh: gx: 16 (over z, x_lo), gy: 8 (over y), gz: 4 (over x_hi, core).
Axes of the slice: x: 4 (x_hi: 2, x_lo: 2; x = x_hi * 2 + x_lo), y: 8, z: 8, core: 2. Of those that a mesh axis runs over, the one named last changes fastest.
Arguments:
- block_input: bfloat16 [64, 64, 4096], P('gx', 'gy', 'gz'), may hold values from -6 to 6
- pre_act: bfloat16 [64, 64, 4096], P('gx', 'gy', 'gz'), may hold values from -6 to 6
- skip_grad: bfloat16 [64, 64, 4096], P('gx', 'gy', 'gz'), may hold values from -6 to 6
- pool_grad: bfloat16 [32, 32, 2048], P('gx', 'gy', 'gz'), may hold values from -6 to 6
- conv1_weight: bfloat16 [64, 1728], P('gx'), may hold values from -0.15625 to 0.15625
- conv2_weight: bfloat16 [64, 1728], P('gx'), may hold values from -0.15625 to 0.15625
Outputs:
- input_grad: bfloat16 [64, 64, 4096], P('gx', 'gy', 'gz')
- conv1_grad: float32 [64, 1728], P('gx')
- conv2_grad: float32 [64, 1728], P('gx')
The draws below stay inside these ranges and needn't reach their ends.
All inputs are finite; a program needn't handle non-finite values.
Results may differ from the reference program's by a relative error of at most 0.0053.
Values may be sent and summed in bfloat16 or wider, within the bound.
No kernel may reach another device: no remote copies, remote signals or barrier semaphores. Data moves between devices by JAX's collectives and lax.ppermute only.
A program may use at most 64 MiB of HBM per device.

```python
import jax
import jax.numpy as jnp
from jax import lax

C = 64
NX = 64
NY = 64
NZ = 64


def strengthened(entries, own_key, source, target, shards_of, factor):
    owner, partner = [(jnp.arange(entries.shape[axis_at]) // (entries.shape[axis_at] // shards_of)).reshape([-1 if axis == axis_at else 1 for axis in range(entries.ndim)]) for axis_at in (source, target)]
    chosen = jax.random.permutation(own_key, shards_of)[partner]
    strong = (owner == chosen) | (owner == (partner + shards_of // 2) % shards_of)
    return jnp.where(strong, factor * entries, entries)


def levels(own_key, dims, pieces, low, top_value):
    gain, own = 1.0, jax.random.fold_in(own_key, 6)
    for dim, parts in pieces:
        heights = jnp.exp(jax.random.uniform(jax.random.fold_in(own, dim), (parts,), jnp.float32, low / len(pieces), top_value / len(pieces)))
        gain = gain * jnp.repeat(heights, dims[dim] // parts).reshape([-1 if axis == dim else 1 for axis in range(len(dims))])
    return gain


def gaussian(rng, shape, scale, most, cuts=(), kind=jnp.bfloat16):
    array = scale * jax.random.normal(rng, shape, jnp.float32)
    if cuts:
        array = array * levels(rng, shape, cuts, -0.22, 0.18)
    return jnp.clip(array, -most, most).astype(kind)


def heavy_noise(key, dims, spread, bound, shards, heavy, held_as=jnp.bfloat16):
    drawn = spread * jax.random.normal(key, dims, jnp.float32)
    if shards:
        drawn = drawn * levels(key, dims, shards, -0.22, 0.18)
    return jnp.clip(strengthened(drawn, jax.random.fold_in(key, 3), *heavy), -bound, bound).astype(held_as)


def setup_inputs(seed: int = 0) -> dict:
    arg_keys = jax.random.split(jax.random.key(seed), 7)
    return {
        "block_input": gaussian(arg_keys[0], (NX, NY, NZ * C), 1.0, 6.0, ((0, 16), (1, 8), (2, 4))),
        "pre_act": gaussian(arg_keys[1], (NX, NY, NZ * C), 1.5, 6.0, ((0, 16), (1, 8), (2, 4))),
        "skip_grad": heavy_noise(arg_keys[2], (NX, NY, NZ * C), 1.0, 6.0, ((0, 16), (1, 8), (2, 4)), (0, 2, 16, 2.0)),
        "pool_grad": gaussian(arg_keys[3], (NX // 2, NY // 2, NZ // 2 * C), 1.0, 6.0, ((0, 16), (1, 8), (2, 4))),
        "conv1_weight": gaussian(arg_keys[4], (C, 27 * C), (27 * C) ** -0.5, 0.15625, ((0, 16),)),
        "conv2_weight": gaussian(arg_keys[5], (C, 27 * C), (27 * C) ** -0.5, 0.15625, ((0, 16),)),
    }


def offset_of(k):
    return (k // 9 - 1, k // 3 % 3 - 1, k % 3 - 1)

def silu_slope(v):
    g = jax.nn.sigmoid(v)
    return g * (1.0 + v * (1.0 - g))

def reference(block_input, pre_act, skip_grad, pool_grad, conv1_weight, conv2_weight):
    chans = conv1_weight.shape[0]
    grid_shape = (NX, NY, NZ, chans)
    input_four = block_input.reshape(grid_shape)
    pre_four = pre_act.reshape(grid_shape).astype(jnp.float32)
    skip_four = skip_grad.reshape(grid_shape).astype(jnp.float32)
    pool_four = pool_grad.reshape(NX // 2, NY // 2, NZ // 2, chans).astype(jnp.float32)
    upsampled = jnp.repeat(jnp.repeat(jnp.repeat(pool_four, 2, axis=0), 2, axis=1), 2, axis=2)
    out_grad = (skip_four + 0.125 * upsampled).astype(jnp.bfloat16)
    act = jax.nn.silu(pre_four).astype(jnp.bfloat16)
    scale_all = 1.0 / jnp.sqrt(jnp.float32(NX * NY * NZ))
    out_flat = out_grad.reshape(-1, chans)
    grads_two = []
    act_grad = jnp.zeros((NX * NY * NZ, chans), jnp.float32)
    for k in range(27):
        d = offset_of(k)
        ahead = jnp.roll(act, (-d[0], -d[1], -d[2]), axis=(0, 1, 2)).reshape(-1, chans)
        grads_two.append(lax.dot_general(out_flat, ahead, (((0,), (0,)), ((), ())), preferred_element_type=jnp.float32))
        behind = jnp.roll(out_grad, (d[0], d[1], d[2]), axis=(0, 1, 2)).reshape(-1, chans)
        block = conv2_weight[:, k * chans:(k + 1) * chans]
        act_grad = act_grad + lax.dot_general(behind, block, (((1,), (0,)), ((), ())), preferred_element_type=jnp.float32)
    pre_grad = (act_grad * silu_slope(pre_four).reshape(-1, chans)).astype(jnp.bfloat16)
    pre_grid = pre_grad.reshape(grid_shape)
    grads_one = []
    total = out_grad.astype(jnp.float32).reshape(-1, chans)
    for k in range(27):
        d = offset_of(k)
        ahead = jnp.roll(input_four, (-d[0], -d[1], -d[2]), axis=(0, 1, 2)).reshape(-1, chans)
        grads_one.append(lax.dot_general(pre_grad, ahead, (((0,), (0,)), ((), ())), preferred_element_type=jnp.float32))
        behind = jnp.roll(pre_grid, (d[0], d[1], d[2]), axis=(0, 1, 2)).reshape(-1, chans)
        block = conv1_weight[:, k * chans:(k + 1) * chans]
        total = total + lax.dot_general(behind, block, (((1,), (0,)), ((), ())), preferred_element_type=jnp.float32)
    input_grad = total.reshape(NX, NY, NZ * chans).astype(jnp.bfloat16)
    conv1_grad = jnp.concatenate(grads_one, axis=1) * scale_all
    conv2_grad = jnp.concatenate(grads_two, axis=1) * scale_all
    return (input_grad, conv1_grad, conv2_grad)
```

```python
import math

import jax
import jax.numpy as jnp
from jax import lax
from jax.sharding import PartitionSpec as P


def padded_2(block, sides, width):
    for axis, dim in sides:
        count = lax.axis_size(axis)
        forward = [(i, i + 1) for i in range(count - 1)]
        forward.append((count - 1, 0))
        backward = [(target, source) for source, target in forward]
        low = lax.ppermute(
            lax.slice_in_dim(block, block.shape[dim] - width, None, axis=dim), axis, forward
        )
        high = lax.ppermute(lax.slice_in_dim(block, 0, width, axis=dim), axis, backward)
        block = jnp.concatenate([low, block, high], axis=dim)
    return block


def offset_of(k):
    return (k // 9 - 1, k // 3 % 3 - 1, k % 3 - 1)


def silu_slope(v):
    g = jax.nn.sigmoid(v)
    return g * (1.0 + v * (1.0 - g))


def window(padded, start, shape):
    lower = (start[0], start[1], start[2], 0)
    upper = (start[0] + shape[0], start[1] + shape[1], start[2] + shape[2], padded.shape[3])
    return lax.slice(padded, lower, upper).reshape(-1, padded.shape[3])


def transpose_conv(weight, padded, margin, shape):
    chans = weight.shape[0]
    total = None
    for k in range(27):
        d = offset_of(k)
        behind = window(padded, (margin - d[0], margin - d[1], margin - d[2]), shape)
        block = weight[:, k * chans : (k + 1) * chans]
        term = lax.dot_general(
            behind, block, (((1,), (0,)), ((), ())), preferred_element_type=jnp.float32
        )
        total = term if total is None else total + term
    return total


def weight_grad(left_flat, padded, margin, shape):
    pieces = []
    for k in range(27):
        d = offset_of(k)
        ahead = window(padded, (margin + d[0], margin + d[1], margin + d[2]), shape)
        pieces.append(
            lax.dot_general(
                left_flat, ahead, (((0,), (0,)), ((), ())), preferred_element_type=jnp.float32
            )
        )
    return jnp.concatenate(pieces, axis=1)


def reduced(grads):
    count = lax.axis_size("gx")
    rows = grads.shape[0] // count
    slots = grads.astype(jnp.bfloat16).reshape(count, rows, grads.shape[1])
    part = lax.all_to_all(slots, "gx", 0, 0, tiled=True).astype(jnp.float32).sum(0)
    part = lax.all_gather(part, "gz", axis=0).sum(0)
    spread = jnp.broadcast_to(part[None], (lax.axis_size("gy"),) + part.shape)
    return lax.all_to_all(spread, "gy", 0, 0, tiled=True).sum(0)


def body(block_input, pre_act, skip_grad, pool_grad, conv1_weight, conv2_weight):
    chans = conv1_weight.shape[1] // 27
    size_x, size_y, merged = block_input.shape
    size_z = merged // chans
    inner = (size_x, size_y, size_z)
    four_shape = (size_x, size_y, size_z, chans)
    both = jnp.concatenate([conv1_weight, conv2_weight], axis=1)
    spread = jnp.broadcast_to(both[None], (lax.axis_size("gx"),) + both.shape)
    gathered = lax.all_to_all(spread, "gx", 0, 0, tiled=True).reshape(chans, -1)
    weight_one, weight_two = gathered[:, : 27 * chans], gathered[:, 27 * chans :]
    pool_four = pool_grad.reshape(size_x // 2, size_y // 2, size_z // 2, chans).astype(jnp.float32)
    upsampled = jnp.repeat(jnp.repeat(jnp.repeat(pool_four, 2, axis=0), 2, axis=1), 2, axis=2)
    out_grad = (skip_grad.reshape(four_shape).astype(jnp.float32) + 0.125 * upsampled).astype(
        jnp.bfloat16
    )
    out_flat = out_grad.reshape(-1, chans)
    input_four = block_input.reshape(four_shape)
    pre_four = pre_act.reshape(four_shape)
    stacked = jnp.concatenate([input_four, pre_four, out_grad], axis=3)
    padded = padded_2(stacked, (("gx", 0), ("gy", 1), ("gz", 2)), 1)
    input_pad = padded[..., :chans]
    act_pad = jax.nn.silu(padded[..., chans : 2 * chans].astype(jnp.float32)).astype(jnp.bfloat16)
    grad_pad = padded[..., 2 * chans :]
    grads_two = weight_grad(out_flat, act_pad, 1, inner)
    act_grad = transpose_conv(weight_two, grad_pad, 1, inner)
    slope = silu_slope(pre_four.astype(jnp.float32)).reshape(-1, chans)
    pre_grad = (act_grad * slope).astype(jnp.bfloat16).reshape(four_shape)
    pre_pad = padded_2(pre_grad, (("gx", 0), ("gy", 1), ("gz", 2)), 1)
    pre_flat = pre_grad.reshape(-1, chans)
    grads_one = weight_grad(pre_flat, input_pad, 1, inner)
    total = out_grad.astype(jnp.float32).reshape(-1, chans) + transpose_conv(
        weight_one, pre_pad, 1, inner
    )
    input_grad = total.reshape(size_x, size_y, merged).astype(jnp.bfloat16)
    cells_all = (
        inner[0]
        * inner[1]
        * inner[2]
        * lax.axis_size("gx")
        * lax.axis_size("gy")
        * lax.axis_size("gz")
    )
    scale_all = 1.0 / math.sqrt(cells_all)
    grads_one = grads_one * scale_all
    grads_two = grads_two * scale_all
    summed = reduced(jnp.concatenate([grads_one, grads_two], axis=1))
    conv1_grad, conv2_grad = summed[:, : 27 * chans], summed[:, 27 * chans :]
    return (input_grad, conv1_grad, conv2_grad)


def solution(mesh):
    in_specs = (
        P("gx", "gy", "gz"),
        P("gx", "gy", "gz"),
        P("gx", "gy", "gz"),
        P("gx", "gy", "gz"),
        P("gx", None),
        P("gx", None),
    )
    out_specs = (P("gx", "gy", "gz"), P("gx", None), P("gx", None))
    return jax.shard_map(body, mesh=mesh, in_specs=in_specs, out_specs=out_specs, check_vma=False)
```

```python
import functools
import math

import jax
import jax.numpy as jnp
from jax import lax
from jax.experimental import pallas as pl
from jax.experimental.pallas import tpu as pltpu
from jax.sharding import PartitionSpec as P

F32, B16 = jnp.float32, jnp.bfloat16
SX, SY, SZ, CH = 4, 8, 16, 64
LANES = SZ * CH
ROWS = 16 * (SX + 5)
WIDE = LANES + 6 * CH
BAND = 6 * CH
DEPTH = 9 * BAND
OWN = 16 * 3
HALO_ROWS = 16 * (SX + 3)
LAYERS = 20


def vmem():
    return pl.BlockSpec(memory_space=pltpu.VMEM)


def call(kernel, outs, scratch, flops, moved, *args):
    return pl.pallas_call(
        kernel,
        out_shape=[jax.ShapeDtypeStruct(shape, dtype) for shape, dtype in outs],
        in_specs=[vmem()] * len(args),
        out_specs=[vmem()] * len(outs),
        scratch_shapes=[pltpu.VMEM(shape, dtype) for shape, dtype in scratch],
        compiler_params=pltpu.CompilerParams(vmem_limit_bytes=48 * 1024 * 1024),
        cost_estimate=pl.CostEstimate(flops=flops, bytes_accessed=moved, transcendentals=0),
    )(*args)


def low_half(shape):
    return lax.broadcasted_iota(jnp.int32, shape, len(shape) - 1) % 128 < 64


def prep_kernel(skip, pool, pre, inp, grad, low, high, up):
    for px in range(SX // 2):
        pieces = []
        for j in range(LANES // 256):
            v = pool[px, :, 128 * j : 128 * (j + 1)].astype(F32)
            turned = pltpu.roll(v, 64, 1)
            first = low_half(v.shape)
            pieces += [jnp.where(first, v, turned), jnp.where(first, turned, v)]
        for y in range(SY):
            for j, piece in enumerate(pieces):
                up[px, y : y + 1, 128 * j : 128 * (j + 1)] = piece[y // 2 : y // 2 + 1, :]
    for x in range(SX):
        value = (skip[x].astype(F32) + 0.125 * up[x // 2]).astype(B16)
        grad[x] = value
        if x < 2:
            low[x] = value
        else:
            high[x - 2] = value
    low[2], low[3] = pre[0], inp[0]
    high[2], high[3] = pre[SX - 1], inp[SX - 1]


def layer_list(grad, pre, inp, xlo, xhi):
    def own(ref):
        return [(ref, x) for x in range(SX)]

    return (
        [(xlo, 0), (xlo, 1)] + own(grad) + [(xhi, 0), (xhi, 1)]
        + [(xlo, 2)] + own(pre) + [(xhi, 2)]
        + [(xlo, 3)] + own(inp) + [(xhi, 3)]
    )


def ypack_kernel(grad, pre, inp, xlo, xhi, low, high):
    for at, (ref, x) in enumerate(layer_list(grad, pre, inp, xlo, xhi)):
        value = ref[x].astype(F32)
        low[at] = value[0:2].astype(B16)
        high[at] = value[SY - 2 : SY].astype(B16)


def zpack_kernel(grad, pre, inp, xlo, xhi, ylo, yhi, low, high, held):
    for out, lane in ((low, 0), (high, LANES - 128)):
        for at, (ref, x) in enumerate(layer_list(grad, pre, inp, xlo, xhi)):
            held[at, 0:2] = ylo[at, :, lane : lane + 128].astype(F32)
            held[at, 2:10] = ref[x, :, lane : lane + 128].astype(F32)
            held[at, 10:12] = yhi[at, :, lane : lane + 128].astype(F32)
        out[...] = held[...].astype(B16)


def bands_kernel(weights, one, two, flat, turned):
    count, rows = weights.shape[0], weights.shape[1]
    flat[...] = jnp.zeros_like(flat)
    for g in range(count):
        flat[g * rows : (g + 1) * rows, 256 : 256 + 54 * CH] = weights[g].astype(F32)
    turned[...] = pltpu.roll(flat[...], flat.shape[1] - 64, 1)
    block = lax.broadcasted_iota(jnp.int32, (CH, 256), 1) // CH
    for which, out in enumerate((one, two)):
        for m in range(9):
            for a in range(6):
                at = 4 + 27 * which + 3 * m + 2 - a
                source = turned if at % 2 else flat
                lane = at // 2 * 128
                valid = (block + 2 - a >= 0) & (block - a <= 0)
                value = jnp.where(valid, source[:, lane : lane + 256], 0.0)
                out[m * BAND + a * CH : m * BAND + (a + 1) * CH, :] = value.astype(B16)


def fill(field, layers, first, x0, ylo, yhi, zlo, zhi):
    field[...] = jnp.zeros_like(field)
    for j, (ref, x) in enumerate(layers):
        at, row = first + j, 16 * (x0 + j + 1)
        field[row : row + 8, 128 : 128 + LANES] = ref[x].astype(F32)
        field[row - 2 : row, 128 : 128 + LANES] = ylo[at].astype(F32)
        field[row + 8 : row + 10, 128 : 128 + LANES] = yhi[at].astype(F32)
        for side, lane in ((zlo, 0), (zhi, 128 + LANES)):
            value = side[at].astype(F32)
            field[row - 2 : row, lane : lane + 128] = value[0:2]
            field[row : row + 8, lane : lane + 128] = value[2:10]
            field[row + 8 : row + 10, lane : lane + 128] = value[10:12]


def spread(value, steps, sign):
    moved = pltpu.roll(value, 64, 1)
    for i, dy in enumerate((-1, 0, 1)):
        by = (-sign * dy) % ROWS
        steps[i] = (pltpu.roll(moved, by, 0) if by else moved).astype(B16)


def own_columns(steps, columns, sign):
    for m in range(9):
        dx, dy = m // 3 - 1, m % 3
        row = OWN + sign * 16 * dx
        for h in range(4):
            columns[64 * h : 64 * (h + 1), BAND * m : BAND * (m + 1)] = steps[
                dy, row : row + 64, 256 * h + 128 : 256 * h + 128 + BAND
            ]


def main_kernel(scale, grad, pre, inp, xlo, xhi, ylo, yhi, zlo, zhi, band,
                slots, pre_out, fg, fa, fi, steps, columns, many, left, left_f, grads_one, grads_two, held):
    layers = layer_list(grad, pre, inp, xlo, xhi)
    halos = (ylo, yhi, zlo, zhi)
    fill(fg, layers[0:8], 0, 0, *halos)
    fill(fa, layers[8:14], 8, 1, *halos)
    fill(fi, layers[14:20], 14, 1, *halos)
    contract = (((0,), (0,)), ((), ()))

    v = fa[...]
    spread((v * jax.nn.sigmoid(v)).astype(B16).astype(F32), steps, 1)
    own_columns(steps, columns, 1)
    left_f[...] = jnp.zeros_like(left_f)
    for h in range(4):
        for x in range(SX):
            row = 64 * h + 16 * x
            left_f[row : row + 8, :] = grad[x, :, 256 * h : 256 * (h + 1)].astype(F32)
    left[...] = left_f[...].astype(B16)
    grads_two[...] = lax.dot_general(left[...], columns[...], contract, preferred_element_type=F32)

    spread(fg[...], steps, -1)
    for m in range(9):
        dx, dy = m // 3 - 1, m % 3
        row = 16 - 16 * dx
        for h in range(5):
            many[HALO_ROWS * h : HALO_ROWS * (h + 1), BAND * m : BAND * (m + 1)] = steps[
                dy, row : row + HALO_ROWS, 256 * h : 256 * h + BAND
            ]
    held[...] = jnp.dot(many[...], band[...], preferred_element_type=F32)
    fg[...] = jnp.zeros_like(fg)
    for h in range(5):
        v = fa[16 : 16 + HALO_ROWS, 256 * h : 256 * (h + 1)]
        g = jax.nn.sigmoid(v)
        value = held[HALO_ROWS * h : HALO_ROWS * (h + 1), :] * (g * (1.0 + v * (1.0 - g)))
        fg[16 : 16 + HALO_ROWS, 256 * h : 256 * (h + 1)] = value.astype(B16).astype(F32)
    pre_out[...] = pltpu.roll(fg[...], 64, 1).astype(B16)

    spread(fi[...], steps, 1)
    own_columns(steps, columns, 1)
    inside = lax.broadcasted_iota(jnp.int32, (64, 256), 0) % 16 < 8
    for h in range(4):
        value = fg[OWN : OWN + 64, 256 * h + 128 : 256 * h + 384]
        left[64 * h : 64 * (h + 1), :] = jnp.where(inside, value, 0.0).astype(B16)
    grads_one[...] = lax.dot_general(left[...], columns[...], contract, preferred_element_type=F32)

    count, rows = slots.shape[0], slots.shape[1]

    def block(kk):
        k, source = (kk, grads_one) if kk < 27 else (kk - 27, grads_two)
        m, t = k // 3, k % 3
        same, other = [], []
        for b in range(4):
            lane = (6 * m + b + t) // 2 * 128
            piece = source[64 * b : 64 * (b + 1), lane : lane + 128]
            (same if (b + t) % 2 == kk % 2 else other).append(piece)
        return (same[0] + same[1]) + pltpu.roll(other[0] + other[1], 64, 1)

    for j in range(27):
        first, second = block(2 * j), block(2 * j + 1)
        value = jnp.where(low_half(first.shape), first, second) * scale
        for g in range(count):
            slots[g, :, 128 * j : 128 * (j + 1)] = value[g * rows : (g + 1) * rows, :].astype(B16)


def last_kernel(pre_grad, grad, band, out, steps, columns, held):
    value = pre_grad[...].astype(F32)
    for i, dy in enumerate((-1, 0, 1)):
        steps[i] = (pltpu.roll(value, dy % ROWS, 0) if dy else value).astype(B16)
    own_columns(steps, columns, -1)
    held[...] = jnp.dot(columns[...], band[...], preferred_element_type=F32)
    for h in range(4):
        for x in range(SX):
            row, lanes = 64 * h + 16 * x, slice(256 * h, 256 * (h + 1))
            out[x, :, lanes] = (held[row : row + 8, :] + grad[x, :, lanes].astype(F32)).astype(B16)


def swapped(low, high, axis):
    count = lax.axis_size(axis)
    up = [(i, (i + 1) % count) for i in range(count)]
    down = [(target, source) for source, target in up]
    return lax.ppermute(high, axis, up), lax.ppermute(low, axis, down)


def reduced(slots):
    part = lax.all_to_all(slots, "gx", 0, 0, tiled=True).astype(F32).sum(0)
    part = lax.all_gather(part, "gz", axis=0).sum(0)
    copies = jnp.broadcast_to(part[None].astype(B16), (lax.axis_size("gy"),) + part.shape)
    return lax.all_to_all(copies, "gy", 0, 0, tiled=True).astype(F32).sum(0)


def body(block_input, pre_act, skip_grad, pool_grad, conv1_weight, conv2_weight):
    count = lax.axis_size("gx")
    rows = CH // count
    cells = SX * SY * SZ * count * lax.axis_size("gy") * lax.axis_size("gz")
    message = ((4, SY, LANES), B16)
    grad, low, high = call(
        prep_kernel,
        [((SX, SY, LANES), B16), message, message],
        [((SX // 2, SY, LANES), F32)],
        100000, 400000,
        skip_grad, pool_grad, pre_act, block_input,
    )
    xlo, xhi = swapped(low, high, "gx")
    both = jnp.concatenate([conv1_weight, conv2_weight], axis=1)
    copies = jnp.broadcast_to(both[None], (count,) + both.shape)
    gathered = lax.all_to_all(copies, "gx", 0, 0, tiled=True)
    fields = (grad, pre_act, block_input, xlo, xhi)
    message = ((LAYERS, 2, LANES), B16)
    ylo, yhi = swapped(*call(ypack_kernel, [message, message], [], 100000, 600000, *fields), "gy")
    message = ((LAYERS, 12, 128), B16)
    zlo, zhi = swapped(
        *call(zpack_kernel, [message, message], [((LAYERS, 12, 128), F32)], 100000, 700000, *fields, ylo, yhi),
        "gz",
    )
    matrix = ((DEPTH, 256), B16)
    flat = ((CH, 54 * CH + 512), F32)
    band_one, band_two = call(bands_kernel, [matrix, matrix], [flat, flat], 1000000, 4000000, gathered)
    field = ((ROWS, WIDE), F32)
    steps = ((3, ROWS, WIDE), B16)
    columns = ((256, DEPTH), B16)
    slots, pre_grad = call(
        functools.partial(main_kernel, 1.0 / math.sqrt(cells)),
        [((count, rows, 54 * CH), B16), ((ROWS, WIDE), B16)],
        [
            field, field, field, steps, columns,
            ((5 * HALO_ROWS, DEPTH), B16), ((256, 256), B16), ((256, 256), F32),
            ((256, DEPTH), F32), ((256, DEPTH), F32), ((5 * HALO_ROWS, 256), F32),
        ],
        2 * 900 * 1000 * 1000, 8000000,
        *fields, ylo, yhi, zlo, zhi, band_two,
    )
    (input_grad,) = call(
        last_kernel,
        [((SX, SY, LANES), B16)],
        [steps, columns, ((256, 256), F32)],
        500000000, 4000000,
        pre_grad, grad, band_one,
    )
    summed = reduced(slots)
    return input_grad, summed[:, : 27 * CH], summed[:, 27 * CH :]


def solution(mesh):
    in_specs = (
        P("gx", "gy", "gz"),
        P("gx", "gy", "gz"),
        P("gx", "gy", "gz"),
        P("gx", "gy", "gz"),
        P("gx", None),
        P("gx", None),
    )
    out_specs = (P("gx", "gy", "gz"), P("gx", None), P("gx", None))
    return jax.shard_map(body, mesh=mesh, in_specs=in_specs, out_specs=out_specs, check_vma=False)
```

```python
import functools
import math

import jax
import jax.numpy as jnp
from jax import lax
from jax.experimental import pallas as pl
from jax.experimental.pallas import tpu as pltpu
from jax.sharding import PartitionSpec as P

F32, B16 = jnp.float32, jnp.bfloat16
SX, SY, SZ, CH = 4, 8, 16, 64
LANES = SZ * CH
ROWS = 16 * (SX + 5)
WIDE = LANES + 6 * CH
BAND = 6 * CH
DEPTH = 9 * BAND
OWN = 16 * 3
HALO_ROWS = 16 * (SX + 3)
LAYERS = 14
SPLIT = 4
PART = 7 * 128


def call(kernel, outs, scratch, flops, moved, *args, space=pltpu.VMEM, grant=48):
    return pl.pallas_call(
        kernel,
        out_shape=[jax.ShapeDtypeStruct(shape, dtype) for shape, dtype in outs],
        in_specs=[pl.BlockSpec(memory_space=space)] * len(args),
        out_specs=[pl.BlockSpec(memory_space=pltpu.VMEM)] * len(outs),
        scratch_shapes=[pltpu.VMEM(*held) if isinstance(held, tuple) else held for held in scratch],
        compiler_params=pltpu.CompilerParams(vmem_limit_bytes=grant * 1024 * 1024),
        cost_estimate=pl.CostEstimate(flops=flops, bytes_accessed=moved, transcendentals=0),
    )(*args)


def low_half(shape):
    return lax.broadcasted_iota(jnp.int32, shape, len(shape) - 1) % 128 < 64


def prep_kernel(skip_in, pool_in, pre_in, inp_in, one_in, two_in,
                grad, pre, inp, low, high, copies, skip, pool, one, two, up, rows, sems):
    moves = [
        pltpu.make_async_copy(source, target, sems.at[i])
        for i, (source, target) in enumerate(
            ((skip_in, skip), (pool_in, pool), (pre_in, pre), (inp_in, inp), (one_in, one), (two_in, two))
        )
    ]
    for move in moves:
        move.start()
    for move in moves:
        move.wait()
    each = one.shape[0]
    rows[0:each], rows[each : 2 * each] = one[...].astype(F32), two[...].astype(F32)
    both = rows[...].astype(B16)
    for g in range(copies.shape[0]):
        copies[g] = both
    for px in range(SX // 2):
        pieces = []
        for j in range(LANES // 256):
            v = pool[px, :, 128 * j : 128 * (j + 1)].astype(F32)
            turned = pltpu.roll(v, 64, 1)
            first = low_half(v.shape)
            pieces += [jnp.where(first, v, turned), jnp.where(first, turned, v)]
        for y in range(SY):
            for j, piece in enumerate(pieces):
                up[px, y : y + 1, 128 * j : 128 * (j + 1)] = piece[y // 2 : y // 2 + 1, :]
    for x in range(SX):
        value = (skip[x].astype(F32) + 0.125 * up[x // 2]).astype(B16)
        grad[x] = value
        if x < 2:
            low[x] = value
        else:
            high[x - 2] = value
    low[2], low[3] = pre[0], inp[0]
    high[2], high[3] = pre[SX - 1], inp[SX - 1]


def fields_of(grad, pre, inp, xlo, xhi):
    def own(ref):
        return [(ref, x) for x in range(SX)]

    return (
        [(xlo, 0), (xlo, 1)] + own(grad) + [(xhi, 0), (xhi, 1)],
        [(xlo, 2)] + own(pre) + [(xhi, 2)],
        [(xlo, 3)] + own(inp) + [(xhi, 3)],
    )


def ypack_kernel(grad, pre, inp, xlo, xhi, low, high, held):
    wide, acts, inputs = fields_of(grad, pre, inp, xlo, xhi)
    for at, (ref, x) in enumerate(wide):
        value = ref[x].astype(F32)
        low[at] = value[0:2].astype(B16)
        high[at] = value[SY - 2 : SY].astype(B16)
    for out, row in ((low, 0), (high, SY - 1)):
        for at, ((a, ax), (i, ix)) in enumerate(zip(acts, inputs)):
            held[0:1] = a[ax].astype(F32)[row : row + 1]
            held[1:2] = i[ix].astype(F32)[row : row + 1]
            out[8 + at] = held[...].astype(B16)


def zpack_kernel(grad, pre, inp, xlo, xhi, ylo, yhi, low, high, held, second):
    wide, acts, inputs = fields_of(grad, pre, inp, xlo, xhi)
    for out, lane, half in ((low, 0, True), (high, LANES - 128, False)):
        cut = slice(lane, lane + 128)
        for at, (ref, x) in enumerate(wide):
            held[at, 0:2] = ylo[at, :, cut].astype(F32)
            held[at, 2:10] = ref[x, :, cut].astype(F32)
            held[at, 10:12] = yhi[at, :, cut].astype(F32)
        for j, ((a, ax), (i, ix)) in enumerate(zip(acts, inputs)):
            at = 8 + j
            below, above = ylo[at, :, cut].astype(F32), yhi[at, :, cut].astype(F32)
            for to, ref, x, row in ((held.at[at], a, ax, 0), (second, i, ix, 1)):
                to[1:2] = below[row : row + 1]
                to[2:10] = ref[x, :, cut].astype(F32)
                to[10:11] = above[row : row + 1]
            v, w = held[at], second[...]
            if half:
                w = pltpu.roll(w, 64, 1)
            else:
                v = pltpu.roll(v, 64, 1)
            held[at] = jnp.where(low_half(v.shape), v, w)
        out[...] = held[...].astype(B16)


def bands_kernel(weights, one, two, flat, turned):
    count, rows = weights.shape[0], weights.shape[1] // 2
    block = lax.broadcasted_iota(jnp.int32, (CH, 256), 1) // CH
    for which, out in enumerate((one, two)):
        flat[...] = jnp.zeros_like(flat)
        for g in range(count):
            value = weights[g].astype(F32)[which * rows : (which + 1) * rows]
            flat[g * rows : (g + 1) * rows, 256 : 256 + 27 * CH] = value
        turned[...] = pltpu.roll(flat[...], flat.shape[1] - 64, 1)
        for m in range(9):
            for a in range(6):
                at = 4 + 3 * m + 2 - a
                source = turned if at % 2 else flat
                lane = at // 2 * 128
                valid = (block + 2 - a >= 0) & (block - a <= 0)
                value = jnp.where(valid, source[:, lane : lane + 256], 0.0)
                out[m * BAND + a * CH : m * BAND + (a + 1) * CH, :] = value.astype(B16)


def fill_wide(field, layers, ylo, yhi, zlo, zhi):
    field[...] = jnp.zeros_like(field)
    for at, (ref, x) in enumerate(layers):
        row = 16 * (at + 1)
        field[row : row + 8, 128 : 128 + LANES] = ref[x].astype(F32)
        field[row - 2 : row, 128 : 128 + LANES] = ylo[at].astype(F32)
        field[row + 8 : row + 10, 128 : 128 + LANES] = yhi[at].astype(F32)
        for side, lane in ((zlo, 0), (zhi, 128 + LANES)):
            value = side[at].astype(F32)
            field[row - 2 : row, lane : lane + 128] = value[0:2]
            field[row : row + 8, lane : lane + 128] = value[2:10]
            field[row + 8 : row + 10, lane : lane + 128] = value[10:12]


def fill_thin(field, layers, second, ylo, yhi, zlo, zhi):
    field[...] = jnp.zeros_like(field)
    for j, (ref, x) in enumerate(layers):
        at, row = 8 + j, 16 * (j + 2)
        field[row : row + 8, 128 : 128 + LANES] = ref[x].astype(F32)
        field[row - 1 : row, 128 : 128 + LANES] = ylo[at].astype(F32)[second : second + 1]
        field[row + 8 : row + 9, 128 : 128 + LANES] = yhi[at].astype(F32)[second : second + 1]
        for side, lane, upper in ((zlo, 0, True), (zhi, 128 + LANES, False)):
            value = side[at].astype(F32)
            if upper != bool(second):
                value = pltpu.roll(value, 64, 1)
            value = jnp.where(low_half(value.shape) != upper, value, 0.0)
            field[row - 1 : row, lane : lane + 128] = value[1:2]
            field[row : row + 8, lane : lane + 128] = value[2:10]
            field[row + 8 : row + 9, lane : lane + 128] = value[10:11]


def spread(value, steps, sign):
    moved = pltpu.roll(value, 64, 1)
    for i, dy in enumerate((-1, 0, 1)):
        by = (-sign * dy) % ROWS
        steps[i] = (pltpu.roll(moved, by, 0) if by else moved).astype(B16)


def own_columns(steps, columns, sign):
    for m in range(9):
        dx, dy = m // 3 - 1, m % 3
        row = OWN + sign * 16 * dx
        for h in range(4):
            columns[64 * h : 64 * (h + 1), BAND * m : BAND * (m + 1)] = steps[
                dy, row : row + 64, 256 * h + 128 : 256 * h + 128 + BAND
            ]


def main_kernel(scale, grad, pre, inp, xlo, xhi, ylo, yhi, zlo, zhi, band,
                slots, pre_out, fg, fa, fi, steps, columns, many, left, left_f, grads_one, grads_two, held):
    wide, acts, inputs = fields_of(grad, pre, inp, xlo, xhi)
    halos = (ylo, yhi, zlo, zhi)
    fill_wide(fg, wide, *halos)
    fill_thin(fa, acts, 0, *halos)
    fill_thin(fi, inputs, 1, *halos)
    contract = (((0,), (0,)), ((), ()))

    v = fa[...]
    spread((v * jax.nn.sigmoid(v)).astype(B16).astype(F32), steps, 1)
    own_columns(steps, columns, 1)
    left_f[...] = jnp.zeros_like(left_f)
    for h in range(4):
        for x in range(SX):
            row = 64 * h + 16 * x
            left_f[row : row + 8, :] = grad[x, :, 256 * h : 256 * (h + 1)].astype(F32)
    left[...] = left_f[...].astype(B16)
    grads_two[...] = lax.dot_general(left[...], columns[...], contract, preferred_element_type=F32)

    spread(fg[...], steps, -1)
    for m in range(9):
        dx, dy = m // 3 - 1, m % 3
        row = 16 - 16 * dx
        for h in range(5):
            many[HALO_ROWS * h : HALO_ROWS * (h + 1), BAND * m : BAND * (m + 1)] = steps[
                dy, row : row + HALO_ROWS, 256 * h : 256 * h + BAND
            ]
    held[...] = jnp.dot(many[...], band[...], preferred_element_type=F32)
    fg[...] = jnp.zeros_like(fg)
    for h in range(5):
        v = fa[16 : 16 + HALO_ROWS, 256 * h : 256 * (h + 1)]
        g = jax.nn.sigmoid(v)
        value = held[HALO_ROWS * h : HALO_ROWS * (h + 1), :] * (g * (1.0 + v * (1.0 - g)))
        fg[16 : 16 + HALO_ROWS, 256 * h : 256 * (h + 1)] = value.astype(B16).astype(F32)
    pre_out[...] = pltpu.roll(fg[...], 64, 1).astype(B16)

    spread(fi[...], steps, 1)
    own_columns(steps, columns, 1)
    inside = lax.broadcasted_iota(jnp.int32, (64, 256), 0) % 16 < 8
    for h in range(4):
        value = fg[OWN : OWN + 64, 256 * h + 128 : 256 * h + 384]
        left[64 * h : 64 * (h + 1), :] = jnp.where(inside, value, 0.0).astype(B16)
    grads_one[...] = lax.dot_general(left[...], columns[...], contract, preferred_element_type=F32)

    count, rows = slots.shape[1], slots.shape[2]

    def block(kk):
        k, source = (kk, grads_one) if kk < 27 else (kk - 27, grads_two)
        m, t = k // 3, k % 3
        same, other = [], []
        for b in range(4):
            lane = (6 * m + b + t) // 2 * 128
            piece = source[64 * b : 64 * (b + 1), lane : lane + 128]
            (same if (b + t) % 2 == kk % 2 else other).append(piece)
        return (same[0] + same[1]) + pltpu.roll(other[0] + other[1], 64, 1)

    for j in range(27):
        first, second = block(2 * j), block(2 * j + 1)
        value = jnp.where(low_half(first.shape), first, second) * scale
        for g in range(count):
            part, lane = j // 7, j % 7 * 128
            slots[part, g, :, lane : lane + 128] = value[g * rows : (g + 1) * rows, :].astype(B16)
    slots[SPLIT - 1, :, :, PART - 128 :] = jnp.zeros((count, rows, 128), B16)


def last_kernel(pre_grad, grad, band, out, steps, columns, held):
    value = pre_grad[...].astype(F32)
    for i, dy in enumerate((-1, 0, 1)):
        steps[i] = (pltpu.roll(value, dy % ROWS, 0) if dy else value).astype(B16)
    own_columns(steps, columns, -1)
    held[...] = jnp.dot(columns[...], band[...], preferred_element_type=F32)
    for h in range(4):
        for x in range(SX):
            row, lanes = 64 * h + 16 * x, slice(256 * h, 256 * (h + 1))
            out[x, :, lanes] = (held[row : row + 8, :] + grad[x, :, lanes].astype(F32)).astype(B16)


def swapped(low, high, axis):
    count = lax.axis_size(axis)
    up = [(i, (i + 1) % count) for i in range(count)]
    down = [(target, source) for source, target in up]
    return lax.ppermute(high, axis, up), lax.ppermute(low, axis, down)


def total_kernel(parts, out):
    value = parts[0].astype(F32)
    for i in range(1, parts.shape[0]):
        value += parts[i].astype(F32)
    value = value.astype(out.dtype)
    if out.ndim == value.ndim:
        out[...] = value
    else:
        for i in range(out.shape[0]):
            out[i] = value


def last_total_kernel(parts, one, two):
    columns = []
    for part in range(SPLIT):
        columns += [parts[part, :, 128 * i : 128 * (i + 1)] for i in range(7)]
    for j in range(13):
        one[:, 128 * j : 128 * (j + 1)] = columns[j]
    one[:, 13 * 128 :] = columns[13][:, 0:64]
    for j in range(14):
        v, w = pltpu.roll(columns[13 + j], 64, 1), pltpu.roll(columns[14 + j], 64, 1)
        value = jnp.where(low_half(v.shape), v, w)
        if j < 13:
            two[:, 128 * j : 128 * (j + 1)] = value
        else:
            two[:, 13 * 128 :] = value[:, 0:64]


def reduced(slots):
    count, rows = slots.shape[1:3]
    gy = lax.axis_size("gy")

    def a2a(array, axis):
        return lax.all_to_all(array, axis, 0, 0, tiled=True)

    (part,) = call(total_kernel, [((count, rows, PART), B16)], [], 1000, 500000, a2a(slots, "gz"))
    (copies,) = call(total_kernel, [((gy, rows, PART), F32)], [], 1000, 500000, a2a(part, "gx"))
    (part,) = call(total_kernel, [((rows, PART), F32)], [], 1000, 500000, a2a(copies, "gy"))
    parts = lax.all_gather(part, "gz", axis=0)
    grads = ((rows, 27 * CH), F32)
    return call(last_total_kernel, [grads, grads], [], 1000, 500000, parts)


def body(block_input, pre_act, skip_grad, pool_grad, conv1_weight, conv2_weight):
    count = lax.axis_size("gx")
    rows = CH // count
    cells = SX * SY * SZ * count * lax.axis_size("gy") * lax.axis_size("gz")
    block, message = ((SX, SY, LANES), B16), ((4, SY, LANES), B16)
    weight = ((rows, 27 * CH), B16)
    grad, pre, inp, low, high, copies = call(
        prep_kernel,
        [block, block, block, message, message, ((count, 2 * rows, 27 * CH), B16)],
        [
            block, ((SX // 2, SY // 2, LANES // 2), B16), weight, weight,
            ((SX // 2, SY, LANES), F32), ((2 * rows, 27 * CH), F32), pltpu.SemaphoreType.DMA((6,)),
        ],
        100000, 400000,
        skip_grad, pool_grad, pre_act, block_input, conv1_weight, conv2_weight,
        space=pltpu.HBM,
        grant=60,
    )
    xlo, xhi = swapped(low, high, "gx")
    gathered = lax.all_to_all(copies, "gx", 0, 0, tiled=True)
    fields = (grad, pre, inp, xlo, xhi)
    message = ((LAYERS, 2, LANES), B16)
    ylo, yhi = swapped(
        *call(ypack_kernel, [message, message], [((2, LANES), F32)], 100000, 600000, *fields), "gy"
    )
    message, held = ((LAYERS, 12, 128), B16), ((LAYERS, 12, 128), F32)
    zlo, zhi = swapped(
        *call(zpack_kernel, [message, message], [held, ((12, 128), F32)], 100000, 700000, *fields, ylo, yhi),
        "gz",
    )
    matrix = ((DEPTH, 256), B16)
    flat = ((CH, 36 * CH), F32)
    band_one, band_two = call(bands_kernel, [matrix, matrix], [flat, flat], 1000000, 4000000, gathered)
    field = ((ROWS, WIDE), F32)
    steps = ((3, ROWS, WIDE), B16)
    columns = ((256, DEPTH), B16)
    slots, pre_grad = call(
        functools.partial(main_kernel, 1.0 / math.sqrt(cells)),
        [((SPLIT, count, rows, PART), B16), ((ROWS, WIDE), B16)],
        [
            field, field, field, steps, columns,
            ((5 * HALO_ROWS, DEPTH), B16), ((256, 256), B16), ((256, 256), F32),
            ((256, DEPTH), F32), ((256, DEPTH), F32), ((5 * HALO_ROWS, 256), F32),
        ],
        2 * 900 * 1000 * 1000, 8000000,
        *fields, ylo, yhi, zlo, zhi, band_two,
    )
    (input_grad,) = call(
        last_kernel,
        [((SX, SY, LANES), B16)],
        [steps, columns, ((256, 256), F32)],
        500000000, 4000000,
        pre_grad, grad, band_one,
    )
    conv1_grad, conv2_grad = reduced(slots)
    return input_grad, conv1_grad, conv2_grad


def solution(mesh):
    in_specs = (
        P("gx", "gy", "gz"),
        P("gx", "gy", "gz"),
        P("gx", "gy", "gz"),
        P("gx", "gy", "gz"),
        P("gx", None),
        P("gx", None),
    )
    out_specs = (P("gx", "gy", "gz"), P("gx", None), P("gx", None))
    return jax.shard_map(body, mesh=mesh, in_specs=in_specs, out_specs=out_specs, check_vma=False)
```

```python
import functools
import math

import jax
import jax.numpy as jnp
from jax import lax
from jax.experimental import pallas as pl
from jax.experimental.pallas import tpu as pltpu
from jax.sharding import PartitionSpec as P

F32, B16 = jnp.float32, jnp.bfloat16
SX, SY, SZ, CH = 4, 8, 16, 64
LANES = SZ * CH
ROWS = 16 * (SX + 5)
WIDE = LANES + 6 * CH
BAND = 6 * CH
DEPTH = 9 * BAND
OWN = 16 * 3
HALO_ROWS = 16 * (SX + 3)
LAYERS = 14


def call(kernel, outs, scratch, flops, moved, *args, space=pltpu.VMEM):
    return pl.pallas_call(
        kernel,
        out_shape=[jax.ShapeDtypeStruct(shape, dtype) for shape, dtype in outs],
        in_specs=[pl.BlockSpec(memory_space=space)] * len(args),
        out_specs=[pl.BlockSpec(memory_space=pltpu.VMEM)] * len(outs),
        scratch_shapes=[pltpu.VMEM(*held) if isinstance(held, tuple) else held for held in scratch],
        compiler_params=pltpu.CompilerParams(vmem_limit_bytes=48 * 1024 * 1024),
        cost_estimate=pl.CostEstimate(flops=flops, bytes_accessed=moved, transcendentals=0),
    )(*args)


def low_half(shape):
    return lax.broadcasted_iota(jnp.int32, shape, len(shape) - 1) % 128 < 64


def prep_kernel(skip_in, pool_in, pre_in, inp_in, one_in, two_in,
                grad, pre, inp, low, high, copies, skip, pool, one, two, up, rows, sems):
    moves = [
        pltpu.make_async_copy(source, target, sems.at[i])
        for i, (source, target) in enumerate(
            ((skip_in, skip), (pool_in, pool), (pre_in, pre), (inp_in, inp), (one_in, one), (two_in, two))
        )
    ]
    for move in moves:
        move.start()
    for move in moves:
        move.wait()
    each = one.shape[0]
    rows[0:each], rows[each : 2 * each] = one[...].astype(F32), two[...].astype(F32)
    both = rows[...].astype(B16)
    for g in range(copies.shape[0]):
        copies[g] = both
    for px in range(SX // 2):
        pieces = []
        for j in range(LANES // 256):
            v = pool[px, :, 128 * j : 128 * (j + 1)].astype(F32)
            turned = pltpu.roll(v, 64, 1)
            first = low_half(v.shape)
            pieces += [jnp.where(first, v, turned), jnp.where(first, turned, v)]
        for y in range(SY):
            for j, piece in enumerate(pieces):
                up[px, y : y + 1, 128 * j : 128 * (j + 1)] = piece[y // 2 : y // 2 + 1, :]
    for x in range(SX):
        value = (skip[x].astype(F32) + 0.125 * up[x // 2]).astype(B16)
        grad[x] = value
        if x < 2:
            low[x] = value
        else:
            high[x - 2] = value
    low[2], low[3] = pre[0], inp[0]
    high[2], high[3] = pre[SX - 1], inp[SX - 1]


def fields_of(grad, pre, inp, xlo, xhi):
    def own(ref):
        return [(ref, x) for x in range(SX)]

    return (
        [(xlo, 0), (xlo, 1)] + own(grad) + [(xhi, 0), (xhi, 1)],
        [(xlo, 2)] + own(pre) + [(xhi, 2)],
        [(xlo, 3)] + own(inp) + [(xhi, 3)],
    )


def ypack_kernel(grad, pre, inp, xlo, xhi, low, high, held):
    wide, acts, inputs = fields_of(grad, pre, inp, xlo, xhi)
    for at, (ref, x) in enumerate(wide):
        value = ref[x].astype(F32)
        low[at] = value[0:2].astype(B16)
        high[at] = value[SY - 2 : SY].astype(B16)
    for out, row in ((low, 0), (high, SY - 1)):
        for at, ((a, ax), (i, ix)) in enumerate(zip(acts, inputs)):
            held[0:1] = a[ax].astype(F32)[row : row + 1]
            held[1:2] = i[ix].astype(F32)[row : row + 1]
            out[8 + at] = held[...].astype(B16)


def zpack_kernel(grad, pre, inp, xlo, xhi, ylo, yhi, slots, held):
    held[...] = jnp.zeros_like(held)
    wide, acts, inputs = fields_of(grad, pre, inp, xlo, xhi)
    size = slots.shape[0]
    me = lax.axis_index("gz")
    slots[...] = jnp.zeros_like(slots)
    for to, lane, half in ((me + size - 1, 0, True), (me + 1, LANES - 128, False)):
        cut = slice(lane, lane + 128)
        for at, (ref, x) in enumerate(wide):
            row = 12 * at
            held[row : row + 2] = ylo[at, :, cut].astype(F32)
            held[row + 2 : row + 10] = ref[x, :, cut].astype(F32)
            held[row + 10 : row + 12] = yhi[at, :, cut].astype(F32)
        for j, ((a, ax), (i, ix)) in enumerate(zip(acts, inputs)):
            row = 12 * (8 + j)
            below, above = ylo[8 + j, :, cut].astype(F32), yhi[8 + j, :, cut].astype(F32)
            v, w = a[ax, :, cut].astype(F32), i[ix, :, cut].astype(F32)

            def joined(first, second):
                if half:
                    second = pltpu.roll(second, 64, 1)
                else:
                    first = pltpu.roll(first, 64, 1)
                return jnp.where(low_half(first.shape), first, second)

            held[row + 2 : row + 10] = joined(v, w)
            for at, pair in ((row + 1, below), (row + 10, above)):
                first, second = jnp.broadcast_to(pair[0:1], (8, 128)), jnp.broadcast_to(pair[1:2], (8, 128))
                held[at : at + 1] = joined(first, second)[0:1]
        slots[lax.rem(to, size)] = held[...].astype(B16)


def bands_kernel(weights, one, two, flat, turned):
    count, rows = weights.shape[0], weights.shape[1] // 2
    block = lax.broadcasted_iota(jnp.int32, (CH, 256), 1) // CH
    for which, out in enumerate((one, two)):
        flat[...] = jnp.zeros_like(flat)
        for g in range(count):
            value = weights[g].astype(F32)[which * rows : (which + 1) * rows]
            flat[g * rows : (g + 1) * rows, 256 : 256 + 27 * CH] = value
        turned[...] = pltpu.roll(flat[...], flat.shape[1] - 64, 1)
        for m in range(9):
            for a in range(6):
                at = 4 + 3 * m + 2 - a
                source = turned if at % 2 else flat
                lane = at // 2 * 128
                valid = (block + 2 - a >= 0) & (block - a <= 0)
                value = jnp.where(valid, source[:, lane : lane + 256], 0.0)
                out[m * BAND + a * CH : m * BAND + (a + 1) * CH, :] = value.astype(B16)


def fill_wide(field, layers, ylo, yhi, zlo, zhi):
    field[...] = jnp.zeros_like(field)
    for at, (ref, x) in enumerate(layers):
        row = 16 * (at + 1)
        field[row : row + 8, 128 : 128 + LANES] = ref[x].astype(F32)
        field[row - 2 : row, 128 : 128 + LANES] = ylo[at].astype(F32)
        field[row + 8 : row + 10, 128 : 128 + LANES] = yhi[at].astype(F32)
        for side, lane in ((zlo, 0), (zhi, 128 + LANES)):
            field[row - 2 : row + 10, lane : lane + 128] = side[12 * at : 12 * at + 12]


def fill_thin(field, layers, second, ylo, yhi, zlo, zhi):
    field[...] = jnp.zeros_like(field)
    for j, (ref, x) in enumerate(layers):
        at, row = 8 + j, 16 * (j + 2)
        field[row : row + 8, 128 : 128 + LANES] = ref[x].astype(F32)
        field[row - 1 : row, 128 : 128 + LANES] = ylo[at].astype(F32)[second : second + 1]
        field[row + 8 : row + 9, 128 : 128 + LANES] = yhi[at].astype(F32)[second : second + 1]
        for side, lane, upper in ((zlo, 0, True), (zhi, 128 + LANES, False)):
            value = side[12 * at : 12 * at + 12]
            if upper != bool(second):
                value = pltpu.roll(value, 64, 1)
            value = jnp.where(low_half(value.shape) != upper, value, 0.0)
            field[row - 1 : row, lane : lane + 128] = value[1:2]
            field[row : row + 8, lane : lane + 128] = value[2:10]
            field[row + 8 : row + 9, lane : lane + 128] = value[10:11]


def spread(value, steps, sign):
    moved = pltpu.roll(value, 64, 1)
    for i, dy in enumerate((-1, 0, 1)):
        by = (-sign * dy) % ROWS
        steps[i] = (pltpu.roll(moved, by, 0) if by else moved).astype(B16)


def own_columns(steps, columns, sign):
    for m in range(9):
        dx, dy = m // 3 - 1, m % 3
        row = OWN + sign * 16 * dx
        for h in range(4):
            columns[64 * h : 64 * (h + 1), BAND * m : BAND * (m + 1)] = steps[
                dy, row : row + 64, 256 * h + 128 : 256 * h + 128 + BAND
            ]


def main_kernel(scale, grad, pre, inp, xlo, xhi, ylo, yhi, sides, band,
                slots, pre_out, fg, fa, fi, steps, columns, many, left, left_f, grads_one, grads_two, held, zlo, zhi):
    wide, acts, inputs = fields_of(grad, pre, inp, xlo, xhi)
    size = sides.shape[0]
    me = lax.axis_index("gz")
    zlo[...] = sides[lax.rem(me + size - 1, size)].astype(F32)
    zhi[...] = sides[lax.rem(me + 1, size)].astype(F32)
    halos = (ylo, yhi, zlo, zhi)
    fill_wide(fg, wide, *halos)
    fill_thin(fa, acts, 0, *halos)
    fill_thin(fi, inputs, 1, *halos)
    contract = (((0,), (0,)), ((), ()))

    v = fa[...]
    spread((v * jax.nn.sigmoid(v)).astype(B16).astype(F32), steps, 1)
    own_columns(steps, columns, 1)
    left_f[...] = jnp.zeros_like(left_f)
    for h in range(4):
        for x in range(SX):
            row = 64 * h + 16 * x
            left_f[row : row + 8, :] = grad[x, :, 256 * h : 256 * (h + 1)].astype(F32)
    left[...] = left_f[...].astype(B16)
    grads_two[...] = lax.dot_general(left[...], columns[...], contract, preferred_element_type=F32)

    spread(fg[...], steps, -1)
    for m in range(9):
        dx, dy = m // 3 - 1, m % 3
        row = 16 - 16 * dx
        for h in range(5):
            many[HALO_ROWS * h : HALO_ROWS * (h + 1), BAND * m : BAND * (m + 1)] = steps[
                dy, row : row + HALO_ROWS, 256 * h : 256 * h + BAND
            ]
    held[...] = jnp.dot(many[...], band[...], preferred_element_type=F32)
    fg[...] = jnp.zeros_like(fg)
    for h in range(5):
        v = fa[16 : 16 + HALO_ROWS, 256 * h : 256 * (h + 1)]
        g = jax.nn.sigmoid(v)
        value = held[HALO_ROWS * h : HALO_ROWS * (h + 1), :] * (g * (1.0 + v * (1.0 - g)))
        fg[16 : 16 + HALO_ROWS, 256 * h : 256 * (h + 1)] = value.astype(B16).astype(F32)
    pre_out[...] = pltpu.roll(fg[...], 64, 1).astype(B16)

    spread(fi[...], steps, 1)
    own_columns(steps, columns, 1)
    inside = lax.broadcasted_iota(jnp.int32, (64, 256), 0) % 16 < 8
    for h in range(4):
        value = fg[OWN : OWN + 64, 256 * h + 128 : 256 * h + 384]
        left[64 * h : 64 * (h + 1), :] = jnp.where(inside, value, 0.0).astype(B16)
    grads_one[...] = lax.dot_general(left[...], columns[...], contract, preferred_element_type=F32)

    count, rows = slots.shape[0], slots.shape[1]

    def block(kk):
        k, source = (kk, grads_one) if kk < 27 else (kk - 27, grads_two)
        m, t = k // 3, k % 3
        same, other = [], []
        for b in range(4):
            lane = (6 * m + b + t) // 2 * 128
            piece = source[64 * b : 64 * (b + 1), lane : lane + 128]
            (same if (b + t) % 2 == kk % 2 else other).append(piece)
        return (same[0] + same[1]) + pltpu.roll(other[0] + other[1], 64, 1)

    for j in range(27):
        first, second = block(2 * j), block(2 * j + 1)
        value = jnp.where(low_half(first.shape), first, second) * scale
        for g in range(count):
            slots[g, :, 128 * j : 128 * (j + 1)] = value[g * rows : (g + 1) * rows, :].astype(B16)


def last_kernel(pre_grad, grad, band, out, steps, columns, held):
    value = pre_grad[...].astype(F32)
    for i, dy in enumerate((-1, 0, 1)):
        steps[i] = (pltpu.roll(value, dy % ROWS, 0) if dy else value).astype(B16)
    own_columns(steps, columns, -1)
    held[...] = jnp.dot(columns[...], band[...], preferred_element_type=F32)
    for h in range(4):
        for x in range(SX):
            row, lanes = 64 * h + 16 * x, slice(256 * h, 256 * (h + 1))
            out[x, :, lanes] = (held[row : row + 8, :] + grad[x, :, lanes].astype(F32)).astype(B16)


def swapped(low, high, axis):
    count = lax.axis_size(axis)
    up = [(i, (i + 1) % count) for i in range(count)]
    down = [(target, source) for source, target in up]
    return lax.ppermute(high, axis, up), lax.ppermute(low, axis, down)


def total_kernel(parts, out):
    value = parts[0].astype(F32)
    for i in range(1, parts.shape[0]):
        value += parts[i].astype(F32)
    value = value.astype(out.dtype)
    if out.ndim == value.ndim:
        out[...] = value
    else:
        for i in range(out.shape[0]):
            out[i] = value


def last_total_kernel(parts, one, two, held):
    value = parts[0].astype(F32)
    for i in range(1, parts.shape[0]):
        value += parts[i].astype(F32)
    held[...] = value
    one[...] = held[:, : 27 * CH]
    held[...] = pltpu.roll(value, 27 * CH, 1)
    two[...] = held[:, : 27 * CH]


def reduced(slots, other):
    rows, columns = slots.shape[1:]
    gy = lax.axis_size("gy")
    parts = lax.all_to_all(slots, "gx", 0, 0, tiled=True)
    parts, other = lax.optimization_barrier((parts, other))
    (part,) = call(total_kernel, [((rows, columns), F32)], [], 1000, 500000, parts)
    parts = lax.all_gather(part, "gz", axis=0)
    (copies,) = call(total_kernel, [((gy, rows, columns), B16)], [], 1000, 500000, parts)
    parts = lax.all_to_all(copies, "gy", 0, 0, tiled=True)
    grads = ((rows, 27 * CH), F32)
    one, two = call(last_total_kernel, [grads, grads], [((rows, columns), F32)], 1000, 500000, parts)
    return other, one, two


def body(block_input, pre_act, skip_grad, pool_grad, conv1_weight, conv2_weight):
    count = lax.axis_size("gx")
    rows = CH // count
    cells = SX * SY * SZ * count * lax.axis_size("gy") * lax.axis_size("gz")
    block, message = ((SX, SY, LANES), B16), ((4, SY, LANES), B16)
    weight = ((rows, 27 * CH), B16)
    grad, pre, inp, low, high, copies = call(
        prep_kernel,
        [block, block, block, message, message, ((count, 2 * rows, 27 * CH), B16)],
        [
            block, ((SX // 2, SY // 2, LANES // 2), B16), weight, weight,
            ((SX // 2, SY, LANES), F32), ((2 * rows, 27 * CH), F32), pltpu.SemaphoreType.DMA((6,)),
        ],
        100000, 400000,
        *(
            pltpu.with_memory_space_constraint(array, pltpu.HBM)
            for array in (skip_grad, pool_grad, pre_act, block_input, conv1_weight, conv2_weight)
        ),
        space=pltpu.HBM,
    )
    xlo, xhi = swapped(low, high, "gx")
    fields = (grad, pre, inp, xlo, xhi)
    message = ((LAYERS, 2, LANES), B16)
    ylo, yhi = swapped(
        *call(ypack_kernel, [message, message], [((2, LANES), F32)], 60000000000, 600000, *fields), "gy"
    )
    side = ((12 * LAYERS, 128), F32)
    gathered = lax.all_to_all(copies, "gx", 0, 0, tiled=True)
    (sides,) = call(
        zpack_kernel,
        [((lax.axis_size("gz"), 12 * LAYERS, 128), B16)],
        [side],
        100000, 700000,
        *fields, ylo, yhi,
    )
    sides = lax.all_to_all(sides, "gz", 0, 0, tiled=True)
    matrix = ((DEPTH, 256), B16)
    flat = ((CH, 36 * CH), F32)
    band_one, band_two = call(bands_kernel, [matrix, matrix], [flat, flat], 1000000, 4000000, gathered)
    field = ((ROWS, WIDE), F32)
    steps = ((3, ROWS, WIDE), B16)
    columns = ((256, DEPTH), B16)
    slots, pre_grad = call(
        functools.partial(main_kernel, 1.0 / math.sqrt(cells)),
        [((count, rows, 54 * CH), B16), ((ROWS, WIDE), B16)],
        [
            field, field, field, steps, columns,
            ((5 * HALO_ROWS, DEPTH), B16), ((256, 256), B16), ((256, 256), F32),
            ((256, DEPTH), F32), ((256, DEPTH), F32), ((5 * HALO_ROWS, 256), F32), side, side,
        ],
        2 * 900 * 1000 * 1000, 8000000,
        *fields, ylo, yhi, sides, band_two,
    )
    (input_grad,) = call(
        last_kernel,
        [((SX, SY, LANES), B16)],
        [steps, columns, ((256, 256), F32)],
        500000000, 4000000,
        pre_grad, grad, band_one,
    )
    return reduced(slots, input_grad)


def solution(mesh):
    in_specs = (
        P("gx", "gy", "gz"),
        P("gx", "gy", "gz"),
        P("gx", "gy", "gz"),
        P("gx", "gy", "gz"),
        P("gx", None),
        P("gx", None),
    )
    out_specs = (P("gx", "gy", "gz"), P("gx", None), P("gx", None))
    return jax.shard_map(body, mesh=mesh, in_specs=in_specs, out_specs=out_specs, check_vma=False)
```

```python
import functools
import math

import jax
import jax.numpy as jnp
from jax import lax
from jax.experimental import pallas as pl
from jax.experimental.pallas import tpu as pltpu
from jax.sharding import PartitionSpec as P

F32, B16 = jnp.float32, jnp.bfloat16
SX, SY, SZ, CH = 4, 8, 16, 64
LANES = SZ * CH
ROWS = 16 * (SX + 5)
WIDE = LANES + 6 * CH
BAND = 6 * CH
DEPTH = 9 * BAND
OWN = 16 * 3
HALO_ROWS = 16 * (SX + 3)
LAYERS = 14


def call(kernel, outs, scratch, flops, moved, *args, space=pltpu.VMEM, grant=12):
    return pl.pallas_call(
        kernel,
        out_shape=[jax.ShapeDtypeStruct(shape, dtype) for shape, dtype in outs],
        in_specs=[pl.BlockSpec(memory_space=space)] * len(args),
        out_specs=[pl.BlockSpec(memory_space=pltpu.VMEM)] * len(outs),
        scratch_shapes=[pltpu.VMEM(*held) if isinstance(held, tuple) else held for held in scratch],
        compiler_params=pltpu.CompilerParams(vmem_limit_bytes=grant * 1024 * 1024),
        cost_estimate=pl.CostEstimate(flops=flops, bytes_accessed=moved, transcendentals=0),
    )(*args)


def low_half(shape):
    return lax.broadcasted_iota(jnp.int32, shape, len(shape) - 1) % 128 < 64


def prep_kernel(skip_in, pool_in, pre_in, inp_in, one_in, two_in,
                grad, pre, inp, low, high, copies, skip, pool, one, two, up, rows, sems):
    moves = [
        pltpu.make_async_copy(source, target, sems.at[i])
        for i, (source, target) in enumerate(
            ((skip_in, skip), (pool_in, pool), (pre_in, pre), (inp_in, inp), (one_in, one), (two_in, two))
        )
    ]
    for move in moves:
        move.start()
    for move in moves:
        move.wait()
    each = one.shape[0]
    rows[0:each], rows[each : 2 * each] = one[...].astype(F32), two[...].astype(F32)
    both = rows[...].astype(B16)
    for g in range(copies.shape[0]):
        copies[g] = both
    for px in range(SX // 2):
        pieces = []
        for j in range(LANES // 256):
            v = pool[px, :, 128 * j : 128 * (j + 1)].astype(F32)
            turned = pltpu.roll(v, 64, 1)
            first = low_half(v.shape)
            pieces += [jnp.where(first, v, turned), jnp.where(first, turned, v)]
        for y in range(SY):
            for j, piece in enumerate(pieces):
                up[px, y : y + 1, 128 * j : 128 * (j + 1)] = piece[y // 2 : y // 2 + 1, :]
    for x in range(SX):
        value = (skip[x].astype(F32) + 0.125 * up[x // 2]).astype(B16)
        grad[x] = value
        if x < 2:
            low[x] = value
        else:
            high[x - 2] = value
    low[2], low[3] = pre[0], inp[0]
    high[2], high[3] = pre[SX - 1], inp[SX - 1]


def fields_of(grad, pre, inp, xlo, xhi):
    def own(ref):
        return [(ref, x) for x in range(SX)]

    return (
        [(xlo, 0), (xlo, 1)] + own(grad) + [(xhi, 0), (xhi, 1)],
        [(xlo, 2)] + own(pre) + [(xhi, 2)],
        [(xlo, 3)] + own(inp) + [(xhi, 3)],
    )


def ypack_kernel(grad, pre, inp, xlo, xhi, low, high, held):
    wide, acts, inputs = fields_of(grad, pre, inp, xlo, xhi)
    for at, (ref, x) in enumerate(wide):
        value = ref[x].astype(F32)
        low[at] = value[0:2].astype(B16)
        high[at] = value[SY - 2 : SY].astype(B16)
    for out, row in ((low, 0), (high, SY - 1)):
        for at, ((a, ax), (i, ix)) in enumerate(zip(acts, inputs)):
            held[0:1] = a[ax].astype(F32)[row : row + 1]
            held[1:2] = i[ix].astype(F32)[row : row + 1]
            out[8 + at] = held[...].astype(B16)


def zpack_kernel(grad, pre, inp, xlo, xhi, ylo, yhi, low, high, held):
    held[...] = jnp.zeros_like(held)
    wide, acts, inputs = fields_of(grad, pre, inp, xlo, xhi)
    for out, lane, half in ((low, 0, True), (high, LANES - 128, False)):
        cut = slice(lane, lane + 128)
        for at, (ref, x) in enumerate(wide):
            row = 12 * at
            held[row : row + 2] = ylo[at, :, cut].astype(F32)
            held[row + 2 : row + 10] = ref[x, :, cut].astype(F32)
            held[row + 10 : row + 12] = yhi[at, :, cut].astype(F32)
        for j, ((a, ax), (i, ix)) in enumerate(zip(acts, inputs)):
            row = 12 * (8 + j)
            below, above = ylo[8 + j, :, cut].astype(F32), yhi[8 + j, :, cut].astype(F32)
            v, w = a[ax, :, cut].astype(F32), i[ix, :, cut].astype(F32)

            def joined(first, second):
                if half:
                    second = pltpu.roll(second, 64, 1)
                else:
                    first = pltpu.roll(first, 64, 1)
                return jnp.where(low_half(first.shape), first, second)

            held[row + 2 : row + 10] = joined(v, w)
            for at, pair in ((row + 1, below), (row + 10, above)):
                first, second = jnp.broadcast_to(pair[0:1], (8, 128)), jnp.broadcast_to(pair[1:2], (8, 128))
                held[at : at + 1] = joined(first, second)[0:1]
        out[...] = held[...].astype(B16)


def bands_kernel(weights, one, two, flat, turned):
    count, rows = weights.shape[0], weights.shape[1] // 2
    block = lax.broadcasted_iota(jnp.int32, (CH, 256), 1) // CH
    for which, out in enumerate((one, two)):
        flat[...] = jnp.zeros_like(flat)
        for g in range(count):
            value = weights[g].astype(F32)[which * rows : (which + 1) * rows]
            flat[g * rows : (g + 1) * rows, 256 : 256 + 27 * CH] = value
        turned[...] = pltpu.roll(flat[...], flat.shape[1] - 64, 1)
        for m in range(9):
            for a in range(6):
                at = 4 + 3 * m + 2 - a
                source = turned if at % 2 else flat
                lane = at // 2 * 128
                valid = (block + 2 - a >= 0) & (block - a <= 0)
                value = jnp.where(valid, source[:, lane : lane + 256], 0.0)
                out[m * BAND + a * CH : m * BAND + (a + 1) * CH, :] = value.astype(B16)


def fill_wide(field, layers, ylo, yhi, zlo, zhi):
    field[...] = jnp.zeros_like(field)
    for at, (ref, x) in enumerate(layers):
        row = 16 * (at + 1)
        field[row : row + 8, 128 : 128 + LANES] = ref[x].astype(F32)
        field[row - 2 : row, 128 : 128 + LANES] = ylo[at].astype(F32)
        field[row + 8 : row + 10, 128 : 128 + LANES] = yhi[at].astype(F32)
        for side, lane in ((zlo, 0), (zhi, 128 + LANES)):
            field[row - 2 : row + 10, lane : lane + 128] = side[12 * at : 12 * at + 12]


def fill_thin(field, layers, second, ylo, yhi, zlo, zhi):
    field[...] = jnp.zeros_like(field)
    for j, (ref, x) in enumerate(layers):
        at, row = 8 + j, 16 * (j + 2)
        field[row : row + 8, 128 : 128 + LANES] = ref[x].astype(F32)
        field[row - 1 : row, 128 : 128 + LANES] = ylo[at].astype(F32)[second : second + 1]
        field[row + 8 : row + 9, 128 : 128 + LANES] = yhi[at].astype(F32)[second : second + 1]
        for side, lane, upper in ((zlo, 0, True), (zhi, 128 + LANES, False)):
            value = side[12 * at : 12 * at + 12]
            if upper != bool(second):
                value = pltpu.roll(value, 64, 1)
            value = jnp.where(low_half(value.shape) != upper, value, 0.0)
            field[row - 1 : row, lane : lane + 128] = value[1:2]
            field[row : row + 8, lane : lane + 128] = value[2:10]
            field[row + 8 : row + 9, lane : lane + 128] = value[10:11]


def spread(value, steps, sign):
    moved = pltpu.roll(value, 64, 1)
    for i, dy in enumerate((-1, 0, 1)):
        by = (-sign * dy) % ROWS
        steps[i] = (pltpu.roll(moved, by, 0) if by else moved).astype(B16)


def own_columns(steps, columns, sign):
    for m in range(9):
        dx, dy = m // 3 - 1, m % 3
        row = OWN + sign * 16 * dx
        for h in range(4):
            columns[64 * h : 64 * (h + 1), BAND * m : BAND * (m + 1)] = steps[
                dy, row : row + 64, 256 * h + 128 : 256 * h + 128 + BAND
            ]


def main_kernel(scale, grad, pre, inp, xlo, xhi, ylo, yhi, below, above, band,
                slots, pre_out, fg, fa, fi, steps, columns, many, left, left_f, grads_one, grads_two, held, zlo, zhi):
    wide, acts, inputs = fields_of(grad, pre, inp, xlo, xhi)
    zlo[...] = below[...].astype(F32)
    zhi[...] = above[...].astype(F32)
    halos = (ylo, yhi, zlo, zhi)
    fill_wide(fg, wide, *halos)
    fill_thin(fa, acts, 0, *halos)
    fill_thin(fi, inputs, 1, *halos)
    contract = (((0,), (0,)), ((), ()))

    v = fa[...]
    spread((v * jax.nn.sigmoid(v)).astype(B16).astype(F32), steps, 1)
    own_columns(steps, columns, 1)
    left_f[...] = jnp.zeros_like(left_f)
    for h in range(4):
        for x in range(SX):
            row = 64 * h + 16 * x
            left_f[row : row + 8, :] = grad[x, :, 256 * h : 256 * (h + 1)].astype(F32)
    left[...] = left_f[...].astype(B16)
    grads_two[...] = lax.dot_general(left[...], columns[...], contract, preferred_element_type=F32)

    spread(fg[...], steps, -1)
    for m in range(9):
        dx, dy = m // 3 - 1, m % 3
        row = 16 - 16 * dx
        for h in range(5):
            many[HALO_ROWS * h : HALO_ROWS * (h + 1), BAND * m : BAND * (m + 1)] = steps[
                dy, row : row + HALO_ROWS, 256 * h : 256 * h + BAND
            ]
    held[...] = jnp.dot(many[...], band[...], preferred_element_type=F32)
    fg[...] = jnp.zeros_like(fg)
    for h in range(5):
        v = fa[16 : 16 + HALO_ROWS, 256 * h : 256 * (h + 1)]
        g = jax.nn.sigmoid(v)
        value = held[HALO_ROWS * h : HALO_ROWS * (h + 1), :] * (g * (1.0 + v * (1.0 - g)))
        fg[16 : 16 + HALO_ROWS, 256 * h : 256 * (h + 1)] = value.astype(B16).astype(F32)
    pre_out[...] = pltpu.roll(fg[...], 64, 1).astype(B16)

    spread(fi[...], steps, 1)
    own_columns(steps, columns, 1)
    inside = lax.broadcasted_iota(jnp.int32, (64, 256), 0) % 16 < 8
    for h in range(4):
        value = fg[OWN : OWN + 64, 256 * h + 128 : 256 * h + 384]
        left[64 * h : 64 * (h + 1), :] = jnp.where(inside, value, 0.0).astype(B16)
    grads_one[...] = lax.dot_general(left[...], columns[...], contract, preferred_element_type=F32)

    count, rows = slots.shape[0], slots.shape[1]

    def block(kk):
        k, source = (kk, grads_one) if kk < 27 else (kk - 27, grads_two)
        m, t = k // 3, k % 3
        same, other = [], []
        for b in range(4):
            lane = (6 * m + b + t) // 2 * 128
            piece = source[64 * b : 64 * (b + 1), lane : lane + 128]
            (same if (b + t) % 2 == kk % 2 else other).append(piece)
        return (same[0] + same[1]) + pltpu.roll(other[0] + other[1], 64, 1)

    for j in range(27):
        first, second = block(2 * j), block(2 * j + 1)
        value = jnp.where(low_half(first.shape), first, second) * scale
        for g in range(count):
            slots[g, :, 128 * j : 128 * (j + 1)] = value[g * rows : (g + 1) * rows, :].astype(B16)


def last_kernel(pre_grad, grad, band, out, steps, columns, held):
    value = pre_grad[...].astype(F32)
    for i, dy in enumerate((-1, 0, 1)):
        steps[i] = (pltpu.roll(value, dy % ROWS, 0) if dy else value).astype(B16)
    own_columns(steps, columns, -1)
    held[...] = jnp.dot(columns[...], band[...], preferred_element_type=F32)
    for h in range(4):
        for x in range(SX):
            row, lanes = 64 * h + 16 * x, slice(256 * h, 256 * (h + 1))
            out[x, :, lanes] = (held[row : row + 8, :] + grad[x, :, lanes].astype(F32)).astype(B16)


def swapped(low, high, axis):
    count = lax.axis_size(axis)
    up = [(i, (i + 1) % count) for i in range(count)]
    down = [(target, source) for source, target in up]
    return lax.ppermute(high, axis, up), lax.ppermute(low, axis, down)


def total_kernel(parts, out):
    value = parts[0].astype(F32)
    for i in range(1, parts.shape[0]):
        value += parts[i].astype(F32)
    value = value.astype(out.dtype)
    if out.ndim == value.ndim:
        out[...] = value
    else:
        for i in range(out.shape[0]):
            out[i] = value


def last_total_kernel(parts, one, two, held):
    value = parts[0].astype(F32)
    for i in range(1, parts.shape[0]):
        value += parts[i].astype(F32)
    held[...] = value
    one[...] = held[:, : 27 * CH]
    held[...] = pltpu.roll(value, 27 * CH, 1)
    two[...] = held[:, : 27 * CH]


def reduced(slots, other):
    rows, columns = slots.shape[1:]
    gy = lax.axis_size("gy")
    parts = lax.all_to_all(slots, "gx", 0, 0, tiled=True)
    parts, other = lax.optimization_barrier((parts, other))
    (part,) = call(total_kernel, [((rows, columns), F32)], [], 1000, 500000, parts)
    parts = lax.all_gather(part, "gz", axis=0)
    (copies,) = call(total_kernel, [((gy, rows, columns), B16)], [], 1000, 500000, parts)
    parts = lax.all_to_all(copies, "gy", 0, 0, tiled=True)
    grads = ((rows, 27 * CH), F32)
    one, two = call(last_total_kernel, [grads, grads], [((rows, columns), F32)], 1000, 500000, parts)
    return other, one, two


def body(block_input, pre_act, skip_grad, pool_grad, conv1_weight, conv2_weight):
    count = lax.axis_size("gx")
    rows = CH // count
    cells = SX * SY * SZ * count * lax.axis_size("gy") * lax.axis_size("gz")
    block, message = ((SX, SY, LANES), B16), ((4, SY, LANES), B16)
    weight = ((rows, 27 * CH), B16)
    grad, pre, inp, low, high, copies = call(
        prep_kernel,
        [block, block, block, message, message, ((count, 2 * rows, 27 * CH), B16)],
        [
            block, ((SX // 2, SY // 2, LANES // 2), B16), weight, weight,
            ((SX // 2, SY, LANES), F32), ((2 * rows, 27 * CH), F32), pltpu.SemaphoreType.DMA((6,)),
        ],
        100000, 400000,
        *(
            pltpu.with_memory_space_constraint(array, pltpu.HBM)
            for array in (skip_grad, pool_grad, pre_act, block_input, conv1_weight, conv2_weight)
        ),
        space=pltpu.HBM,
    )
    xlo, xhi = swapped(low, high, "gx")
    fields = (grad, pre, inp, xlo, xhi)
    message = ((LAYERS, 2, LANES), B16)
    ylo, yhi = swapped(
        *call(ypack_kernel, [message, message], [((2, LANES), F32)], 60000000000, 600000, *fields), "gy"
    )
    side = ((12 * LAYERS, 128), F32)
    gathered = lax.all_to_all(copies, "gx", 0, 0, tiled=True)
    message = ((12 * LAYERS, 128), B16)
    below, above = swapped(
        *call(zpack_kernel, [message, message], [side], 100000, 700000, *fields, ylo, yhi), "gz"
    )
    matrix = ((DEPTH, 256), B16)
    flat = ((CH, 36 * CH), F32)
    band_one, band_two = call(bands_kernel, [matrix, matrix], [flat, flat], 1000000, 4000000, gathered)
    field = ((ROWS, WIDE), F32)
    steps = ((3, ROWS, WIDE), B16)
    columns = ((256, DEPTH), B16)
    slots, pre_grad = call(
        functools.partial(main_kernel, 1.0 / math.sqrt(cells)),
        [((count, rows, 54 * CH), B16), ((ROWS, WIDE), B16)],
        [
            field, field, field, steps, columns,
            ((5 * HALO_ROWS, DEPTH), B16), ((256, 256), B16), ((256, 256), F32),
            ((256, DEPTH), F32), ((256, DEPTH), F32), ((5 * HALO_ROWS, 256), F32), side, side,
        ],
        2 * 900 * 1000 * 1000, 8000000,
        *fields, ylo, yhi, below, above, band_two,
        grant=32,
    )
    (input_grad,) = call(
        last_kernel,
        [((SX, SY, LANES), B16)],
        [steps, columns, ((256, 256), F32)],
        500000000, 4000000,
        pre_grad, grad, band_one,
    )
    return reduced(slots, input_grad)


def solution(mesh):
    in_specs = (
        P("gx", "gy", "gz"),
        P("gx", "gy", "gz"),
        P("gx", "gy", "gz"),
        P("gx", "gy", "gz"),
        P("gx", None),
        P("gx", None),
    )
    out_specs = (P("gx", "gy", "gz"), P("gx", None), P("gx", None))
    return jax.shard_map(body, mesh=mesh, in_specs=in_specs, out_specs=out_specs, check_vma=False)
```

```python
import functools
import math

import jax
import jax.numpy as jnp
from jax import lax
from jax.experimental import pallas as pl
from jax.experimental.pallas import tpu as pltpu
from jax.sharding import PartitionSpec as P

F32, B16 = jnp.float32, jnp.bfloat16
SX, SY, SZ, CH = 4, 8, 16, 64
LANES = SZ * CH
ROWS = 16 * (SX + 5)
WIDE = LANES + 6 * CH
BAND = 6 * CH
DEPTH = 9 * BAND
OWN = 16 * 3
HALO_ROWS = 16 * (SX + 3)
LAYERS = 14


def call(kernel, outs, scratch, flops, moved, *args, space=pltpu.VMEM, grant=12):
    return pl.pallas_call(
        kernel,
        out_shape=[jax.ShapeDtypeStruct(shape, dtype) for shape, dtype in outs],
        in_specs=[pl.BlockSpec(memory_space=space)] * len(args),
        out_specs=[pl.BlockSpec(memory_space=pltpu.VMEM)] * len(outs),
        scratch_shapes=[pltpu.VMEM(*held) if isinstance(held, tuple) else held for held in scratch],
        compiler_params=pltpu.CompilerParams(vmem_limit_bytes=grant * 1024 * 1024),
        cost_estimate=pl.CostEstimate(flops=flops, bytes_accessed=moved, transcendentals=0),
    )(*args)


def low_half(shape):
    return lax.broadcasted_iota(jnp.int32, shape, len(shape) - 1) % 128 < 64


def prep_kernel(skip_in, pool_in, pre_in, inp_in, one_in, two_in,
                grad, pre, inp, low, high, copies, skip, pool, one, two, up, rows, sems):
    moves = [
        pltpu.make_async_copy(source, target, sems.at[i])
        for i, (source, target) in enumerate(
            ((skip_in, skip), (pool_in, pool), (pre_in, pre), (inp_in, inp), (one_in, one), (two_in, two))
        )
    ]
    for move in moves:
        move.start()
    for move in moves:
        move.wait()
    each = one.shape[0]
    rows[0:each], rows[each : 2 * each] = one[...].astype(F32), two[...].astype(F32)
    both = rows[...].astype(B16)
    for g in range(copies.shape[0]):
        copies[g] = both
    for px in range(SX // 2):
        pieces = []
        for j in range(LANES // 256):
            v = pool[px, :, 128 * j : 128 * (j + 1)].astype(F32)
            turned = pltpu.roll(v, 64, 1)
            first = low_half(v.shape)
            pieces += [jnp.where(first, v, turned), jnp.where(first, turned, v)]
        for y in range(SY):
            for j, piece in enumerate(pieces):
                up[px, y : y + 1, 128 * j : 128 * (j + 1)] = piece[y // 2 : y // 2 + 1, :]
    for x in range(SX):
        value = (skip[x].astype(F32) + 0.125 * up[x // 2]).astype(B16)
        grad[x] = value
        if x < 2:
            low[x] = value
        else:
            high[x - 2] = value
    low[2], low[3] = pre[0], inp[0]
    high[2], high[3] = pre[SX - 1], inp[SX - 1]


def fields_of(grad, pre, inp, xlo, xhi):
    def own(ref):
        return [(ref, x) for x in range(SX)]

    return (
        [(xlo, 0), (xlo, 1)] + own(grad) + [(xhi, 0), (xhi, 1)],
        [(xlo, 2)] + own(pre) + [(xhi, 2)],
        [(xlo, 3)] + own(inp) + [(xhi, 3)],
    )


def ypack_kernel(grad, pre, inp, xlo, xhi, low, high, held):
    wide, acts, inputs = fields_of(grad, pre, inp, xlo, xhi)
    for at, (ref, x) in enumerate(wide):
        value = ref[x].astype(F32)
        low[at] = value[0:2].astype(B16)
        high[at] = value[SY - 2 : SY].astype(B16)
    for out, row in ((low, 0), (high, SY - 1)):
        for at, ((a, ax), (i, ix)) in enumerate(zip(acts, inputs)):
            held[0:1] = a[ax].astype(F32)[row : row + 1]
            held[1:2] = i[ix].astype(F32)[row : row + 1]
            out[8 + at] = held[...].astype(B16)


def zpack_kernel(grad, pre, inp, xlo, xhi, ylo, yhi, low, high, held):
    held[...] = jnp.zeros_like(held)
    wide, acts, inputs = fields_of(grad, pre, inp, xlo, xhi)
    for out, lane, half in ((low, 0, True), (high, LANES - 128, False)):
        cut = slice(lane, lane + 128)
        for at, (ref, x) in enumerate(wide):
            row = 12 * at
            held[row : row + 2] = ylo[at, :, cut].astype(F32)
            held[row + 2 : row + 10] = ref[x, :, cut].astype(F32)
            held[row + 10 : row + 12] = yhi[at, :, cut].astype(F32)
        for j, ((a, ax), (i, ix)) in enumerate(zip(acts, inputs)):
            row = 12 * (8 + j)
            below, above = ylo[8 + j, :, cut].astype(F32), yhi[8 + j, :, cut].astype(F32)
            v, w = a[ax, :, cut].astype(F32), i[ix, :, cut].astype(F32)

            def joined(first, second):
                if half:
                    second = pltpu.roll(second, 64, 1)
                else:
                    first = pltpu.roll(first, 64, 1)
                return jnp.where(low_half(first.shape), first, second)

            held[row + 2 : row + 10] = joined(v, w)
            for at, pair in ((row + 1, below), (row + 10, above)):
                first, second = jnp.broadcast_to(pair[0:1], (8, 128)), jnp.broadcast_to(pair[1:2], (8, 128))
                held[at : at + 1] = joined(first, second)[0:1]
        out[...] = held[...].astype(B16)


def bands_kernel(weights, one, two, flat, turned):
    count, rows = weights.shape[0], weights.shape[1] // 2
    block = lax.broadcasted_iota(jnp.int32, (CH, 256), 1) // CH
    for which, out in enumerate((one, two)):
        flat[...] = jnp.zeros_like(flat)
        for g in range(count):
            value = weights[g].astype(F32)[which * rows : (which + 1) * rows]
            flat[g * rows : (g + 1) * rows, 256 : 256 + 27 * CH] = value
        turned[...] = pltpu.roll(flat[...], flat.shape[1] - 64, 1)
        for m in range(9):
            for a in range(6):
                at = 4 + 3 * m + 2 - a
                source = turned if at % 2 else flat
                lane = at // 2 * 128
                valid = (block + 2 - a >= 0) & (block - a <= 0)
                value = jnp.where(valid, source[:, lane : lane + 256], 0.0)
                out[m * BAND + a * CH : m * BAND + (a + 1) * CH, :] = value.astype(B16)


def fill_wide(field, layers, ylo, yhi, zlo, zhi):
    field[...] = jnp.zeros_like(field)
    for at, (ref, x) in enumerate(layers):
        row = 16 * (at + 1)
        field[row : row + 8, 128 : 128 + LANES] = ref[x].astype(F32)
        field[row - 2 : row, 128 : 128 + LANES] = ylo[at].astype(F32)
        field[row + 8 : row + 10, 128 : 128 + LANES] = yhi[at].astype(F32)
        for side, lane in ((zlo, 0), (zhi, 128 + LANES)):
            field[row - 2 : row + 10, lane : lane + 128] = side[12 * at : 12 * at + 12]


def fill_thin(field, layers, second, ylo, yhi, zlo, zhi):
    field[...] = jnp.zeros_like(field)
    for j, (ref, x) in enumerate(layers):
        at, row = 8 + j, 16 * (j + 2)
        field[row : row + 8, 128 : 128 + LANES] = ref[x].astype(F32)
        field[row - 1 : row, 128 : 128 + LANES] = ylo[at].astype(F32)[second : second + 1]
        field[row + 8 : row + 9, 128 : 128 + LANES] = yhi[at].astype(F32)[second : second + 1]
        for side, lane, upper in ((zlo, 0, True), (zhi, 128 + LANES, False)):
            value = side[12 * at : 12 * at + 12]
            if upper != bool(second):
                value = pltpu.roll(value, 64, 1)
            value = jnp.where(low_half(value.shape) != upper, value, 0.0)
            field[row - 1 : row, lane : lane + 128] = value[1:2]
            field[row : row + 8, lane : lane + 128] = value[2:10]
            field[row + 8 : row + 9, lane : lane + 128] = value[10:11]


def spread(value, steps, sign):
    moved = pltpu.roll(value, 64, 1)
    for i, dy in enumerate((-1, 0, 1)):
        by = (-sign * dy) % ROWS
        steps[i] = (pltpu.roll(moved, by, 0) if by else moved).astype(B16)


def own_columns(steps, columns, sign):
    for m in range(9):
        dx, dy = m // 3 - 1, m % 3
        row = OWN + sign * 16 * dx
        for h in range(4):
            columns[64 * h : 64 * (h + 1), BAND * m : BAND * (m + 1)] = steps[
                dy, row : row + 64, 256 * h + 128 : 256 * h + 128 + BAND
            ]


def main_kernel(scale, grad, pre, inp, xlo, xhi, ylo, yhi, below, above, band,
                kept, sent, pre_out, fg, fa, fi, steps, columns, many, left, left_f, grads_one, grads_two, held, zlo, zhi):
    wide, acts, inputs = fields_of(grad, pre, inp, xlo, xhi)
    zlo[...] = below[...].astype(F32)
    zhi[...] = above[...].astype(F32)
    halos = (ylo, yhi, zlo, zhi)
    fill_wide(fg, wide, *halos)
    fill_thin(fa, acts, 0, *halos)
    fill_thin(fi, inputs, 1, *halos)
    contract = (((0,), (0,)), ((), ()))

    v = fa[...]
    spread((v * jax.nn.sigmoid(v)).astype(B16).astype(F32), steps, 1)
    own_columns(steps, columns, 1)
    left_f[...] = jnp.zeros_like(left_f)
    for h in range(4):
        for x in range(SX):
            row = 64 * h + 16 * x
            left_f[row : row + 8, :] = grad[x, :, 256 * h : 256 * (h + 1)].astype(F32)
    left[...] = left_f[...].astype(B16)
    grads_two[...] = lax.dot_general(left[...], columns[...], contract, preferred_element_type=F32)

    spread(fg[...], steps, -1)
    for m in range(9):
        dx, dy = m // 3 - 1, m % 3
        row = 16 - 16 * dx
        for h in range(5):
            many[HALO_ROWS * h : HALO_ROWS * (h + 1), BAND * m : BAND * (m + 1)] = steps[
                dy, row : row + HALO_ROWS, 256 * h : 256 * h + BAND
            ]
    held[...] = jnp.dot(many[...], band[...], preferred_element_type=F32)
    fg[...] = jnp.zeros_like(fg)
    for h in range(5):
        v = fa[16 : 16 + HALO_ROWS, 256 * h : 256 * (h + 1)]
        g = jax.nn.sigmoid(v)
        value = held[HALO_ROWS * h : HALO_ROWS * (h + 1), :] * (g * (1.0 + v * (1.0 - g)))
        fg[16 : 16 + HALO_ROWS, 256 * h : 256 * (h + 1)] = value.astype(B16).astype(F32)
    pre_out[...] = pltpu.roll(fg[...], 64, 1).astype(B16)

    spread(fi[...], steps, 1)
    own_columns(steps, columns, 1)
    inside = lax.broadcasted_iota(jnp.int32, (64, 256), 0) % 16 < 8
    for h in range(4):
        value = fg[OWN : OWN + 64, 256 * h + 128 : 256 * h + 384]
        left[64 * h : 64 * (h + 1), :] = jnp.where(inside, value, 0.0).astype(B16)
    grads_one[...] = lax.dot_general(left[...], columns[...], contract, preferred_element_type=F32)

    count, rows = kept.shape[0], kept.shape[1]
    even = lax.rem(lax.axis_index("gz"), 2) == 0

    def block(source, k):
        m, t = k // 3, k % 3
        same, other = [], []
        for b in range(4):
            lane = (6 * m + b + t) // 2 * 128
            piece = source[64 * b : 64 * (b + 1), lane : lane + 128]
            (same if (b + t) % 2 == k % 2 else other).append(piece)
        return (same[0] + same[1]) + pltpu.roll(other[0] + other[1], 64, 1)

    for j in range(14):
        pair = []
        for source in (grads_one, grads_two):
            value = block(source, 2 * j)
            if j < 13:
                value = jnp.where(low_half(value.shape), value, block(source, 2 * j + 1))
            pair.append(value * scale)
        width = 128 if j < 13 else 64
        keep = jnp.where(even, pair[0], pair[1])[:, :width]
        send = jnp.where(even, pair[1], pair[0])[:, :width]
        for g in range(count):
            kept[g, :, 128 * j : 128 * j + width] = keep[g * rows : (g + 1) * rows, :]
            sent[g, :, 128 * j : 128 * j + width] = send[g * rows : (g + 1) * rows, :].astype(B16)


def last_kernel(pre_grad, grad, band, out, steps, columns, held):
    value = pre_grad[...].astype(F32)
    for i, dy in enumerate((-1, 0, 1)):
        steps[i] = (pltpu.roll(value, dy % ROWS, 0) if dy else value).astype(B16)
    own_columns(steps, columns, -1)
    held[...] = jnp.dot(columns[...], band[...], preferred_element_type=F32)
    for h in range(4):
        for x in range(SX):
            row, lanes = 64 * h + 16 * x, slice(256 * h, 256 * (h + 1))
            out[x, :, lanes] = (held[row : row + 8, :] + grad[x, :, lanes].astype(F32)).astype(B16)


def swapped(low, high, axis):
    count = lax.axis_size(axis)
    up = [(i, (i + 1) % count) for i in range(count)]
    down = [(target, source) for source, target in up]
    return lax.ppermute(high, axis, up), lax.ppermute(low, axis, down)


def total_kernel(parts, out):
    value = parts[0].astype(F32)
    for i in range(1, parts.shape[0]):
        value += parts[i].astype(F32)
    value = value.astype(out.dtype)
    if out.ndim == value.ndim:
        out[...] = value
    else:
        for i in range(out.shape[0]):
            out[i] = value


def pair_kernel(kept, came, out):
    out[...] = (kept[...] + came[...].astype(F32)).astype(B16)


def last_total_kernel(parts, one, two):
    first, second = parts[0], parts[1]
    for i in range(2, parts.shape[0], 2):
        first += parts[i]
        second += parts[i + 1]
    one[...] = first
    two[...] = second


def reduced(kept, sent, other):
    rows, columns = kept.shape[1:]
    gy, gz = lax.axis_size("gy"), lax.axis_size("gz")
    came = lax.ppermute(sent, "gz", [(i, i + 1 - 2 * (i % 2)) for i in range(gz)])
    came, other = lax.optimization_barrier((came, other))
    (slots,) = call(pair_kernel, [(kept.shape, B16)], [], 1000, 500000, kept, came)
    parts = lax.all_to_all(slots, "gx", 0, 0, tiled=True)
    (copies,) = call(total_kernel, [((gy, rows, columns), B16)], [], 1000, 500000, parts)
    parts = lax.all_to_all(copies, "gy", 0, 0, tiled=True)
    (part,) = call(total_kernel, [((rows, columns), F32)], [], 1000, 500000, parts)
    parts = lax.all_gather(part, "gz", axis=0)
    grads = ((rows, columns), F32)
    one, two = call(last_total_kernel, [grads, grads], [], 1000, 500000, parts)
    return other, one, two


def body(block_input, pre_act, skip_grad, pool_grad, conv1_weight, conv2_weight):
    count = lax.axis_size("gx")
    rows = CH // count
    cells = SX * SY * SZ * count * lax.axis_size("gy") * lax.axis_size("gz")
    block, message = ((SX, SY, LANES), B16), ((4, SY, LANES), B16)
    weight = ((rows, 27 * CH), B16)
    grad, pre, inp, low, high, copies = call(
        prep_kernel,
        [block, block, block, message, message, ((count, 2 * rows, 27 * CH), B16)],
        [
            block, ((SX // 2, SY // 2, LANES // 2), B16), weight, weight,
            ((SX // 2, SY, LANES), F32), ((2 * rows, 27 * CH), F32), pltpu.SemaphoreType.DMA((6,)),
        ],
        100000, 400000,
        *(
            pltpu.with_memory_space_constraint(array, pltpu.HBM)
            for array in (skip_grad, pool_grad, pre_act, block_input, conv1_weight, conv2_weight)
        ),
        space=pltpu.HBM,
    )
    xlo, xhi = swapped(low, high, "gx")
    fields = (grad, pre, inp, xlo, xhi)
    message = ((LAYERS, 2, LANES), B16)
    ylo, yhi = swapped(
        *call(ypack_kernel, [message, message], [((2, LANES), F32)], 60000000000, 600000, *fields), "gy"
    )
    side = ((12 * LAYERS, 128), F32)
    gathered = lax.all_to_all(copies, "gx", 0, 0, tiled=True)
    message = ((12 * LAYERS, 128), B16)
    below, above = swapped(
        *call(zpack_kernel, [message, message], [side], 100000, 700000, *fields, ylo, yhi), "gz"
    )
    matrix = ((DEPTH, 256), B16)
    flat = ((CH, 36 * CH), F32)
    band_one, band_two = call(bands_kernel, [matrix, matrix], [flat, flat], 1000000, 4000000, gathered)
    field = ((ROWS, WIDE), F32)
    steps = ((3, ROWS, WIDE), B16)
    columns = ((256, DEPTH), B16)
    kept, sent, pre_grad = call(
        functools.partial(main_kernel, 1.0 / math.sqrt(cells)),
        [((count, rows, 27 * CH), F32), ((count, rows, 27 * CH), B16), ((ROWS, WIDE), B16)],
        [
            field, field, field, steps, columns,
            ((5 * HALO_ROWS, DEPTH), B16), ((256, 256), B16), ((256, 256), F32),
            ((256, DEPTH), F32), ((256, DEPTH), F32), ((5 * HALO_ROWS, 256), F32), side, side,
        ],
        2 * 900 * 1000 * 1000, 8000000,
        *fields, ylo, yhi, below, above, band_two,
        grant=32,
    )
    (input_grad,) = call(
        last_kernel,
        [((SX, SY, LANES), B16)],
        [steps, columns, ((256, 256), F32)],
        500000000, 4000000,
        pre_grad, grad, band_one,
    )
    return reduced(kept, sent, input_grad)


def solution(mesh):
    in_specs = (
        P("gx", "gy", "gz"),
        P("gx", "gy", "gz"),
        P("gx", "gy", "gz"),
        P("gx", "gy", "gz"),
        P("gx", None),
        P("gx", None),
    )
    out_specs = (P("gx", "gy", "gz"), P("gx", None), P("gx", None))
    return jax.shard_map(body, mesh=mesh, in_specs=in_specs, out_specs=out_specs, check_vma=False)
```

```python
import functools
import math

import jax
import jax.numpy as jnp
from jax import lax
from jax.experimental import pallas as pl
from jax.experimental.pallas import tpu as pltpu
from jax.sharding import PartitionSpec as P

F32, B16 = jnp.float32, jnp.bfloat16
SX, SY, SZ, CH = 4, 8, 16, 64
LANES = SZ * CH
ROWS = 16 * (SX + 5)
WIDE = LANES + 6 * CH
BAND = 6 * CH
DEPTH = 9 * BAND
OWN = 16 * 3
HALO_ROWS = 16 * (SX + 3)
LAYERS = 14


def call(kernel, outs, scratch, flops, moved, *args, space=pltpu.VMEM, grant=12):
    return pl.pallas_call(
        kernel,
        out_shape=[jax.ShapeDtypeStruct(shape, dtype) for shape, dtype in outs],
        in_specs=[pl.BlockSpec(memory_space=space)] * len(args),
        out_specs=[pl.BlockSpec(memory_space=pltpu.VMEM)] * len(outs),
        scratch_shapes=[pltpu.VMEM(*held) if isinstance(held, tuple) else held for held in scratch],
        compiler_params=pltpu.CompilerParams(vmem_limit_bytes=grant * 1024 * 1024),
        cost_estimate=pl.CostEstimate(flops=flops, bytes_accessed=moved, transcendentals=0),
    )(*args)


def low_half(shape):
    return lax.broadcasted_iota(jnp.int32, shape, len(shape) - 1) % 128 < 64


class Either:
    def __init__(self, axis, if_odd, if_even):
        self.odd = lax.rem(lax.axis_index(axis), 2) == 1
        self.refs = if_odd, if_even

    def __getitem__(self, at):
        first, second = (ref[at].astype(F32) for ref in self.refs)
        return jnp.where(self.odd, first, second)


def below_above(axis, far, near):
    return Either(axis, near, far), Either(axis, far, near)


def far_near(axis, low, high):
    odd = lax.rem(lax.axis_index(axis), 2) == 1
    return jnp.where(odd, high, low).astype(B16), jnp.where(odd, low, high).astype(B16)


def prep_kernel(skip_in, pool_in, pre_in, inp_in, one_in, two_in,
                grad, pre, inp, far, near, copies, skip, pool, one, two, up, rows, sems):
    moves = [
        pltpu.make_async_copy(source, target, sems.at[i])
        for i, (source, target) in enumerate(
            ((skip_in, skip), (pool_in, pool), (pre_in, pre), (inp_in, inp), (one_in, one), (two_in, two))
        )
    ]
    for move in moves:
        move.start()
    for move in moves:
        move.wait()
    each = one.shape[0]
    rows[0:each], rows[each : 2 * each] = one[...].astype(F32), two[...].astype(F32)
    both = rows[...].astype(B16)
    for g in range(copies.shape[0]):
        copies[g] = both
    for px in range(SX // 2):
        pieces = []
        for j in range(LANES // 256):
            v = pool[px, :, 128 * j : 128 * (j + 1)].astype(F32)
            turned = pltpu.roll(v, 64, 1)
            first = low_half(v.shape)
            pieces += [jnp.where(first, v, turned), jnp.where(first, turned, v)]
        for y in range(SY):
            for j, piece in enumerate(pieces):
                up[px, y : y + 1, 128 * j : 128 * (j + 1)] = piece[y // 2 : y // 2 + 1, :]
    for x in range(SX):
        value = (skip[x].astype(F32) + 0.125 * up[x // 2]).astype(B16)
        grad[x] = value
    ends = ((grad, 0, 2), (grad, 1, 3), (pre, 0, SX - 1), (inp, 0, SX - 1))
    for at, (ref, bottom, top) in enumerate(ends):
        far[at], near[at] = far_near("gx", ref[bottom].astype(F32), ref[top].astype(F32))


def fields_of(grad, pre, inp, xlo, xhi):
    def own(ref):
        return [(ref, x) for x in range(SX)]

    return (
        [(xlo, 0), (xlo, 1)] + own(grad) + [(xhi, 0), (xhi, 1)],
        [(xlo, 2)] + own(pre) + [(xhi, 2)],
        [(xlo, 3)] + own(inp) + [(xhi, 3)],
    )


def ypack_kernel(grad, pre, inp, xfar, xnear, far, near, held):
    wide, acts, inputs = fields_of(grad, pre, inp, *below_above("gx", xfar, xnear))
    for at, (ref, x) in enumerate(wide):
        value = ref[x].astype(F32)
        far[at], near[at] = far_near("gy", value[0:2], value[SY - 2 : SY])
    for at, ((a, ax), (i, ix)) in enumerate(zip(acts, inputs)):
        v, w = a[ax].astype(F32), i[ix].astype(F32)
        held[0:1], held[1:2] = v[0:1], w[0:1]
        held[2:3], held[3:4] = v[SY - 1 :], w[SY - 1 :]
        far[8 + at], near[8 + at] = far_near("gy", held[0:2], held[2:4])


def zpack_kernel(grad, pre, inp, xfar, xnear, yfar, ynear, far, near, low, high):
    wide, acts, inputs = fields_of(grad, pre, inp, *below_above("gx", xfar, xnear))
    ylo, yhi = below_above("gy", yfar, ynear)
    for held, lane, half in ((low, 0, True), (high, LANES - 128, False)):
        held[...] = jnp.zeros_like(held)
        cut = slice(lane, lane + 128)
        for at, (ref, x) in enumerate(wide):
            row = 12 * at
            held[row : row + 2] = ylo[at, :, cut].astype(F32)
            held[row + 2 : row + 10] = ref[x, :, cut].astype(F32)
            held[row + 10 : row + 12] = yhi[at, :, cut].astype(F32)
        for j, ((a, ax), (i, ix)) in enumerate(zip(acts, inputs)):
            row = 12 * (8 + j)
            below, above = ylo[8 + j, :, cut].astype(F32), yhi[8 + j, :, cut].astype(F32)
            v, w = a[ax, :, cut].astype(F32), i[ix, :, cut].astype(F32)

            def joined(first, second):
                if half:
                    second = pltpu.roll(second, 64, 1)
                else:
                    first = pltpu.roll(first, 64, 1)
                return jnp.where(low_half(first.shape), first, second)

            held[row + 2 : row + 10] = joined(v, w)
            for at, pair in ((row + 1, below), (row + 10, above)):
                first, second = jnp.broadcast_to(pair[0:1], (8, 128)), jnp.broadcast_to(pair[1:2], (8, 128))
                held[at : at + 1] = joined(first, second)[0:1]
    far[...], near[...] = far_near("gz", low[...], high[...])


def bands_kernel(weights, one, two, flat, turned):
    count, rows = weights.shape[0], weights.shape[1] // 2
    block = lax.broadcasted_iota(jnp.int32, (CH, 256), 1) // CH
    for which, out in enumerate((one, two)):
        flat[...] = jnp.zeros_like(flat)
        for g in range(count):
            value = weights[g].astype(F32)[which * rows : (which + 1) * rows]
            flat[g * rows : (g + 1) * rows, 256 : 256 + 27 * CH] = value
        turned[...] = pltpu.roll(flat[...], flat.shape[1] - 64, 1)
        for m in range(9):
            for a in range(6):
                at = 4 + 3 * m + 2 - a
                source = turned if at % 2 else flat
                lane = at // 2 * 128
                valid = (block + 2 - a >= 0) & (block - a <= 0)
                value = jnp.where(valid, source[:, lane : lane + 256], 0.0)
                out[m * BAND + a * CH : m * BAND + (a + 1) * CH, :] = value.astype(B16)


def fill_wide(field, layers, ylo, yhi, zlo, zhi):
    field[...] = jnp.zeros_like(field)
    for at, (ref, x) in enumerate(layers):
        row = 16 * (at + 1)
        field[row : row + 8, 128 : 128 + LANES] = ref[x].astype(F32)
        field[row - 2 : row, 128 : 128 + LANES] = ylo[at].astype(F32)
        field[row + 8 : row + 10, 128 : 128 + LANES] = yhi[at].astype(F32)
        for side, lane in ((zlo, 0), (zhi, 128 + LANES)):
            field[row - 2 : row + 10, lane : lane + 128] = side[12 * at : 12 * at + 12]


def fill_thin(field, layers, second, ylo, yhi, zlo, zhi):
    field[...] = jnp.zeros_like(field)
    for j, (ref, x) in enumerate(layers):
        at, row = 8 + j, 16 * (j + 2)
        field[row : row + 8, 128 : 128 + LANES] = ref[x].astype(F32)
        field[row - 1 : row, 128 : 128 + LANES] = ylo[at].astype(F32)[second : second + 1]
        field[row + 8 : row + 9, 128 : 128 + LANES] = yhi[at].astype(F32)[second : second + 1]
        for side, lane, upper in ((zlo, 0, True), (zhi, 128 + LANES, False)):
            value = side[12 * at : 12 * at + 12]
            if upper != bool(second):
                value = pltpu.roll(value, 64, 1)
            value = jnp.where(low_half(value.shape) != upper, value, 0.0)
            field[row - 1 : row, lane : lane + 128] = value[1:2]
            field[row : row + 8, lane : lane + 128] = value[2:10]
            field[row + 8 : row + 9, lane : lane + 128] = value[10:11]


def spread(value, steps, sign):
    moved = pltpu.roll(value, 64, 1)
    for i, dy in enumerate((-1, 0, 1)):
        by = (-sign * dy) % ROWS
        steps[i] = (pltpu.roll(moved, by, 0) if by else moved).astype(B16)


def own_columns(steps, columns, sign):
    for m in range(9):
        dx, dy = m // 3 - 1, m % 3
        row = OWN + sign * 16 * dx
        for h in range(4):
            columns[64 * h : 64 * (h + 1), BAND * m : BAND * (m + 1)] = steps[
                dy, row : row + 64, 256 * h + 128 : 256 * h + 128 + BAND
            ]


def main_kernel(scale, grad, pre, inp, xfar, xnear, yfar, ynear, zfar, znear, band,
                kept, sent, pre_out, fg, fa, fi, steps, columns, many, left, left_f, grads_one, grads_two, held, zlo, zhi):
    wide, acts, inputs = fields_of(grad, pre, inp, *below_above("gx", xfar, xnear))
    ylo, yhi = below_above("gy", yfar, ynear)
    below, above = below_above("gz", zfar, znear)
    zlo[...] = below[...]
    zhi[...] = above[...]
    halos = (ylo, yhi, zlo, zhi)
    fill_wide(fg, wide, *halos)
    fill_thin(fa, acts, 0, *halos)
    fill_thin(fi, inputs, 1, *halos)
    contract = (((0,), (0,)), ((), ()))

    v = fa[...]
    spread((v * jax.nn.sigmoid(v)).astype(B16).astype(F32), steps, 1)
    own_columns(steps, columns, 1)
    left_f[...] = jnp.zeros_like(left_f)
    for h in range(4):
        for x in range(SX):
            row = 64 * h + 16 * x
            left_f[row : row + 8, :] = grad[x, :, 256 * h : 256 * (h + 1)].astype(F32)
    left[...] = left_f[...].astype(B16)
    grads_two[...] = lax.dot_general(left[...], columns[...], contract, preferred_element_type=F32)

    spread(fg[...], steps, -1)
    for m in range(9):
        dx, dy = m // 3 - 1, m % 3
        row = 16 - 16 * dx
        for h in range(5):
            many[HALO_ROWS * h : HALO_ROWS * (h + 1), BAND * m : BAND * (m + 1)] = steps[
                dy, row : row + HALO_ROWS, 256 * h : 256 * h + BAND
            ]
    held[...] = jnp.dot(many[...], band[...], preferred_element_type=F32)
    fg[...] = jnp.zeros_like(fg)
    for h in range(5):
        v = fa[16 : 16 + HALO_ROWS, 256 * h : 256 * (h + 1)]
        g = jax.nn.sigmoid(v)
        value = held[HALO_ROWS * h : HALO_ROWS * (h + 1), :] * (g * (1.0 + v * (1.0 - g)))
        fg[16 : 16 + HALO_ROWS, 256 * h : 256 * (h + 1)] = value.astype(B16).astype(F32)
    pre_out[...] = pltpu.roll(fg[...], 64, 1).astype(B16)

    spread(fi[...], steps, 1)
    own_columns(steps, columns, 1)
    inside = lax.broadcasted_iota(jnp.int32, (64, 256), 0) % 16 < 8
    for h in range(4):
        value = fg[OWN : OWN + 64, 256 * h + 128 : 256 * h + 384]
        left[64 * h : 64 * (h + 1), :] = jnp.where(inside, value, 0.0).astype(B16)
    grads_one[...] = lax.dot_general(left[...], columns[...], contract, preferred_element_type=F32)

    count, rows = kept.shape[0], kept.shape[1]
    even = lax.rem(lax.axis_index("gz"), 2) == 0

    def block(source, k):
        m, t = k // 3, k % 3
        same, other = [], []
        for b in range(4):
            lane = (6 * m + b + t) // 2 * 128
            piece = source[64 * b : 64 * (b + 1), lane : lane + 128]
            (same if (b + t) % 2 == k % 2 else other).append(piece)
        return (same[0] + same[1]) + pltpu.roll(other[0] + other[1], 64, 1)

    for j in range(14):
        pair = []
        for source in (grads_one, grads_two):
            value = block(source, 2 * j)
            if j < 13:
                value = jnp.where(low_half(value.shape), value, block(source, 2 * j + 1))
            pair.append(value * scale)
        width = 128 if j < 13 else 64
        keep = jnp.where(even, pair[0], pair[1])[:, :width]
        send = jnp.where(even, pair[1], pair[0])[:, :width]
        for g in range(count):
            kept[g, :, 128 * j : 128 * j + width] = keep[g * rows : (g + 1) * rows, :]
            sent[g, :, 128 * j : 128 * j + width] = send[g * rows : (g + 1) * rows, :].astype(B16)


def last_kernel(pre_grad, grad, band, out, steps, columns, held):
    value = pre_grad[...].astype(F32)
    for i, dy in enumerate((-1, 0, 1)):
        steps[i] = (pltpu.roll(value, dy % ROWS, 0) if dy else value).astype(B16)
    own_columns(steps, columns, -1)
    held[...] = jnp.dot(columns[...], band[...], preferred_element_type=F32)
    for h in range(4):
        for x in range(SX):
            row, lanes = 64 * h + 16 * x, slice(256 * h, 256 * (h + 1))
            out[x, :, lanes] = (held[row : row + 8, :] + grad[x, :, lanes].astype(F32)).astype(B16)


def swapped(far, near, axis):
    count = lax.axis_size(axis)
    steps = [1 if i % 2 else -1 for i in range(count)]
    return (
        lax.ppermute(far, axis, [(i, (i + step) % count) for i, step in enumerate(steps)]),
        lax.ppermute(near, axis, [(i, i - step) for i, step in enumerate(steps)]),
    )


def total_kernel(parts, out):
    value = parts[0].astype(F32)
    for i in range(1, parts.shape[0]):
        value += parts[i].astype(F32)
    value = value.astype(out.dtype)
    if out.ndim == value.ndim:
        out[...] = value
    else:
        for i in range(out.shape[0]):
            out[i] = value


def pair_kernel(kept, came, out):
    out[...] = (kept[...] + came[...].astype(F32)).astype(B16)


def last_total_kernel(parts, one, two):
    first, second = parts[0], parts[1]
    for i in range(2, parts.shape[0], 2):
        first += parts[i]
        second += parts[i + 1]
    one[...] = first
    two[...] = second


def reduced(kept, sent, other):
    rows, columns = kept.shape[1:]
    gy, gz = lax.axis_size("gy"), lax.axis_size("gz")
    came = lax.ppermute(sent, "gz", [(i, i + 1 - 2 * (i % 2)) for i in range(gz)])
    came, other = lax.optimization_barrier((came, other))
    (slots,) = call(pair_kernel, [(kept.shape, B16)], [], 1000, 500000, kept, came)
    parts = lax.all_to_all(slots, "gx", 0, 0, tiled=True)
    (copies,) = call(total_kernel, [((gy, rows, columns), B16)], [], 1000, 500000, parts)
    parts = lax.all_to_all(copies, "gy", 0, 0, tiled=True)
    (part,) = call(total_kernel, [((rows, columns), F32)], [], 1000, 500000, parts)
    parts = lax.all_gather(part, "gz", axis=0)
    grads = ((rows, columns), F32)
    one, two = call(last_total_kernel, [grads, grads], [], 1000, 500000, parts)
    return other, one, two


def body(block_input, pre_act, skip_grad, pool_grad, conv1_weight, conv2_weight):
    count = lax.axis_size("gx")
    rows = CH // count
    cells = SX * SY * SZ * count * lax.axis_size("gy") * lax.axis_size("gz")
    block, message = ((SX, SY, LANES), B16), ((4, SY, LANES), B16)
    weight = ((rows, 27 * CH), B16)
    grad, pre, inp, far, near, copies = call(
        prep_kernel,
        [block, block, block, message, message, ((count, 2 * rows, 27 * CH), B16)],
        [
            block, ((SX // 2, SY // 2, LANES // 2), B16), weight, weight,
            ((SX // 2, SY, LANES), F32), ((2 * rows, 27 * CH), F32), pltpu.SemaphoreType.DMA((6,)),
        ],
        100000, 400000,
        *(
            pltpu.with_memory_space_constraint(array, pltpu.HBM)
            for array in (skip_grad, pool_grad, pre_act, block_input, conv1_weight, conv2_weight)
        ),
        space=pltpu.HBM,
    )
    xfar, xnear = swapped(far, near, "gx")
    fields = (grad, pre, inp, xfar, xnear)
    message = ((LAYERS, 2, LANES), B16)
    yfar, ynear = swapped(
        *call(ypack_kernel, [message, message], [((4, LANES), F32)], 60000000000, 600000, *fields), "gy"
    )
    side = ((12 * LAYERS, 128), F32)
    gathered = lax.all_to_all(copies, "gx", 0, 0, tiled=True)
    message = ((12 * LAYERS, 128), B16)
    zfar, znear = swapped(
        *call(zpack_kernel, [message, message], [side, side], 100000, 700000, *fields, yfar, ynear), "gz"
    )
    matrix = ((DEPTH, 256), B16)
    flat = ((CH, 36 * CH), F32)
    band_one, band_two = call(bands_kernel, [matrix, matrix], [flat, flat], 1000000, 4000000, gathered)
    field = ((ROWS, WIDE), F32)
    steps = ((3, ROWS, WIDE), B16)
    columns = ((256, DEPTH), B16)
    kept, sent, pre_grad = call(
        functools.partial(main_kernel, 1.0 / math.sqrt(cells)),
        [((count, rows, 27 * CH), F32), ((count, rows, 27 * CH), B16), ((ROWS, WIDE), B16)],
        [
            field, field, field, steps, columns,
            ((5 * HALO_ROWS, DEPTH), B16), ((256, 256), B16), ((256, 256), F32),
            ((256, DEPTH), F32), ((256, DEPTH), F32), ((5 * HALO_ROWS, 256), F32), side, side,
        ],
        2 * 900 * 1000 * 1000, 8000000,
        *fields, yfar, ynear, zfar, znear, band_two,
        grant=32,
    )
    (input_grad,) = call(
        last_kernel,
        [((SX, SY, LANES), B16)],
        [steps, columns, ((256, 256), F32)],
        500000000, 4000000,
        pre_grad, grad, band_one,
    )
    return reduced(kept, sent, input_grad)


def solution(mesh):
    in_specs = (
        P("gx", "gy", "gz"),
        P("gx", "gy", "gz"),
        P("gx", "gy", "gz"),
        P("gx", "gy", "gz"),
        P("gx", None),
        P("gx", None),
    )
    out_specs = (P("gx", "gy", "gz"), P("gx", None), P("gx", None))
    return jax.shard_map(body, mesh=mesh, in_specs=in_specs, out_specs=out_specs, check_vma=False)
```

```python
import functools
import math

import jax
import jax.numpy as jnp
from jax import lax
from jax.experimental import pallas as pl
from jax.experimental.pallas import tpu as pltpu
from jax.sharding import PartitionSpec as P

F32, B16 = jnp.float32, jnp.bfloat16
SX, SY, SZ, CH = 4, 8, 16, 64
LANES = SZ * CH
ROWS = 16 * (SX + 5)
WIDE = LANES + 6 * CH
BAND = 6 * CH
DEPTH = 9 * BAND
OWN = 16 * 3
HALO_ROWS = 16 * (SX + 3)
LAYERS = 14


def call(kernel, outs, scratch, flops, moved, *args, space=pltpu.VMEM, grant=12):
    return pl.pallas_call(
        kernel,
        out_shape=[jax.ShapeDtypeStruct(shape, dtype) for shape, dtype in outs],
        in_specs=[pl.BlockSpec(memory_space=space)] * len(args),
        out_specs=[pl.BlockSpec(memory_space=pltpu.VMEM)] * len(outs),
        scratch_shapes=[pltpu.VMEM(*held) if isinstance(held, tuple) else held for held in scratch],
        compiler_params=pltpu.CompilerParams(vmem_limit_bytes=grant * 1024 * 1024),
        cost_estimate=pl.CostEstimate(flops=flops, bytes_accessed=moved, transcendentals=0),
    )(*args)


def low_half(shape):
    return lax.broadcasted_iota(jnp.int32, shape, len(shape) - 1) % 128 < 64


class Either:
    def __init__(self, axis, if_odd, if_even):
        self.odd = lax.rem(lax.axis_index(axis), 2) == 1
        self.refs = if_odd, if_even

    def __getitem__(self, at):
        first, second = (ref[at].astype(F32) for ref in self.refs)
        return jnp.where(self.odd, first, second)


def below_above(axis, far, near):
    return Either(axis, near, far), Either(axis, far, near)


def far_near(axis, low, high):
    odd = lax.rem(lax.axis_index(axis), 2) == 1
    return jnp.where(odd, high, low).astype(B16), jnp.where(odd, low, high).astype(B16)


def prep_kernel(skip_in, pool_in, pre_in, inp_in, one_in, two_in,
                grad, pre, inp, far, near, copies, skip, pool, one, two, up, rows, sems):
    moves = [
        pltpu.make_async_copy(source, target, sems.at[i])
        for i, (source, target) in enumerate(
            ((skip_in, skip), (pool_in, pool), (pre_in, pre), (inp_in, inp), (one_in, one), (two_in, two))
        )
    ]
    for move in moves:
        move.start()
    for move in moves:
        move.wait()
    each = one.shape[0]
    rows[0:each], rows[each : 2 * each] = one[...].astype(F32), two[...].astype(F32)
    both = rows[...].astype(B16)
    for g in range(copies.shape[0]):
        copies[g] = both
    for px in range(SX // 2):
        pieces = []
        for j in range(LANES // 256):
            v = pool[px, :, 128 * j : 128 * (j + 1)].astype(F32)
            turned = pltpu.roll(v, 64, 1)
            first = low_half(v.shape)
            pieces += [jnp.where(first, v, turned), jnp.where(first, turned, v)]
        for y in range(SY):
            for j, piece in enumerate(pieces):
                up[px, y : y + 1, 128 * j : 128 * (j + 1)] = piece[y // 2 : y // 2 + 1, :]
    for x in range(SX):
        value = (skip[x].astype(F32) + 0.125 * up[x // 2]).astype(B16)
        grad[x] = value
    ends = ((grad, 0, 2), (grad, 1, 3), (pre, 0, SX - 1), (inp, 0, SX - 1))
    for at, (ref, bottom, top) in enumerate(ends):
        far[at], near[at] = far_near("gx", ref[bottom].astype(F32), ref[top].astype(F32))


def fields_of(grad, pre, inp, xlo, xhi):
    def own(ref):
        return [(ref, x) for x in range(SX)]

    return (
        [(xlo, 0), (xlo, 1)] + own(grad) + [(xhi, 0), (xhi, 1)],
        [(xlo, 2)] + own(pre) + [(xhi, 2)],
        [(xlo, 3)] + own(inp) + [(xhi, 3)],
    )


def ypack_kernel(grad, pre, inp, xfar, xnear, far, near, held):
    wide, acts, inputs = fields_of(grad, pre, inp, *below_above("gx", xfar, xnear))
    for at, (ref, x) in enumerate(wide):
        value = ref[x].astype(F32)
        far[at], near[at] = far_near("gy", value[0:2], value[SY - 2 : SY])
    for at, ((a, ax), (i, ix)) in enumerate(zip(acts, inputs)):
        v, w = a[ax].astype(F32), i[ix].astype(F32)
        held[0:1], held[1:2] = v[0:1], w[0:1]
        held[2:3], held[3:4] = v[SY - 1 :], w[SY - 1 :]
        far[8 + at], near[8 + at] = far_near("gy", held[0:2], held[2:4])


def zpack_kernel(grad, pre, inp, xfar, xnear, yfar, ynear, far, near, low, high):
    wide, acts, inputs = fields_of(grad, pre, inp, *below_above("gx", xfar, xnear))
    ylo, yhi = below_above("gy", yfar, ynear)
    for held, lane, half in ((low, 0, True), (high, LANES - 128, False)):
        held[...] = jnp.zeros_like(held)
        cut = slice(lane, lane + 128)
        for at, (ref, x) in enumerate(wide):
            row = 12 * at
            held[row : row + 2] = ylo[at, :, cut].astype(F32)
            held[row + 2 : row + 10] = ref[x, :, cut].astype(F32)
            held[row + 10 : row + 12] = yhi[at, :, cut].astype(F32)
        for j, ((a, ax), (i, ix)) in enumerate(zip(acts, inputs)):
            row = 12 * (8 + j)
            below, above = ylo[8 + j, :, cut].astype(F32), yhi[8 + j, :, cut].astype(F32)
            v, w = a[ax, :, cut].astype(F32), i[ix, :, cut].astype(F32)

            def joined(first, second):
                if half:
                    second = pltpu.roll(second, 64, 1)
                else:
                    first = pltpu.roll(first, 64, 1)
                return jnp.where(low_half(first.shape), first, second)

            held[row + 2 : row + 10] = joined(v, w)
            for at, pair in ((row + 1, below), (row + 10, above)):
                first, second = jnp.broadcast_to(pair[0:1], (8, 128)), jnp.broadcast_to(pair[1:2], (8, 128))
                held[at : at + 1] = joined(first, second)[0:1]
    far[...], near[...] = far_near("gz", low[...], high[...])


def bands_kernel(weights, one, two, flat, turned):
    count, rows = weights.shape[0], weights.shape[1] // 2
    block = lax.broadcasted_iota(jnp.int32, (CH, 256), 1) // CH
    for which, out in enumerate((one, two)):
        flat[...] = jnp.zeros_like(flat)
        for g in range(count):
            value = weights[g].astype(F32)[which * rows : (which + 1) * rows]
            flat[g * rows : (g + 1) * rows, 256 : 256 + 27 * CH] = value
        turned[...] = pltpu.roll(flat[...], flat.shape[1] - 64, 1)
        for m in range(9):
            for a in range(6):
                at = 4 + 3 * m + 2 - a
                source = turned if at % 2 else flat
                lane = at // 2 * 128
                valid = (block + 2 - a >= 0) & (block - a <= 0)
                value = jnp.where(valid, source[:, lane : lane + 256], 0.0)
                out[m * BAND + a * CH : m * BAND + (a + 1) * CH, :] = value.astype(B16)


def fill_wide(field, layers, ylo, yhi, zlo, zhi):
    field[...] = jnp.zeros_like(field)
    for at, (ref, x) in enumerate(layers):
        row = 16 * (at + 1)
        field[row : row + 8, 128 : 128 + LANES] = ref[x].astype(F32)
        field[row - 2 : row, 128 : 128 + LANES] = ylo[at].astype(F32)
        field[row + 8 : row + 10, 128 : 128 + LANES] = yhi[at].astype(F32)
        for side, lane in ((zlo, 0), (zhi, 128 + LANES)):
            field[row - 2 : row + 10, lane : lane + 128] = side[12 * at : 12 * at + 12]


def fill_thin(field, layers, second, ylo, yhi, zlo, zhi):
    field[...] = jnp.zeros_like(field)
    for j, (ref, x) in enumerate(layers):
        at, row = 8 + j, 16 * (j + 2)
        field[row : row + 8, 128 : 128 + LANES] = ref[x].astype(F32)
        field[row - 1 : row, 128 : 128 + LANES] = ylo[at].astype(F32)[second : second + 1]
        field[row + 8 : row + 9, 128 : 128 + LANES] = yhi[at].astype(F32)[second : second + 1]
        for side, lane, upper in ((zlo, 0, True), (zhi, 128 + LANES, False)):
            value = side[12 * at : 12 * at + 12]
            if upper != bool(second):
                value = pltpu.roll(value, 64, 1)
            value = jnp.where(low_half(value.shape) != upper, value, 0.0)
            field[row - 1 : row, lane : lane + 128] = value[1:2]
            field[row : row + 8, lane : lane + 128] = value[2:10]
            field[row + 8 : row + 9, lane : lane + 128] = value[10:11]


def spread(value, steps, sign):
    moved = pltpu.roll(value, 64, 1)
    for i, dy in enumerate((-1, 0, 1)):
        by = (-sign * dy) % ROWS
        steps[i] = (pltpu.roll(moved, by, 0) if by else moved).astype(B16)


def own_columns(steps, columns, sign):
    for m in range(9):
        dx, dy = m // 3 - 1, m % 3
        row = OWN + sign * 16 * dx
        for h in range(4):
            columns[64 * h : 64 * (h + 1), BAND * m : BAND * (m + 1)] = steps[
                dy, row : row + 64, 256 * h + 128 : 256 * h + 128 + BAND
            ]


def main_kernel(scale, grad, pre, inp, xfar, xnear, yfar, ynear, zfar, znear, band,
                kept, sent, pre_out, fg, fa, fi, steps, columns, many, left, left_f, grads_one, grads_two, held, zlo, zhi):
    wide, acts, inputs = fields_of(grad, pre, inp, *below_above("gx", xfar, xnear))
    ylo, yhi = below_above("gy", yfar, ynear)
    below, above = below_above("gz", zfar, znear)
    zlo[...] = below[...]
    zhi[...] = above[...]
    halos = (ylo, yhi, zlo, zhi)
    fill_wide(fg, wide, *halos)
    fill_thin(fa, acts, 0, *halos)
    fill_thin(fi, inputs, 1, *halos)
    contract = (((0,), (0,)), ((), ()))

    v = fa[...]
    spread((v * jax.nn.sigmoid(v)).astype(B16).astype(F32), steps, 1)
    own_columns(steps, columns, 1)
    left_f[...] = jnp.zeros_like(left_f)
    for h in range(4):
        for x in range(SX):
            row = 64 * h + 16 * x
            left_f[row : row + 8, :] = grad[x, :, 256 * h : 256 * (h + 1)].astype(F32)
    left[...] = left_f[...].astype(B16)
    grads_two[...] = lax.dot_general(left[...], columns[...], contract, preferred_element_type=F32)

    spread(fg[...], steps, -1)
    for m in range(9):
        dx, dy = m // 3 - 1, m % 3
        row = 16 - 16 * dx
        for h in range(5):
            many[HALO_ROWS * h : HALO_ROWS * (h + 1), BAND * m : BAND * (m + 1)] = steps[
                dy, row : row + HALO_ROWS, 256 * h : 256 * h + BAND
            ]
    held[...] = jnp.dot(many[...], band[...], preferred_element_type=F32)
    fg[...] = jnp.zeros_like(fg)
    for h in range(5):
        v = fa[16 : 16 + HALO_ROWS, 256 * h : 256 * (h + 1)]
        g = jax.nn.sigmoid(v)
        value = held[HALO_ROWS * h : HALO_ROWS * (h + 1), :] * (g * (1.0 + v * (1.0 - g)))
        fg[16 : 16 + HALO_ROWS, 256 * h : 256 * (h + 1)] = value.astype(B16).astype(F32)
    pre_out[...] = pltpu.roll(fg[...], 64, 1).astype(B16)

    spread(fi[...], steps, 1)
    own_columns(steps, columns, 1)
    inside = lax.broadcasted_iota(jnp.int32, (64, 256), 0) % 16 < 8
    for h in range(4):
        value = fg[OWN : OWN + 64, 256 * h + 128 : 256 * h + 384]
        left[64 * h : 64 * (h + 1), :] = jnp.where(inside, value, 0.0).astype(B16)
    grads_one[...] = lax.dot_general(left[...], columns[...], contract, preferred_element_type=F32)

    count, rows = kept.shape[0], kept.shape[1]
    even = lax.rem(lax.axis_index("gz"), 2) == 0

    def block(source, k):
        m, t = k // 3, k % 3
        same, other = [], []
        for b in range(4):
            lane = (6 * m + b + t) // 2 * 128
            piece = source[64 * b : 64 * (b + 1), lane : lane + 128]
            (same if (b + t) % 2 == k % 2 else other).append(piece)
        return (same[0] + same[1]) + pltpu.roll(other[0] + other[1], 64, 1)

    for j in range(14):
        pair = []
        for source in (grads_one, grads_two):
            value = block(source, 2 * j)
            if j < 13:
                value = jnp.where(low_half(value.shape), value, block(source, 2 * j + 1))
            pair.append(value * scale)
        width = 128 if j < 13 else 64
        keep = jnp.where(even, pair[0], pair[1])[:, :width]
        send = jnp.where(even, pair[1], pair[0])[:, :width]
        for g in range(count):
            kept[g, :, 128 * j : 128 * j + width] = keep[g * rows : (g + 1) * rows, :]
            sent[g, :, 128 * j : 128 * j + width] = send[g * rows : (g + 1) * rows, :].astype(B16)


def last_kernel(pre_grad, grad, band, out, steps, columns, held):
    value = pre_grad[...].astype(F32)
    for i, dy in enumerate((-1, 0, 1)):
        steps[i] = (pltpu.roll(value, dy % ROWS, 0) if dy else value).astype(B16)
    own_columns(steps, columns, -1)
    held[...] = jnp.dot(columns[...], band[...], preferred_element_type=F32)
    for h in range(4):
        for x in range(SX):
            row, lanes = 64 * h + 16 * x, slice(256 * h, 256 * (h + 1))
            out[x, :, lanes] = (held[row : row + 8, :] + grad[x, :, lanes].astype(F32)).astype(B16)


def swapped(far, near, axis):
    count = lax.axis_size(axis)
    steps = [1 if i % 2 else -1 for i in range(count)]
    return (
        lax.ppermute(far, axis, [(i, (i + step) % count) for i, step in enumerate(steps)]),
        lax.ppermute(near, axis, [(i, i - step) for i, step in enumerate(steps)]),
    )


def total_kernel(parts, out):
    value = parts[0].astype(F32)
    for i in range(1, parts.shape[0]):
        value += parts[i].astype(F32)
    value = value.astype(out.dtype)
    if out.ndim == value.ndim:
        out[...] = value
    else:
        for i in range(out.shape[0]):
            out[i] = value


def pair_kernel(kept, came, stay, leave):
    odd = lax.rem(lax.axis_index("gx"), 2) == 1
    for i in range(stay.shape[0]):
        first, second = (kept[2 * i + j] + came[2 * i + j].astype(F32) for j in range(2))
        stay[i] = jnp.where(odd, second, first)
        leave[i] = jnp.where(odd, first, second).astype(B16)


def add_kernel(kept, came, out):
    out[...] = (kept[...] + came[...].astype(F32)).astype(B16)


def last_total_kernel(parts, one, two):
    first, second = parts[0], parts[1]
    for i in range(2, parts.shape[0], 2):
        first += parts[i]
        second += parts[i + 1]
    one[...] = first
    two[...] = second


def reduced(kept, sent, other):
    rows, columns = kept.shape[1:]
    gy, gz = lax.axis_size("gy"), lax.axis_size("gz")
    came = lax.ppermute(sent, "gz", [(i, i + 1 - 2 * (i % 2)) for i in range(gz)])
    came, other = lax.optimization_barrier((came, other))
    count = kept.shape[0]
    half = (count // 2, rows, columns)
    stay, leave = call(pair_kernel, [(half, F32), (half, B16)], [], 1000, 500000, kept, came)
    came = lax.ppermute(leave, "gx", [(i, i + 1 - 2 * (i % 2)) for i in range(count)])
    (slots,) = call(add_kernel, [(half, B16)], [], 1000, 500000, stay, came)
    groups = [list(range(0, count, 2)), list(range(1, count, 2))]
    parts = lax.all_to_all(slots, "gx", 0, 0, axis_index_groups=groups, tiled=True)
    (copies,) = call(total_kernel, [((gy, rows, columns), B16)], [], 1000, 500000, parts)
    parts = lax.all_to_all(copies, "gy", 0, 0, tiled=True)
    (part,) = call(total_kernel, [((rows, columns), F32)], [], 1000, 500000, parts)
    parts = lax.all_gather(part, "gz", axis=0)
    grads = ((rows, columns), F32)
    one, two = call(last_total_kernel, [grads, grads], [], 1000, 500000, parts)
    return other, one, two


def body(block_input, pre_act, skip_grad, pool_grad, conv1_weight, conv2_weight):
    count = lax.axis_size("gx")
    rows = CH // count
    cells = SX * SY * SZ * count * lax.axis_size("gy") * lax.axis_size("gz")
    block, message = ((SX, SY, LANES), B16), ((4, SY, LANES), B16)
    weight = ((rows, 27 * CH), B16)
    grad, pre, inp, far, near, copies = call(
        prep_kernel,
        [block, block, block, message, message, ((count, 2 * rows, 27 * CH), B16)],
        [
            block, ((SX // 2, SY // 2, LANES // 2), B16), weight, weight,
            ((SX // 2, SY, LANES), F32), ((2 * rows, 27 * CH), F32), pltpu.SemaphoreType.DMA((6,)),
        ],
        100000, 400000,
        *(
            pltpu.with_memory_space_constraint(array, pltpu.HBM)
            for array in (skip_grad, pool_grad, pre_act, block_input, conv1_weight, conv2_weight)
        ),
        space=pltpu.HBM,
    )
    xfar, xnear = swapped(far, near, "gx")
    fields = (grad, pre, inp, xfar, xnear)
    message = ((LAYERS, 2, LANES), B16)
    yfar, ynear = swapped(
        *call(ypack_kernel, [message, message], [((4, LANES), F32)], 60000000000, 600000, *fields), "gy"
    )
    side = ((12 * LAYERS, 128), F32)
    gathered = lax.all_to_all(copies, "gx", 0, 0, tiled=True)
    message = ((12 * LAYERS, 128), B16)
    zfar, znear = swapped(
        *call(zpack_kernel, [message, message], [side, side], 100000, 700000, *fields, yfar, ynear), "gz"
    )
    matrix = ((DEPTH, 256), B16)
    flat = ((CH, 36 * CH), F32)
    band_one, band_two = call(bands_kernel, [matrix, matrix], [flat, flat], 1000000, 4000000, gathered)
    field = ((ROWS, WIDE), F32)
    steps = ((3, ROWS, WIDE), B16)
    columns = ((256, DEPTH), B16)
    kept, sent, pre_grad = call(
        functools.partial(main_kernel, 1.0 / math.sqrt(cells)),
        [((count, rows, 27 * CH), F32), ((count, rows, 27 * CH), B16), ((ROWS, WIDE), B16)],
        [
            field, field, field, steps, columns,
            ((5 * HALO_ROWS, DEPTH), B16), ((256, 256), B16), ((256, 256), F32),
            ((256, DEPTH), F32), ((256, DEPTH), F32), ((5 * HALO_ROWS, 256), F32), side, side,
        ],
        2 * 900 * 1000 * 1000, 8000000,
        *fields, yfar, ynear, zfar, znear, band_two,
        grant=32,
    )
    (input_grad,) = call(
        last_kernel,
        [((SX, SY, LANES), B16)],
        [steps, columns, ((256, 256), F32)],
        500000000, 4000000,
        pre_grad, grad, band_one,
    )
    return reduced(kept, sent, input_grad)


def solution(mesh):
    in_specs = (
        P("gx", "gy", "gz"),
        P("gx", "gy", "gz"),
        P("gx", "gy", "gz"),
        P("gx", "gy", "gz"),
        P("gx", None),
        P("gx", None),
    )
    out_specs = (P("gx", "gy", "gz"), P("gx", None), P("gx", None))
    return jax.shard_map(body, mesh=mesh, in_specs=in_specs, out_specs=out_specs, check_vma=False)
```

```python
import functools
import math

import jax
import jax.numpy as jnp
from jax import lax
from jax.experimental import pallas as pl
from jax.experimental.pallas import tpu as pltpu
from jax.sharding import PartitionSpec as P

F32, B16 = jnp.float32, jnp.bfloat16
SX, SY, SZ, CH = 4, 8, 16, 64
LANES = SZ * CH
ROWS = 16 * (SX + 5)
WIDE = LANES + 6 * CH
BAND = 4 * CH
OWN_GROUPS, HALO_GROUPS = SZ // 2, SZ // 2 + 2
DEPTH = 9 * BAND
OWN_ROWS = 8 * SX
HALO_ROWS = 8 * (SX + 2)
EDGES = HALO_GROUPS * HALO_ROWS
MANY = EDGES + HALO_GROUPS * 16
LAYERS = 14


def call(kernel, outs, scratch, flops, moved, *args, space=pltpu.VMEM, grant=12):
    return pl.pallas_call(
        kernel,
        out_shape=[jax.ShapeDtypeStruct(shape, dtype) for shape, dtype in outs],
        in_specs=[pl.BlockSpec(memory_space=space)] * len(args),
        out_specs=[pl.BlockSpec(memory_space=pltpu.VMEM)] * len(outs),
        scratch_shapes=[pltpu.VMEM(*held) if isinstance(held, tuple) else held for held in scratch],
        compiler_params=pltpu.CompilerParams(vmem_limit_bytes=grant * 1024 * 1024),
        cost_estimate=pl.CostEstimate(flops=flops, bytes_accessed=moved, transcendentals=0),
    )(*args)


def low_half(shape):
    return lax.broadcasted_iota(jnp.int32, shape, len(shape) - 1) % 128 < 64


class Either:
    def __init__(self, axis, if_odd, if_even):
        self.odd = lax.rem(lax.axis_index(axis), 2) == 1
        self.refs = if_odd, if_even

    def __getitem__(self, at):
        first, second = (ref[at].astype(F32) for ref in self.refs)
        return jnp.where(self.odd, first, second)


def below_above(axis, far, near):
    return Either(axis, near, far), Either(axis, far, near)


def far_near(axis, low, high):
    odd = lax.rem(lax.axis_index(axis), 2) == 1
    return jnp.where(odd, high, low).astype(B16), jnp.where(odd, low, high).astype(B16)


def prep_kernel(skip_in, pool_in, pre_in, inp_in, one_in, two_in,
                grad, pre, inp, far, near, copies, skip, pool, one, two, up, rows, sems):
    moves = [
        pltpu.make_async_copy(source, target, sems.at[i])
        for i, (source, target) in enumerate(
            ((skip_in, skip), (pool_in, pool), (pre_in, pre), (inp_in, inp), (one_in, one), (two_in, two))
        )
    ]
    for move in moves:
        move.start()
    for move in moves:
        move.wait()
    each = one.shape[0]
    rows[0:each], rows[each : 2 * each] = one[...].astype(F32), two[...].astype(F32)
    both = rows[...].astype(B16)
    for g in range(copies.shape[0]):
        copies[g] = both
    for px in range(SX // 2):
        pieces = []
        for j in range(LANES // 256):
            v = pool[px, :, 128 * j : 128 * (j + 1)].astype(F32)
            turned = pltpu.roll(v, 64, 1)
            first = low_half(v.shape)
            pieces += [jnp.where(first, v, turned), jnp.where(first, turned, v)]
        for y in range(SY):
            for j, piece in enumerate(pieces):
                up[px, y : y + 1, 128 * j : 128 * (j + 1)] = piece[y // 2 : y // 2 + 1, :]
    for x in range(SX):
        value = (skip[x].astype(F32) + 0.125 * up[x // 2]).astype(B16)
        grad[x] = value
    ends = ((grad, 0, 2), (grad, 1, 3), (pre, 0, SX - 1), (inp, 0, SX - 1))
    for at, (ref, bottom, top) in enumerate(ends):
        far[at], near[at] = far_near("gx", ref[bottom].astype(F32), ref[top].astype(F32))


def fields_of(grad, pre, inp, xlo, xhi):
    def own(ref):
        return [(ref, x) for x in range(SX)]

    return (
        [(xlo, 0), (xlo, 1)] + own(grad) + [(xhi, 0), (xhi, 1)],
        [(xlo, 2)] + own(pre) + [(xhi, 2)],
        [(xlo, 3)] + own(inp) + [(xhi, 3)],
    )


def ypack_kernel(grad, pre, inp, xfar, xnear, far, near, held):
    wide, acts, inputs = fields_of(grad, pre, inp, *below_above("gx", xfar, xnear))
    for at, (ref, x) in enumerate(wide):
        value = ref[x].astype(F32)
        far[at], near[at] = far_near("gy", value[0:2], value[SY - 2 : SY])
    for at, ((a, ax), (i, ix)) in enumerate(zip(acts, inputs)):
        v, w = a[ax].astype(F32), i[ix].astype(F32)
        held[0:1], held[1:2] = v[0:1], w[0:1]
        held[2:3], held[3:4] = v[SY - 1 :], w[SY - 1 :]
        far[8 + at], near[8 + at] = far_near("gy", held[0:2], held[2:4])


def zpack_kernel(grad, pre, inp, xfar, xnear, yfar, ynear, far, near, low, high):
    wide, acts, inputs = fields_of(grad, pre, inp, *below_above("gx", xfar, xnear))
    ylo, yhi = below_above("gy", yfar, ynear)
    for held, lane, half in ((low, 0, True), (high, LANES - 128, False)):
        held[...] = jnp.zeros_like(held)
        cut = slice(lane, lane + 128)
        for at, (ref, x) in enumerate(wide):
            row = 12 * at
            held[row : row + 2] = ylo[at, :, cut].astype(F32)
            held[row + 2 : row + 10] = ref[x, :, cut].astype(F32)
            held[row + 10 : row + 12] = yhi[at, :, cut].astype(F32)
        for j, ((a, ax), (i, ix)) in enumerate(zip(acts, inputs)):
            row = 12 * (8 + j)
            below, above = ylo[8 + j, :, cut].astype(F32), yhi[8 + j, :, cut].astype(F32)
            v, w = a[ax, :, cut].astype(F32), i[ix, :, cut].astype(F32)

            def joined(first, second):
                if half:
                    second = pltpu.roll(second, 64, 1)
                else:
                    first = pltpu.roll(first, 64, 1)
                return jnp.where(low_half(first.shape), first, second)

            held[row + 2 : row + 10] = joined(v, w)
            for at, pair in ((row + 1, below), (row + 10, above)):
                first, second = jnp.broadcast_to(pair[0:1], (8, 128)), jnp.broadcast_to(pair[1:2], (8, 128))
                held[at : at + 1] = joined(first, second)[0:1]
    far[...], near[...] = far_near("gz", low[...], high[...])


def bands_kernel(weights, one, two, flat, turned):
    count, rows = weights.shape[0], weights.shape[1] // 2
    block = lax.broadcasted_iota(jnp.int32, (CH, 128), 1) // CH
    for which, out in enumerate((one, two)):
        flat[...] = jnp.zeros_like(flat)
        for g in range(count):
            value = weights[g].astype(F32)[which * rows : (which + 1) * rows]
            flat[g * rows : (g + 1) * rows, 256 : 256 + 27 * CH] = value
        turned[...] = pltpu.roll(flat[...], flat.shape[1] - 64, 1)
        for m in range(9):
            for a in range(4):
                at = 4 + 3 * m + 2 - a
                source = turned if at % 2 else flat
                lane = at // 2 * 128
                valid = (block + 2 - a >= 0) & (block - a <= 0)
                value = jnp.where(valid, source[:, lane : lane + 128], 0.0)
                out[m * BAND + a * CH : m * BAND + (a + 1) * CH, :] = value.astype(B16)


def fill_wide(field, layers, ylo, yhi, zlo, zhi):
    field[...] = jnp.zeros_like(field)
    for at, (ref, x) in enumerate(layers):
        row = 16 * (at + 1)
        field[row : row + 8, 128 : 128 + LANES] = ref[x].astype(F32)
        field[row - 2 : row, 128 : 128 + LANES] = ylo[at].astype(F32)
        field[row + 8 : row + 10, 128 : 128 + LANES] = yhi[at].astype(F32)
        for side, lane in ((zlo, 0), (zhi, 128 + LANES)):
            field[row - 2 : row + 10, lane : lane + 128] = side[12 * at : 12 * at + 12]


def fill_thin(field, layers, second, ylo, yhi, zlo, zhi):
    field[...] = jnp.zeros_like(field)
    for j, (ref, x) in enumerate(layers):
        at, row = 8 + j, 16 * (j + 2)
        field[row : row + 8, 128 : 128 + LANES] = ref[x].astype(F32)
        field[row - 1 : row, 128 : 128 + LANES] = ylo[at].astype(F32)[second : second + 1]
        field[row + 8 : row + 9, 128 : 128 + LANES] = yhi[at].astype(F32)[second : second + 1]
        for side, lane, upper in ((zlo, 0, True), (zhi, 128 + LANES, False)):
            value = side[12 * at : 12 * at + 12]
            if upper != bool(second):
                value = pltpu.roll(value, 64, 1)
            value = jnp.where(low_half(value.shape) != upper, value, 0.0)
            field[row - 1 : row, lane : lane + 128] = value[1:2]
            field[row : row + 8, lane : lane + 128] = value[2:10]
            field[row + 8 : row + 9, lane : lane + 128] = value[10:11]


def spread(moved, evens, odds, sign, layers):
    for i, dy in enumerate((-1, 0, 1)):
        by = (-sign * dy) % ROWS
        value = pltpu.roll(moved, by, 0) if by else moved
        tiles = [value[16 * (x + 1) : 16 * (x + 1) + 8] for x in layers]
        evens[i, 0 : 8 * len(tiles)] = jnp.concatenate(tiles, 0).astype(B16)
        odds[i, 0 : 8 * len(tiles) - 16] = jnp.concatenate(tiles[1:-1], 0).astype(B16)


def stepped(evens, odds, dy, dx, rows, lane):
    ref, row = (odds, 0) if dx == 0 else (evens, 8 + 8 * dx)
    return ref[dy, row : row + rows, lane : lane + BAND]


def own_columns(evens, odds, columns, sign):
    for m in range(9):
        for h in range(OWN_GROUPS):
            columns[OWN_ROWS * h : OWN_ROWS * (h + 1), BAND * m : BAND * (m + 1)] = stepped(
                evens, odds, m % 3, sign * (m // 3 - 1), OWN_ROWS, 128 * h + 128
            )


def edge_rows(count):
    row = lax.broadcasted_iota(jnp.int32, (16 * count, ROWS), 0)
    column = lax.broadcasted_iota(jnp.int32, (16 * count, ROWS), 1)
    m, x = row // 16 + (4 if count == 1 else 0), row % 8
    source = 16 * (x - m // 3 + 2) + jnp.where(row % 16 < 8, -1, 8) - m % 3 + 1
    return jnp.where(column == source, 1.0, 0.0).astype(B16)


def slope(v):
    g = jax.nn.sigmoid(v)
    return g * (1.0 + v * (1.0 - g))


def main_kernel(scale, grad, pre, inp, xfar, xnear, yfar, ynear, zfar, znear, band,
                kept, sent, pre_out, fg, fa, fi, moved, picked, evens, odds, columns, many, left, left_f, grads_one, grads_two, held, zlo, zhi):
    wide, acts, inputs = fields_of(grad, pre, inp, *below_above("gx", xfar, xnear))
    ylo, yhi = below_above("gy", yfar, ynear)
    below, above = below_above("gz", zfar, znear)
    zlo[...] = below[...]
    zhi[...] = above[...]
    halos = (ylo, yhi, zlo, zhi)
    fill_wide(fg, wide, *halos)
    fill_thin(fa, acts, 0, *halos)
    fill_thin(fi, inputs, 1, *halos)
    contract = (((0,), (0,)), ((), ()))

    v = fa[...]
    act = (v * jax.nn.sigmoid(v)).astype(B16).astype(F32)
    spread(pltpu.roll(act, 64, 1), evens, odds, 1, range(1, SX + 3))
    own_columns(evens, odds, columns, 1)
    for h in range(OWN_GROUPS):
        for x in range(SX):
            row = OWN_ROWS * h + 8 * x
            left_f[row : row + 8, :] = grad[x, :, 128 * h : 128 * (h + 1)].astype(F32)
    left[...] = left_f[...].astype(B16)
    grads_two[...] = lax.dot_general(left[...], columns[...], contract, preferred_element_type=F32)

    moved[...] = pltpu.roll(fg[...], 64, 1)
    spread(moved[...], evens, odds, -1, range(SX + 4))
    for m in range(9):
        dx, dy = m // 3 - 1, m % 3
        for h in range(HALO_GROUPS):
            many[HALO_ROWS * h : HALO_ROWS * (h + 1), BAND * m : BAND * (m + 1)] = stepped(
                evens, odds, dy, -dx, HALO_ROWS, 128 * h
            )
    picked[...] = jnp.dot(edge_rows(9), moved[...].astype(B16), preferred_element_type=F32).astype(B16)
    for m in range(9):
        for h in range(HALO_GROUPS):
            row = EDGES + 16 * h
            many[row : row + 16, BAND * m : BAND * (m + 1)] = picked[
                16 * m : 16 * (m + 1), 128 * h : 128 * h + BAND
            ]
    held[...] = jnp.dot(many[...], band[...], preferred_element_type=F32)
    fg[:, 128 * HALO_GROUPS :] = jnp.zeros((ROWS, WIDE - 128 * HALO_GROUPS), F32)
    place = edge_rows(1)
    beside = slope(jnp.dot(place, fa[:, : 128 * HALO_GROUPS].astype(B16), preferred_element_type=F32))
    for h in range(HALO_GROUPS):
        lanes = slice(128 * h, 128 * (h + 1))
        value = (held[EDGES + 16 * h : EDGES + 16 * (h + 1), :] * beside[:, lanes]).astype(B16)
        fg[:, lanes] = lax.dot_general(place, value, contract, preferred_element_type=F32)
        for x in range(1, SX + 3):
            row, at = HALO_ROWS * h + 8 * (x - 1), slice(16 * (x + 1), 16 * (x + 1) + 8)
            value = held[row : row + 8, :] * slope(fa[at, lanes])
            fg[at, lanes] = value.astype(B16).astype(F32)
    pre_out[...] = pltpu.roll(fg[...], 64, 1).astype(B16)

    spread(pltpu.roll(fi[...], 64, 1), evens, odds, 1, range(1, SX + 3))
    own_columns(evens, odds, columns, 1)
    for h in range(OWN_GROUPS):
        for x in range(SX):
            row, at = OWN_ROWS * h + 8 * x, 16 * (x + 3)
            left_f[row : row + 8, :] = fg[at : at + 8, 128 * h + 128 : 128 * h + 256]
    left[...] = left_f[...].astype(B16)
    grads_one[...] = lax.dot_general(left[...], columns[...], contract, preferred_element_type=F32)

    count, rows = kept.shape[0], kept.shape[1]
    even = lax.rem(lax.axis_index("gz"), 2) == 0

    def block(source, k):
        m, t = k // 3, k % 3
        pieces = []
        for b in ((k + t) % 2, (k + t + 1) % 2):
            lane = (4 * m + b + t) // 2 * 128
            pieces.append(source[64 * b : 64 * (b + 1), lane : lane + 128])
        return pieces[0] + pltpu.roll(pieces[1], 64, 1)

    for j in range(14):
        pair = []
        for source in (grads_one, grads_two):
            value = block(source, 2 * j)
            if j < 13:
                value = jnp.where(low_half(value.shape), value, block(source, 2 * j + 1))
            pair.append(value * scale)
        width = 128 if j < 13 else 64
        keep = jnp.where(even, pair[0], pair[1])[:, :width]
        send = jnp.where(even, pair[1], pair[0])[:, :width]
        for g in range(count):
            kept[g, :, 128 * j : 128 * j + width] = keep[g * rows : (g + 1) * rows, :]
            sent[g, :, 128 * j : 128 * j + width] = send[g * rows : (g + 1) * rows, :].astype(B16)


def last_kernel(pre_grad, grad, band, out, evens, odds, columns, held):
    spread(pre_grad[...].astype(F32), evens, odds, -1, range(1, SX + 3))
    own_columns(evens, odds, columns, -1)
    held[...] = jnp.dot(columns[...], band[...], preferred_element_type=F32)
    for h in range(OWN_GROUPS):
        for x in range(SX):
            row, lanes = OWN_ROWS * h + 8 * x, slice(128 * h, 128 * (h + 1))
            out[x, :, lanes] = (held[row : row + 8, :] + grad[x, :, lanes].astype(F32)).astype(B16)


def swapped(far, near, axis):
    count = lax.axis_size(axis)
    steps = [1 if i % 2 else -1 for i in range(count)]
    return (
        lax.ppermute(far, axis, [(i, (i + step) % count) for i, step in enumerate(steps)]),
        lax.ppermute(near, axis, [(i, i - step) for i, step in enumerate(steps)]),
    )


def total_kernel(parts, out):
    value = parts[0].astype(F32)
    for i in range(1, parts.shape[0]):
        value += parts[i].astype(F32)
    value = value.astype(out.dtype)
    if out.ndim == value.ndim:
        out[...] = value
    else:
        for i in range(out.shape[0]):
            out[i] = value


def pair_kernel(kept, came, out):
    out[...] = (kept[...] + came[...].astype(F32)).astype(B16)


def last_total_kernel(parts, one, two):
    first, second = parts[0], parts[1]
    for i in range(2, parts.shape[0], 2):
        first += parts[i]
        second += parts[i + 1]
    one[...] = first
    two[...] = second


def reduced(kept, sent, other):
    rows, columns = kept.shape[1:]
    gy, gz = lax.axis_size("gy"), lax.axis_size("gz")
    came = lax.ppermute(sent, "gz", [(i, i + 1 - 2 * (i % 2)) for i in range(gz)])
    came, other = lax.optimization_barrier((came, other))
    (slots,) = call(pair_kernel, [(kept.shape, B16)], [], 1000, 500000, kept, came)
    parts = lax.all_to_all(slots, "gx", 0, 0, tiled=True)
    (copies,) = call(total_kernel, [((gy, rows, columns), B16)], [], 1000, 500000, parts)
    parts = lax.all_to_all(copies, "gy", 0, 0, tiled=True)
    (part,) = call(total_kernel, [((rows, columns), F32)], [], 1000, 500000, parts)
    parts = lax.all_gather(part, "gz", axis=0)
    grads = ((rows, columns), F32)
    one, two = call(last_total_kernel, [grads, grads], [], 1000, 500000, parts)
    return other, one, two


def body(block_input, pre_act, skip_grad, pool_grad, conv1_weight, conv2_weight):
    count = lax.axis_size("gx")
    rows = CH // count
    cells = SX * SY * SZ * count * lax.axis_size("gy") * lax.axis_size("gz")
    block, message = ((SX, SY, LANES), B16), ((4, SY, LANES), B16)
    weight = ((rows, 27 * CH), B16)
    grad, pre, inp, far, near, copies = call(
        prep_kernel,
        [block, block, block, message, message, ((count, 2 * rows, 27 * CH), B16)],
        [
            block, ((SX // 2, SY // 2, LANES // 2), B16), weight, weight,
            ((SX // 2, SY, LANES), F32), ((2 * rows, 27 * CH), F32), pltpu.SemaphoreType.DMA((6,)),
        ],
        100000, 400000,
        *(
            pltpu.with_memory_space_constraint(array, pltpu.HBM)
            for array in (skip_grad, pool_grad, pre_act, block_input, conv1_weight, conv2_weight)
        ),
        space=pltpu.HBM,
    )
    xfar, xnear = swapped(far, near, "gx")
    fields = (grad, pre, inp, xfar, xnear)
    message = ((LAYERS, 2, LANES), B16)
    yfar, ynear = swapped(
        *call(ypack_kernel, [message, message], [((4, LANES), F32)], 60000000000, 600000, *fields), "gy"
    )
    side = ((12 * LAYERS, 128), F32)
    gathered = lax.all_to_all(copies, "gx", 0, 0, tiled=True)
    message = ((12 * LAYERS, 128), B16)
    zfar, znear = swapped(
        *call(zpack_kernel, [message, message], [side, side], 100000, 700000, *fields, yfar, ynear), "gz"
    )
    matrix = ((DEPTH, 128), B16)
    flat = ((CH, 36 * CH), F32)
    band_one, band_two = call(bands_kernel, [matrix, matrix], [flat, flat], 1000000, 4000000, gathered)
    field = ((ROWS, WIDE), F32)
    evens, odds = ((3, 8 * (SX + 4), WIDE), B16), ((3, 8 * (SX + 2), WIDE), B16)
    columns = ((OWN_GROUPS * OWN_ROWS, DEPTH), B16)
    kept, sent, pre_grad = call(
        functools.partial(main_kernel, 1.0 / math.sqrt(cells)),
        [((count, rows, 27 * CH), F32), ((count, rows, 27 * CH), B16), ((ROWS, WIDE), B16)],
        [
            field, field, field, field, ((ROWS, WIDE), B16), evens, odds, columns,
            ((MANY, DEPTH), B16), ((OWN_GROUPS * OWN_ROWS, 128), B16), ((OWN_GROUPS * OWN_ROWS, 128), F32),
            ((128, DEPTH), F32), ((128, DEPTH), F32), ((MANY, 128), F32), side, side,
        ],
        2 * 900 * 1000 * 1000, 8000000,
        *fields, yfar, ynear, zfar, znear, band_two,
        grant=32,
    )
    (input_grad,) = call(
        last_kernel,
        [((SX, SY, LANES), B16)],
        [evens, odds, columns, ((OWN_GROUPS * OWN_ROWS, 128), F32)],
        500000000, 4000000,
        pre_grad, grad, band_one,
    )
    return reduced(kept, sent, input_grad)


def solution(mesh):
    in_specs = (
        P("gx", "gy", "gz"),
        P("gx", "gy", "gz"),
        P("gx", "gy", "gz"),
        P("gx", "gy", "gz"),
        P("gx", None),
        P("gx", None),
    )
    out_specs = (P("gx", "gy", "gz"), P("gx", None), P("gx", None))
    return jax.shard_map(body, mesh=mesh, in_specs=in_specs, out_specs=out_specs, check_vma=False)
```

```python
import functools
import math

import jax
import jax.numpy as jnp
from jax import lax
from jax.experimental import pallas as pl
from jax.experimental.pallas import tpu as pltpu
from jax.sharding import PartitionSpec as P

F32, B16 = jnp.float32, jnp.bfloat16
SX, SY, SZ, CH = 4, 8, 16, 64
LANES = SZ * CH
ROWS = 16 * (SX + 5)
WIDE = LANES + 6 * CH
BAND = 4 * CH
OWN_GROUPS, HALO_GROUPS = SZ // 2, SZ // 2 + 2
DEPTH = 9 * BAND
OWN_ROWS = 8 * SX
HALO_ROWS = 8 * (SX + 2)
EDGES = HALO_GROUPS * HALO_ROWS
MANY = EDGES + HALO_GROUPS * 16
LAYERS = 14


def call(kernel, outs, scratch, flops, moved, *args, space=pltpu.VMEM, grant=12):
    return pl.pallas_call(
        kernel,
        out_shape=[jax.ShapeDtypeStruct(shape, dtype) for shape, dtype in outs],
        in_specs=[pl.BlockSpec(memory_space=space)] * len(args),
        out_specs=[pl.BlockSpec(memory_space=pltpu.VMEM)] * len(outs),
        scratch_shapes=[pltpu.VMEM(*held) if isinstance(held, tuple) else held for held in scratch],
        compiler_params=pltpu.CompilerParams(vmem_limit_bytes=grant * 1024 * 1024),
        cost_estimate=pl.CostEstimate(flops=flops, bytes_accessed=moved, transcendentals=0),
    )(*args)


def low_half(shape):
    return lax.broadcasted_iota(jnp.int32, shape, len(shape) - 1) % 128 < 64


class Either:
    def __init__(self, axis, if_odd, if_even):
        self.odd = lax.rem(lax.axis_index(axis), 2) == 1
        self.refs = if_odd, if_even

    def __getitem__(self, at):
        first, second = (ref[at].astype(F32) for ref in self.refs)
        return jnp.where(self.odd, first, second)


def below_above(axis, far, near):
    return Either(axis, near, far), Either(axis, far, near)


def far_near(axis, low, high):
    odd = lax.rem(lax.axis_index(axis), 2) == 1
    return jnp.where(odd, high, low).astype(B16), jnp.where(odd, low, high).astype(B16)


def prep_kernel(skip_in, pool_in, pre_in, inp_in, one_in, two_in,
                grad, pre, inp, far, near, copies, skip, pool, one, two, up, rows, sems):
    moves = [
        pltpu.make_async_copy(source, target, sems.at[i])
        for i, (source, target) in enumerate(
            ((skip_in, skip), (pool_in, pool), (pre_in, pre), (inp_in, inp), (one_in, one), (two_in, two))
        )
    ]
    for move in moves:
        move.start()
    for move in moves:
        move.wait()
    each = one.shape[0]
    rows[0:each], rows[each : 2 * each] = one[...].astype(F32), two[...].astype(F32)
    both = rows[...].astype(B16)
    for g in range(copies.shape[0]):
        copies[g] = both
    for px in range(SX // 2):
        pieces = []
        for j in range(LANES // 256):
            v = pool[px, :, 128 * j : 128 * (j + 1)].astype(F32)
            turned = pltpu.roll(v, 64, 1)
            first = low_half(v.shape)
            pieces += [jnp.where(first, v, turned), jnp.where(first, turned, v)]
        for y in range(SY):
            for j, piece in enumerate(pieces):
                up[px, y : y + 1, 128 * j : 128 * (j + 1)] = piece[y // 2 : y // 2 + 1, :]
    for x in range(SX):
        value = (skip[x].astype(F32) + 0.125 * up[x // 2]).astype(B16)
        grad[x] = value
    ends = ((grad, 0, 2), (grad, 1, 3), (pre, 0, SX - 1), (inp, 0, SX - 1))
    for at, (ref, bottom, top) in enumerate(ends):
        far[at], near[at] = far_near("gx", ref[bottom].astype(F32), ref[top].astype(F32))


def fields_of(grad, pre, inp, xlo, xhi):
    def own(ref):
        return [(ref, x) for x in range(SX)]

    return (
        [(xlo, 0), (xlo, 1)] + own(grad) + [(xhi, 0), (xhi, 1)],
        [(xlo, 2)] + own(pre) + [(xhi, 2)],
        [(xlo, 3)] + own(inp) + [(xhi, 3)],
    )


def ypack_kernel(grad, pre, inp, xfar, xnear, far, near, held):
    wide, acts, inputs = fields_of(grad, pre, inp, *below_above("gx", xfar, xnear))
    for at, (ref, x) in enumerate(wide):
        value = ref[x].astype(F32)
        far[at], near[at] = far_near("gy", value[0:2], value[SY - 2 : SY])
    for at, ((a, ax), (i, ix)) in enumerate(zip(acts, inputs)):
        v, w = a[ax].astype(F32), i[ix].astype(F32)
        held[0:1], held[1:2] = v[0:1], w[0:1]
        held[2:3], held[3:4] = v[SY - 1 :], w[SY - 1 :]
        far[8 + at], near[8 + at] = far_near("gy", held[0:2], held[2:4])


def zpack_kernel(grad, pre, inp, xfar, xnear, yfar, ynear, far, near, low, high):
    wide, acts, inputs = fields_of(grad, pre, inp, *below_above("gx", xfar, xnear))
    ylo, yhi = below_above("gy", yfar, ynear)
    for held, lane, half in ((low, 0, True), (high, LANES - 128, False)):
        held[...] = jnp.zeros_like(held)
        cut = slice(lane, lane + 128)
        for at, (ref, x) in enumerate(wide):
            row = 12 * at
            held[row : row + 2] = ylo[at, :, cut].astype(F32)
            held[row + 2 : row + 10] = ref[x, :, cut].astype(F32)
            held[row + 10 : row + 12] = yhi[at, :, cut].astype(F32)
        for j, ((a, ax), (i, ix)) in enumerate(zip(acts, inputs)):
            row = 12 * (8 + j)
            below, above = ylo[8 + j, :, cut].astype(F32), yhi[8 + j, :, cut].astype(F32)
            v, w = a[ax, :, cut].astype(F32), i[ix, :, cut].astype(F32)

            def joined(first, second):
                if half:
                    second = pltpu.roll(second, 64, 1)
                else:
                    first = pltpu.roll(first, 64, 1)
                return jnp.where(low_half(first.shape), first, second)

            held[row + 2 : row + 10] = joined(v, w)
            for at, pair in ((row + 1, below), (row + 10, above)):
                first, second = jnp.broadcast_to(pair[0:1], (8, 128)), jnp.broadcast_to(pair[1:2], (8, 128))
                held[at : at + 1] = joined(first, second)[0:1]
    far[...], near[...] = far_near("gz", low[...], high[...])


def bands_kernel(weights, one, two, flat, turned):
    count, rows = weights.shape[0], weights.shape[1] // 2
    block = lax.broadcasted_iota(jnp.int32, (CH, 128), 1) // CH
    for which, out in enumerate((one, two)):
        flat[...] = jnp.zeros_like(flat)
        for g in range(count):
            value = weights[g].astype(F32)[which * rows : (which + 1) * rows]
            flat[g * rows : (g + 1) * rows, 256 : 256 + 27 * CH] = value
        turned[...] = pltpu.roll(flat[...], flat.shape[1] - 64, 1)
        for m in range(9):
            for a in range(4):
                at = 4 + 3 * m + 2 - a
                source = turned if at % 2 else flat
                lane = at // 2 * 128
                valid = (block + 2 - a >= 0) & (block - a <= 0)
                value = jnp.where(valid, source[:, lane : lane + 128], 0.0)
                out[m * BAND + a * CH : m * BAND + (a + 1) * CH, :] = value.astype(B16)


def fill_wide(field, layers, ylo, yhi, zlo, zhi):
    field[...] = jnp.zeros_like(field)
    for at, (ref, x) in enumerate(layers):
        row = 16 * (at + 1)
        field[row : row + 8, 128 : 128 + LANES] = ref[x].astype(F32)
        field[row - 2 : row, 128 : 128 + LANES] = ylo[at].astype(F32)
        field[row + 8 : row + 10, 128 : 128 + LANES] = yhi[at].astype(F32)
        for side, lane in ((zlo, 0), (zhi, 128 + LANES)):
            field[row - 2 : row + 10, lane : lane + 128] = side[12 * at : 12 * at + 12]


def fill_thin(field, layers, second, ylo, yhi, zlo, zhi):
    field[...] = jnp.zeros_like(field)
    for j, (ref, x) in enumerate(layers):
        at, row = 8 + j, 16 * (j + 2)
        field[row : row + 8, 128 : 128 + LANES] = ref[x].astype(F32)
        field[row - 1 : row, 128 : 128 + LANES] = ylo[at].astype(F32)[second : second + 1]
        field[row + 8 : row + 9, 128 : 128 + LANES] = yhi[at].astype(F32)[second : second + 1]
        for side, lane, upper in ((zlo, 0, True), (zhi, 128 + LANES, False)):
            value = side[12 * at : 12 * at + 12]
            if upper != bool(second):
                value = pltpu.roll(value, 64, 1)
            value = jnp.where(low_half(value.shape) != upper, value, 0.0)
            field[row - 1 : row, lane : lane + 128] = value[1:2]
            field[row : row + 8, lane : lane + 128] = value[2:10]
            field[row + 8 : row + 9, lane : lane + 128] = value[10:11]


def spread(moved, evens, odds, sign, layers):
    for i, dy in enumerate((-1, 0, 1)):
        by = (-sign * dy) % ROWS
        value = pltpu.roll(moved, by, 0) if by else moved
        tiles = [value[16 * (x + 1) : 16 * (x + 1) + 8] for x in layers]
        evens[i, 0 : 8 * len(tiles)] = jnp.concatenate(tiles, 0).astype(B16)
        odds[i, 0 : 8 * len(tiles) - 16] = jnp.concatenate(tiles[1:-1], 0).astype(B16)


def stepped(evens, odds, dy, dx, rows, lane):
    ref, row = (odds, 0) if dx == 0 else (evens, 8 + 8 * dx)
    return ref[dy, row : row + rows, lane : lane + BAND]


def own_columns(evens, odds, columns, sign):
    for m in range(9):
        for h in range(OWN_GROUPS):
            columns[OWN_ROWS * h : OWN_ROWS * (h + 1), BAND * m : BAND * (m + 1)] = stepped(
                evens, odds, m % 3, sign * (m // 3 - 1), OWN_ROWS, 128 * h + 128
            )


def edge_rows(count):
    row = lax.broadcasted_iota(jnp.int32, (16 * count, ROWS), 0)
    column = lax.broadcasted_iota(jnp.int32, (16 * count, ROWS), 1)
    m, x = row // 16 + (4 if count == 1 else 0), row % 8
    source = 16 * (x - m // 3 + 2) + jnp.where(row % 16 < 8, -1, 8) - m % 3 + 1
    return jnp.where(column == source, 1.0, 0.0).astype(B16)


def slope(v):
    g = jax.nn.sigmoid(v)
    return g * (1.0 + v * (1.0 - g))


def main_kernel(scale, grad, pre, inp, xfar, xnear, yfar, ynear, zfar, znear, band,
                kept, sent, pre_out, fg, fa, fi, moved, picked, evens, odds, columns, many, left, left_f, grads_one, grads_two, held, zlo, zhi):
    wide, acts, inputs = fields_of(grad, pre, inp, *below_above("gx", xfar, xnear))
    ylo, yhi = below_above("gy", yfar, ynear)
    below, above = below_above("gz", zfar, znear)
    zlo[...] = below[...]
    zhi[...] = above[...]
    halos = (ylo, yhi, zlo, zhi)
    fill_wide(fg, wide, *halos)
    fill_thin(fa, acts, 0, *halos)
    fill_thin(fi, inputs, 1, *halos)
    contract = (((0,), (0,)), ((), ()))

    v = fa[...]
    act = (v * jax.nn.sigmoid(v)).astype(B16).astype(F32)
    spread(pltpu.roll(act, 64, 1), evens, odds, 1, range(1, SX + 3))
    own_columns(evens, odds, columns, 1)
    for h in range(OWN_GROUPS):
        for x in range(SX):
            row = OWN_ROWS * h + 8 * x
            left_f[row : row + 8, :] = grad[x, :, 128 * h : 128 * (h + 1)].astype(F32)
    left[...] = left_f[...].astype(B16)
    grads_two[...] = lax.dot_general(left[...], columns[...], contract, preferred_element_type=F32)

    moved[...] = pltpu.roll(fg[...], 64, 1)
    spread(moved[...], evens, odds, -1, range(SX + 4))
    for m in range(9):
        dx, dy = m // 3 - 1, m % 3
        for h in range(HALO_GROUPS):
            many[HALO_ROWS * h : HALO_ROWS * (h + 1), BAND * m : BAND * (m + 1)] = stepped(
                evens, odds, dy, -dx, HALO_ROWS, 128 * h
            )
    picked[...] = jnp.dot(edge_rows(9), moved[...].astype(B16), preferred_element_type=F32).astype(B16)
    for m in range(9):
        for h in range(HALO_GROUPS):
            row = EDGES + 16 * h
            many[row : row + 16, BAND * m : BAND * (m + 1)] = picked[
                16 * m : 16 * (m + 1), 128 * h : 128 * h + BAND
            ]
    held[...] = jnp.dot(many[...], band[...], preferred_element_type=F32)
    fg[:, 128 * HALO_GROUPS :] = jnp.zeros((ROWS, WIDE - 128 * HALO_GROUPS), F32)
    place = edge_rows(1)
    beside = slope(jnp.dot(place, fa[:, : 128 * HALO_GROUPS].astype(B16), preferred_element_type=F32))
    for h in range(HALO_GROUPS):
        lanes = slice(128 * h, 128 * (h + 1))
        value = (held[EDGES + 16 * h : EDGES + 16 * (h + 1), :] * beside[:, lanes]).astype(B16)
        fg[:, lanes] = lax.dot_general(place, value, contract, preferred_element_type=F32)
        for x in range(1, SX + 3):
            row, at = HALO_ROWS * h + 8 * (x - 1), slice(16 * (x + 1), 16 * (x + 1) + 8)
            value = held[row : row + 8, :] * slope(fa[at, lanes])
            fg[at, lanes] = value.astype(B16).astype(F32)
    pre_out[...] = pltpu.roll(fg[...], 64, 1).astype(B16)

    spread(pltpu.roll(fi[...], 64, 1), evens, odds, 1, range(1, SX + 3))
    own_columns(evens, odds, columns, 1)
    for h in range(OWN_GROUPS):
        for x in range(SX):
            row, at = OWN_ROWS * h + 8 * x, 16 * (x + 3)
            left_f[row : row + 8, :] = fg[at : at + 8, 128 * h + 128 : 128 * h + 256]
    left[...] = left_f[...].astype(B16)
    grads_one[...] = lax.dot_general(left[...], columns[...], contract, preferred_element_type=F32)

    count, rows = kept.shape[0], kept.shape[1]
    even = lax.rem(lax.axis_index("gz"), 2) == 0

    def block(source, k):
        m, t = k // 3, k % 3
        pieces = []
        for b in ((k + t) % 2, (k + t + 1) % 2):
            lane = (4 * m + b + t) // 2 * 128
            pieces.append(source[64 * b : 64 * (b + 1), lane : lane + 128])
        return pieces[0] + pltpu.roll(pieces[1], 64, 1)

    for j in range(14):
        pair = []
        for source in (grads_one, grads_two):
            value = block(source, 2 * j)
            if j < 13:
                value = jnp.where(low_half(value.shape), value, block(source, 2 * j + 1))
            pair.append(value * scale)
        width = 128 if j < 13 else 64
        keep = jnp.where(even, pair[0], pair[1])[:, :width]
        send = jnp.where(even, pair[1], pair[0])[:, :width]
        for g in range(count):
            kept[g, :, 128 * j : 128 * j + width] = keep[g * rows : (g + 1) * rows, :]
            sent[g, :, 128 * j : 128 * j + width] = send[g * rows : (g + 1) * rows, :].astype(B16)


def last_kernel(pre_grad, grad, band, out, evens, odds, columns, held):
    spread(pre_grad[...].astype(F32), evens, odds, -1, range(1, SX + 3))
    own_columns(evens, odds, columns, -1)
    held[...] = jnp.dot(columns[...], band[...], preferred_element_type=F32)
    for h in range(OWN_GROUPS):
        for x in range(SX):
            row, lanes = OWN_ROWS * h + 8 * x, slice(128 * h, 128 * (h + 1))
            out[x, :, lanes] = (held[row : row + 8, :] + grad[x, :, lanes].astype(F32)).astype(B16)


def swapped(far, near, axis):
    count = lax.axis_size(axis)
    steps = [1 if i % 2 else -1 for i in range(count)]
    return (
        lax.ppermute(far, axis, [(i, (i + step) % count) for i, step in enumerate(steps)]),
        lax.ppermute(near, axis, [(i, i - step) for i, step in enumerate(steps)]),
    )


def total_kernel(parts, out):
    value = parts[0].astype(F32)
    for i in range(1, parts.shape[0]):
        value += parts[i].astype(F32)
    value = value.astype(out.dtype)
    if out.ndim == value.ndim:
        out[...] = value
    else:
        for i in range(out.shape[0]):
            out[i] = value


def pair_kernel(kept, came, out):
    out[...] = (kept[...] + came[...].astype(F32)).astype(B16)


def last_total_kernel(parts, one, two):
    first, second = parts[0], parts[1]
    for i in range(2, parts.shape[0], 2):
        first += parts[i]
        second += parts[i + 1]
    one[...] = first
    two[...] = second


def reduced(kept, sent, other):
    rows, columns = kept.shape[1:]
    gy, gz = lax.axis_size("gy"), lax.axis_size("gz")
    came = lax.ppermute(sent, "gz", [(i, i + 1 - 2 * (i % 2)) for i in range(gz)])
    (slots,) = call(pair_kernel, [(kept.shape, B16)], [], 1000, 500000, kept, came)
    parts = lax.all_to_all(slots, "gx", 0, 0, tiled=True)
    parts, other = lax.optimization_barrier((parts, other))
    (copies,) = call(total_kernel, [((gy, rows, columns), B16)], [], 1000, 500000, parts)
    parts = lax.all_to_all(copies, "gy", 0, 0, tiled=True)
    (part,) = call(total_kernel, [((rows, columns), F32)], [], 1000, 500000, parts)
    parts = lax.all_gather(part, "gz", axis=0)
    grads = ((rows, columns), F32)
    one, two = call(last_total_kernel, [grads, grads], [], 1000, 500000, parts)
    return other, one, two


def body(block_input, pre_act, skip_grad, pool_grad, conv1_weight, conv2_weight):
    count = lax.axis_size("gx")
    rows = CH // count
    cells = SX * SY * SZ * count * lax.axis_size("gy") * lax.axis_size("gz")
    block, message = ((SX, SY, LANES), B16), ((4, SY, LANES), B16)
    weight = ((rows, 27 * CH), B16)
    grad, pre, inp, far, near, copies = call(
        prep_kernel,
        [block, block, block, message, message, ((count, 2 * rows, 27 * CH), B16)],
        [
            block, ((SX // 2, SY // 2, LANES // 2), B16), weight, weight,
            ((SX // 2, SY, LANES), F32), ((2 * rows, 27 * CH), F32), pltpu.SemaphoreType.DMA((6,)),
        ],
        100000, 400000,
        *(
            pltpu.with_memory_space_constraint(array, pltpu.HBM)
            for array in (skip_grad, pool_grad, pre_act, block_input, conv1_weight, conv2_weight)
        ),
        space=pltpu.HBM,
    )
    xfar, xnear = swapped(far, near, "gx")
    fields = (grad, pre, inp, xfar, xnear)
    message = ((LAYERS, 2, LANES), B16)
    yfar, ynear = swapped(
        *call(ypack_kernel, [message, message], [((4, LANES), F32)], 60000000000, 600000, *fields), "gy"
    )
    side = ((12 * LAYERS, 128), F32)
    gathered = lax.all_to_all(copies, "gx", 0, 0, tiled=True)
    message = ((12 * LAYERS, 128), B16)
    zfar, znear = swapped(
        *call(zpack_kernel, [message, message], [side, side], 100000, 700000, *fields, yfar, ynear), "gz"
    )
    matrix = ((DEPTH, 128), B16)
    flat = ((CH, 36 * CH), F32)
    band_one, band_two = call(bands_kernel, [matrix, matrix], [flat, flat], 1000000, 4000000, gathered)
    field = ((ROWS, WIDE), F32)
    evens, odds = ((3, 8 * (SX + 4), WIDE), B16), ((3, 8 * (SX + 2), WIDE), B16)
    columns = ((OWN_GROUPS * OWN_ROWS, DEPTH), B16)
    kept, sent, pre_grad = call(
        functools.partial(main_kernel, 1.0 / math.sqrt(cells)),
        [((count, rows, 27 * CH), F32), ((count, rows, 27 * CH), B16), ((ROWS, WIDE), B16)],
        [
            field, field, field, field, ((ROWS, WIDE), B16), evens, odds, columns,
            ((MANY, DEPTH), B16), ((OWN_GROUPS * OWN_ROWS, 128), B16), ((OWN_GROUPS * OWN_ROWS, 128), F32),
            ((128, DEPTH), F32), ((128, DEPTH), F32), ((MANY, 128), F32), side, side,
        ],
        2 * 900 * 1000 * 1000, 8000000,
        *fields, yfar, ynear, zfar, znear, band_two,
        grant=32,
    )
    (input_grad,) = call(
        last_kernel,
        [((SX, SY, LANES), B16)],
        [evens, odds, columns, ((OWN_GROUPS * OWN_ROWS, 128), F32)],
        500000000, 4000000,
        pre_grad, grad, band_one,
    )
    return reduced(kept, sent, input_grad)


def solution(mesh):
    in_specs = (
        P("gx", "gy", "gz"),
        P("gx", "gy", "gz"),
        P("gx", "gy", "gz"),
        P("gx", "gy", "gz"),
        P("gx", None),
        P("gx", None),
    )
    out_specs = (P("gx", "gy", "gz"), P("gx", None), P("gx", None))
    return jax.shard_map(body, mesh=mesh, in_specs=in_specs, out_specs=out_specs, check_vma=False)
```

```python
import functools
import math

import jax
import jax.numpy as jnp
from jax import lax
from jax.experimental import pallas as pl
from jax.experimental.pallas import tpu as pltpu
from jax.sharding import PartitionSpec as P

F32, B16 = jnp.float32, jnp.bfloat16
SX, SY, SZ, CH = 4, 8, 16, 64
LANES = SZ * CH
ROWS = 16 * (SX + 5)
WIDE = LANES + 6 * CH
BAND = 4 * CH
OWN_GROUPS, HALO_GROUPS = SZ // 2, SZ // 2 + 2
DEPTH = 9 * BAND
OWN_ROWS = 8 * SX
HALO_ROWS = 8 * (SX + 2)
EDGES = HALO_GROUPS * HALO_ROWS
MANY = EDGES + HALO_GROUPS * 16
LAYERS = 14


def call(kernel, outs, scratch, flops, moved, *args, space=pltpu.VMEM, grant=12):
    return pl.pallas_call(
        kernel,
        out_shape=[jax.ShapeDtypeStruct(shape, dtype) for shape, dtype in outs],
        in_specs=[pl.BlockSpec(memory_space=space)] * len(args),
        out_specs=[pl.BlockSpec(memory_space=pltpu.VMEM)] * len(outs),
        scratch_shapes=[pltpu.VMEM(*held) if isinstance(held, tuple) else held for held in scratch],
        compiler_params=pltpu.CompilerParams(vmem_limit_bytes=grant * 1024 * 1024),
        cost_estimate=pl.CostEstimate(flops=flops, bytes_accessed=moved, transcendentals=0),
    )(*args)


def low_half(shape):
    return lax.broadcasted_iota(jnp.int32, shape, len(shape) - 1) % 128 < 64


class Either:
    def __init__(self, axis, if_odd, if_even):
        self.odd = lax.rem(lax.axis_index(axis), 2) == 1
        self.refs = if_odd, if_even

    def __getitem__(self, at):
        first, second = (ref[at].astype(F32) for ref in self.refs)
        return jnp.where(self.odd, first, second)


def below_above(axis, far, near):
    return Either(axis, near, far), Either(axis, far, near)


def far_near(axis, low, high):
    odd = lax.rem(lax.axis_index(axis), 2) == 1
    return jnp.where(odd, high, low).astype(B16), jnp.where(odd, low, high).astype(B16)


def prep_kernel(skip_in, pool_in, pre_in, inp_in, one_in, two_in,
                grad, pre, inp, far, near, copies, skip, pool, one, two, up, rows, sems):
    moves = [
        pltpu.make_async_copy(source, target, sems.at[i])
        for i, (source, target) in enumerate(
            ((skip_in, skip), (pool_in, pool), (pre_in, pre), (inp_in, inp), (one_in, one), (two_in, two))
        )
    ]
    for move in moves:
        move.start()
    for move in moves:
        move.wait()
    each = one.shape[0]
    rows[0:each], rows[each : 2 * each] = one[...].astype(F32), two[...].astype(F32)
    both = rows[...].astype(B16)
    for g in range(copies.shape[0]):
        copies[g] = both
    for px in range(SX // 2):
        pieces = []
        for j in range(LANES // 256):
            v = pool[px, :, 128 * j : 128 * (j + 1)].astype(F32)
            turned = pltpu.roll(v, 64, 1)
            first = low_half(v.shape)
            pieces += [jnp.where(first, v, turned), jnp.where(first, turned, v)]
        for y in range(SY):
            for j, piece in enumerate(pieces):
                up[px, y : y + 1, 128 * j : 128 * (j + 1)] = piece[y // 2 : y // 2 + 1, :]
    for x in range(SX):
        value = (skip[x].astype(F32) + 0.125 * up[x // 2]).astype(B16)
        grad[x] = value
    ends = ((grad, 0, 2), (grad, 1, 3), (pre, 0, SX - 1), (inp, 0, SX - 1))
    for at, (ref, bottom, top) in enumerate(ends):
        far[at], near[at] = far_near("gx", ref[bottom].astype(F32), ref[top].astype(F32))


def fields_of(grad, pre, inp, xlo, xhi):
    def own(ref):
        return [(ref, x) for x in range(SX)]

    return (
        [(xlo, 0), (xlo, 1)] + own(grad) + [(xhi, 0), (xhi, 1)],
        [(xlo, 2)] + own(pre) + [(xhi, 2)],
        [(xlo, 3)] + own(inp) + [(xhi, 3)],
    )


def ypack_kernel(grad, pre, inp, xfar, xnear, far, near, held):
    wide, acts, inputs = fields_of(grad, pre, inp, *below_above("gx", xfar, xnear))
    for at, (ref, x) in enumerate(wide):
        value = ref[x].astype(F32)
        far[at], near[at] = far_near("gy", value[0:2], value[SY - 2 : SY])
    for at, ((a, ax), (i, ix)) in enumerate(zip(acts, inputs)):
        v, w = a[ax].astype(F32), i[ix].astype(F32)
        held[0:1], held[1:2] = v[0:1], w[0:1]
        held[2:3], held[3:4] = v[SY - 1 :], w[SY - 1 :]
        far[8 + at], near[8 + at] = far_near("gy", held[0:2], held[2:4])


def zpack_kernel(grad, pre, inp, xfar, xnear, yfar, ynear, far, near, low, high):
    wide, acts, inputs = fields_of(grad, pre, inp, *below_above("gx", xfar, xnear))
    ylo, yhi = below_above("gy", yfar, ynear)
    for held, lane, half in ((low, 0, True), (high, LANES - 128, False)):
        held[...] = jnp.zeros_like(held)
        cut = slice(lane, lane + 128)
        for at, (ref, x) in enumerate(wide):
            row = 12 * at
            held[row : row + 2] = ylo[at, :, cut].astype(F32)
            held[row + 2 : row + 10] = ref[x, :, cut].astype(F32)
            held[row + 10 : row + 12] = yhi[at, :, cut].astype(F32)
        for j, ((a, ax), (i, ix)) in enumerate(zip(acts, inputs)):
            row = 12 * (8 + j)
            below, above = ylo[8 + j, :, cut].astype(F32), yhi[8 + j, :, cut].astype(F32)
            v, w = a[ax, :, cut].astype(F32), i[ix, :, cut].astype(F32)

            def joined(first, second):
                if half:
                    second = pltpu.roll(second, 64, 1)
                else:
                    first = pltpu.roll(first, 64, 1)
                return jnp.where(low_half(first.shape), first, second)

            held[row + 2 : row + 10] = joined(v, w)
            for at, pair in ((row + 1, below), (row + 10, above)):
                first, second = jnp.broadcast_to(pair[0:1], (8, 128)), jnp.broadcast_to(pair[1:2], (8, 128))
                held[at : at + 1] = joined(first, second)[0:1]
    far[...], near[...] = far_near("gz", low[...], high[...])


def bands_kernel(weights, one, two, flat, turned):
    count, rows = weights.shape[0], weights.shape[1] // 2
    block = lax.broadcasted_iota(jnp.int32, (CH, 128), 1) // CH
    for which, out in enumerate((one, two)):
        flat[...] = jnp.zeros_like(flat)
        for g in range(count):
            value = weights[g].astype(F32)[which * rows : (which + 1) * rows]
            flat[g * rows : (g + 1) * rows, 256 : 256 + 27 * CH] = value
        turned[...] = pltpu.roll(flat[...], flat.shape[1] - 64, 1)
        for m in range(9):
            for a in range(4):
                at = 4 + 3 * m + 2 - a
                source = turned if at % 2 else flat
                lane = at // 2 * 128
                valid = (block + 2 - a >= 0) & (block - a <= 0)
                value = jnp.where(valid, source[:, lane : lane + 128], 0.0)
                out[m * BAND + a * CH : m * BAND + (a + 1) * CH, :] = value.astype(B16)


def fill_wide(field, layers, ylo, yhi, zlo, zhi):
    field[...] = jnp.zeros_like(field)
    for at, (ref, x) in enumerate(layers):
        row = 16 * (at + 1)
        field[row : row + 8, 128 : 128 + LANES] = ref[x].astype(F32)
        field[row - 2 : row, 128 : 128 + LANES] = ylo[at].astype(F32)
        field[row + 8 : row + 10, 128 : 128 + LANES] = yhi[at].astype(F32)
        for side, lane in ((zlo, 0), (zhi, 128 + LANES)):
            field[row - 2 : row + 10, lane : lane + 128] = side[12 * at : 12 * at + 12]


def fill_thin(field, layers, second, ylo, yhi, zlo, zhi):
    field[...] = jnp.zeros_like(field)
    for j, (ref, x) in enumerate(layers):
        at, row = 8 + j, 16 * (j + 2)
        field[row : row + 8, 128 : 128 + LANES] = ref[x].astype(F32)
        field[row - 1 : row, 128 : 128 + LANES] = ylo[at].astype(F32)[second : second + 1]
        field[row + 8 : row + 9, 128 : 128 + LANES] = yhi[at].astype(F32)[second : second + 1]
        for side, lane, upper in ((zlo, 0, True), (zhi, 128 + LANES, False)):
            value = side[12 * at : 12 * at + 12]
            if upper != bool(second):
                value = pltpu.roll(value, 64, 1)
            value = jnp.where(low_half(value.shape) != upper, value, 0.0)
            field[row - 1 : row, lane : lane + 128] = value[1:2]
            field[row : row + 8, lane : lane + 128] = value[2:10]
            field[row + 8 : row + 9, lane : lane + 128] = value[10:11]


def spread(moved, evens, odds, sign, layers):
    for i, dy in enumerate((-1, 0, 1)):
        by = (-sign * dy) % ROWS
        value = pltpu.roll(moved, by, 0) if by else moved
        tiles = [value[16 * (x + 1) : 16 * (x + 1) + 8] for x in layers]
        evens[i, 0 : 8 * len(tiles)] = jnp.concatenate(tiles, 0).astype(B16)
        odds[i, 0 : 8 * len(tiles) - 16] = jnp.concatenate(tiles[1:-1], 0).astype(B16)


def stepped(evens, odds, dy, dx, rows, lane):
    ref, row = (odds, 0) if dx == 0 else (evens, 8 + 8 * dx)
    return ref[dy, row : row + rows, lane : lane + BAND]


def own_columns(evens, odds, columns, sign):
    for m in range(9):
        for h in range(OWN_GROUPS):
            columns[OWN_ROWS * h : OWN_ROWS * (h + 1), BAND * m : BAND * (m + 1)] = stepped(
                evens, odds, m % 3, sign * (m // 3 - 1), OWN_ROWS, 128 * h + 128
            )


def edge_rows(count):
    row = lax.broadcasted_iota(jnp.int32, (16 * count, ROWS), 0)
    column = lax.broadcasted_iota(jnp.int32, (16 * count, ROWS), 1)
    m, x = row // 16 + (4 if count == 1 else 0), row % 8
    source = 16 * (x - m // 3 + 2) + jnp.where(row % 16 < 8, -1, 8) - m % 3 + 1
    return jnp.where(column == source, 1.0, 0.0).astype(B16)


def slope(v):
    g = jax.nn.sigmoid(v)
    return g * (1.0 + v * (1.0 - g))


def main_kernel(scale, grad, pre, inp, xfar, xnear, yfar, ynear, zfar, znear, band,
                kept, sent, pre_out, fg, fa, fi, moved, picked, evens, odds, columns, many, left, left_f, grads_one, grads_two, held, zlo, zhi):
    wide, acts, inputs = fields_of(grad, pre, inp, *below_above("gx", xfar, xnear))
    ylo, yhi = below_above("gy", yfar, ynear)
    below, above = below_above("gz", zfar, znear)
    zlo[...] = below[...]
    zhi[...] = above[...]
    halos = (ylo, yhi, zlo, zhi)
    fill_wide(fg, wide, *halos)
    fill_thin(fa, acts, 0, *halos)
    fill_thin(fi, inputs, 1, *halos)
    contract = (((0,), (0,)), ((), ()))

    v = fa[...]
    act = (v * jax.nn.sigmoid(v)).astype(B16).astype(F32)
    spread(pltpu.roll(act, 64, 1), evens, odds, 1, range(1, SX + 3))
    own_columns(evens, odds, columns, 1)
    for h in range(OWN_GROUPS):
        for x in range(SX):
            row = OWN_ROWS * h + 8 * x
            left_f[row : row + 8, :] = grad[x, :, 128 * h : 128 * (h + 1)].astype(F32)
    left[...] = left_f[...].astype(B16)
    grads_two[...] = lax.dot_general(left[...], columns[...], contract, preferred_element_type=F32)

    moved[...] = pltpu.roll(fg[...], 64, 1)
    spread(moved[...], evens, odds, -1, range(SX + 4))
    for m in range(9):
        dx, dy = m // 3 - 1, m % 3
        for h in range(HALO_GROUPS):
            many[HALO_ROWS * h : HALO_ROWS * (h + 1), BAND * m : BAND * (m + 1)] = stepped(
                evens, odds, dy, -dx, HALO_ROWS, 128 * h
            )
    picked[...] = jnp.dot(edge_rows(9), moved[...].astype(B16), preferred_element_type=F32).astype(B16)
    for m in range(9):
        for h in range(HALO_GROUPS):
            row = EDGES + 16 * h
            many[row : row + 16, BAND * m : BAND * (m + 1)] = picked[
                16 * m : 16 * (m + 1), 128 * h : 128 * h + BAND
            ]
    held[...] = jnp.dot(many[...], band[...], preferred_element_type=F32)
    fg[:, 128 * HALO_GROUPS :] = jnp.zeros((ROWS, WIDE - 128 * HALO_GROUPS), F32)
    place = edge_rows(1)
    beside = slope(jnp.dot(place, fa[:, : 128 * HALO_GROUPS].astype(B16), preferred_element_type=F32))
    ends = jnp.concatenate(
        [held[EDGES + 16 * h : EDGES + 16 * (h + 1), :] for h in range(HALO_GROUPS)], 1
    )
    value = (ends * beside).astype(B16)
    fg[:, : 128 * HALO_GROUPS] = lax.dot_general(place, value, contract, preferred_element_type=F32)
    for h in range(HALO_GROUPS):
        lanes = slice(128 * h, 128 * (h + 1))
        for x in range(1, SX + 3):
            row, at = HALO_ROWS * h + 8 * (x - 1), slice(16 * (x + 1), 16 * (x + 1) + 8)
            value = held[row : row + 8, :] * slope(fa[at, lanes])
            fg[at, lanes] = value.astype(B16).astype(F32)
    pre_out[...] = pltpu.roll(fg[...], 64, 1).astype(B16)

    spread(pltpu.roll(fi[...], 64, 1), evens, odds, 1, range(1, SX + 3))
    own_columns(evens, odds, columns, 1)
    for h in range(OWN_GROUPS):
        for x in range(SX):
            row, at = OWN_ROWS * h + 8 * x, 16 * (x + 3)
            left_f[row : row + 8, :] = fg[at : at + 8, 128 * h + 128 : 128 * h + 256]
    left[...] = left_f[...].astype(B16)
    grads_one[...] = lax.dot_general(left[...], columns[...], contract, preferred_element_type=F32)

    count, rows = kept.shape[0], kept.shape[1]
    even = lax.rem(lax.axis_index("gz"), 2) == 0

    def block(source, k):
        m, t = k // 3, k % 3
        pieces = []
        for b in ((k + t) % 2, (k + t + 1) % 2):
            lane = (4 * m + b + t) // 2 * 128
            pieces.append(source[64 * b : 64 * (b + 1), lane : lane + 128])
        return pieces[0] + pltpu.roll(pieces[1], 64, 1)

    for j in range(14):
        pair = []
        for source in (grads_one, grads_two):
            value = block(source, 2 * j)
            if j < 13:
                value = jnp.where(low_half(value.shape), value, block(source, 2 * j + 1))
            pair.append(value * scale)
        width = 128 if j < 13 else 64
        keep = jnp.where(even, pair[0], pair[1])[:, :width]
        send = jnp.where(even, pair[1], pair[0])[:, :width]
        for g in range(count):
            kept[g, :, 128 * j : 128 * j + width] = keep[g * rows : (g + 1) * rows, :]
            sent[g, :, 128 * j : 128 * j + width] = send[g * rows : (g + 1) * rows, :].astype(B16)


def last_kernel(pre_grad, grad, band, out, evens, odds, columns, held):
    spread(pre_grad[...].astype(F32), evens, odds, -1, range(1, SX + 3))
    own_columns(evens, odds, columns, -1)
    held[...] = jnp.dot(columns[...], band[...], preferred_element_type=F32)
    for h in range(OWN_GROUPS):
        for x in range(SX):
            row, lanes = OWN_ROWS * h + 8 * x, slice(128 * h, 128 * (h + 1))
            out[x, :, lanes] = (held[row : row + 8, :] + grad[x, :, lanes].astype(F32)).astype(B16)


def swapped(far, near, axis):
    count = lax.axis_size(axis)
    steps = [1 if i % 2 else -1 for i in range(count)]
    return (
        lax.ppermute(far, axis, [(i, (i + step) % count) for i, step in enumerate(steps)]),
        lax.ppermute(near, axis, [(i, i - step) for i, step in enumerate(steps)]),
    )


def total_kernel(parts, out):
    value = parts[0].astype(F32)
    for i in range(1, parts.shape[0]):
        value += parts[i].astype(F32)
    value = value.astype(out.dtype)
    if out.ndim == value.ndim:
        out[...] = value
    else:
        for i in range(out.shape[0]):
            out[i] = value


def pair_kernel(kept, came, out):
    out[...] = (kept[...] + came[...].astype(F32)).astype(B16)


def last_total_kernel(parts, one, two):
    first, second = parts[0], parts[1]
    for i in range(2, parts.shape[0], 2):
        first += parts[i]
        second += parts[i + 1]
    one[...] = first
    two[...] = second


def reduced(kept, sent, other):
    rows, columns = kept.shape[1:]
    gy, gz = lax.axis_size("gy"), lax.axis_size("gz")
    came = lax.ppermute(sent, "gz", [(i, i + 1 - 2 * (i % 2)) for i in range(gz)])
    came, other = lax.optimization_barrier((came, other))
    (slots,) = call(pair_kernel, [(kept.shape, B16)], [], 1000, 500000, kept, came)
    parts = lax.all_to_all(slots, "gx", 0, 0, tiled=True)
    (copies,) = call(total_kernel, [((gy, rows, columns), B16)], [], 1000, 500000, parts)
    parts = lax.all_to_all(copies, "gy", 0, 0, tiled=True)
    (part,) = call(total_kernel, [((rows, columns), F32)], [], 1000, 500000, parts)
    parts = lax.all_gather(part, "gz", axis=0)
    grads = ((rows, columns), F32)
    one, two = call(last_total_kernel, [grads, grads], [], 1000, 500000, parts)
    return other, one, two


def body(block_input, pre_act, skip_grad, pool_grad, conv1_weight, conv2_weight):
    count = lax.axis_size("gx")
    rows = CH // count
    cells = SX * SY * SZ * count * lax.axis_size("gy") * lax.axis_size("gz")
    block, message = ((SX, SY, LANES), B16), ((4, SY, LANES), B16)
    weight = ((rows, 27 * CH), B16)
    grad, pre, inp, far, near, copies = call(
        prep_kernel,
        [block, block, block, message, message, ((count, 2 * rows, 27 * CH), B16)],
        [
            block, ((SX // 2, SY // 2, LANES // 2), B16), weight, weight,
            ((SX // 2, SY, LANES), F32), ((2 * rows, 27 * CH), F32), pltpu.SemaphoreType.DMA((6,)),
        ],
        100000, 400000,
        *(
            pltpu.with_memory_space_constraint(array, pltpu.HBM)
            for array in (skip_grad, pool_grad, pre_act, block_input, conv1_weight, conv2_weight)
        ),
        space=pltpu.HBM,
    )
    xfar, xnear = swapped(far, near, "gx")
    fields = (grad, pre, inp, xfar, xnear)
    message = ((LAYERS, 2, LANES), B16)
    yfar, ynear = swapped(
        *call(ypack_kernel, [message, message], [((4, LANES), F32)], 60000000000, 600000, *fields), "gy"
    )
    side = ((12 * LAYERS, 128), F32)
    gathered = lax.all_to_all(copies, "gx", 0, 0, tiled=True)
    message = ((12 * LAYERS, 128), B16)
    zfar, znear = swapped(
        *call(zpack_kernel, [message, message], [side, side], 100000, 700000, *fields, yfar, ynear), "gz"
    )
    matrix = ((DEPTH, 128), B16)
    flat = ((CH, 36 * CH), F32)
    band_one, band_two = call(bands_kernel, [matrix, matrix], [flat, flat], 1000000, 4000000, gathered)
    field = ((ROWS, WIDE), F32)
    evens, odds = ((3, 8 * (SX + 4), WIDE), B16), ((3, 8 * (SX + 2), WIDE), B16)
    columns = ((OWN_GROUPS * OWN_ROWS, DEPTH), B16)
    kept, sent, pre_grad = call(
        functools.partial(main_kernel, 1.0 / math.sqrt(cells)),
        [((count, rows, 27 * CH), F32), ((count, rows, 27 * CH), B16), ((ROWS, WIDE), B16)],
        [
            field, field, field, field, ((ROWS, WIDE), B16), evens, odds, columns,
            ((MANY, DEPTH), B16), ((OWN_GROUPS * OWN_ROWS, 128), B16), ((OWN_GROUPS * OWN_ROWS, 128), F32),
            ((128, DEPTH), F32), ((128, DEPTH), F32), ((MANY, 128), F32), side, side,
        ],
        2 * 900 * 1000 * 1000, 8000000,
        *fields, yfar, ynear, zfar, znear, band_two,
        grant=32,
    )
    (input_grad,) = call(
        last_kernel,
        [((SX, SY, LANES), B16)],
        [evens, odds, columns, ((OWN_GROUPS * OWN_ROWS, 128), F32)],
        500000000, 4000000,
        pre_grad, grad, band_one,
    )
    return reduced(kept, sent, input_grad)


def solution(mesh):
    in_specs = (
        P("gx", "gy", "gz"),
        P("gx", "gy", "gz"),
        P("gx", "gy", "gz"),
        P("gx", "gy", "gz"),
        P("gx", None),
        P("gx", None),
    )
    out_specs = (P("gx", "gy", "gz"), P("gx", None), P("gx", None))
    return jax.shard_map(body, mesh=mesh, in_specs=in_specs, out_specs=out_specs, check_vma=False)
```

```python
import functools
import math

import jax
import jax.numpy as jnp
from jax import lax
from jax.experimental import pallas as pl
from jax.experimental.pallas import tpu as pltpu
from jax.sharding import PartitionSpec as P

F32, B16 = jnp.float32, jnp.bfloat16
SX, SY, SZ, CH = 4, 8, 16, 64
LANES = SZ * CH
ROWS = 16 * (SX + 5)
WIDE = LANES + 6 * CH
BAND = 4 * CH
OWN_GROUPS, HALO_GROUPS = SZ // 2, SZ // 2 + 2
DEPTH = 9 * BAND
OWN_ROWS = 8 * SX
HALO_ROWS = 8 * (SX + 2)
EDGES = HALO_GROUPS * HALO_ROWS
MANY = EDGES + HALO_GROUPS * 16
LAYERS = 14


def call(kernel, outs, scratch, flops, moved, *args, space=pltpu.VMEM, grant=12):
    return pl.pallas_call(
        kernel,
        out_shape=[jax.ShapeDtypeStruct(shape, dtype) for shape, dtype in outs],
        in_specs=[pl.BlockSpec(memory_space=space)] * len(args),
        out_specs=[pl.BlockSpec(memory_space=pltpu.VMEM)] * len(outs),
        scratch_shapes=[pltpu.VMEM(*held) if isinstance(held, tuple) else held for held in scratch],
        compiler_params=pltpu.CompilerParams(vmem_limit_bytes=grant * 1024 * 1024),
        cost_estimate=pl.CostEstimate(flops=flops, bytes_accessed=moved, transcendentals=0),
    )(*args)


def low_half(shape):
    return lax.broadcasted_iota(jnp.int32, shape, len(shape) - 1) % 128 < 64


class Either:
    def __init__(self, axis, if_odd, if_even):
        self.odd = lax.rem(lax.axis_index(axis), 2) == 1
        self.refs = if_odd, if_even

    def __getitem__(self, at):
        first, second = (ref[at].astype(F32) for ref in self.refs)
        return jnp.where(self.odd, first, second)


def below_above(axis, far, near):
    return Either(axis, near, far), Either(axis, far, near)


def far_near(axis, low, high):
    odd = lax.rem(lax.axis_index(axis), 2) == 1
    return jnp.where(odd, high, low).astype(B16), jnp.where(odd, low, high).astype(B16)


def prep_kernel(skip_in, pool_in, pre_in, inp_in, one_in, two_in,
                grad, pre, inp, far, near, copies, skip, pool, one, two, up, rows, sems):
    moves = [
        pltpu.make_async_copy(source, target, sems.at[i])
        for i, (source, target) in enumerate(
            ((skip_in, skip), (pool_in, pool), (pre_in, pre), (inp_in, inp), (one_in, one), (two_in, two))
        )
    ]
    for move in moves:
        move.start()
    for move in moves:
        move.wait()
    each = one.shape[0]
    rows[0:each], rows[each : 2 * each] = one[...].astype(F32), two[...].astype(F32)
    both = rows[...].astype(B16)
    for g in range(copies.shape[0]):
        copies[g] = both
    for px in range(SX // 2):
        pieces = []
        for j in range(LANES // 256):
            v = pool[px, :, 128 * j : 128 * (j + 1)].astype(F32)
            turned = pltpu.roll(v, 64, 1)
            first = low_half(v.shape)
            pieces += [jnp.where(first, v, turned), jnp.where(first, turned, v)]
        for y in range(SY):
            for j, piece in enumerate(pieces):
                up[px, y : y + 1, 128 * j : 128 * (j + 1)] = piece[y // 2 : y // 2 + 1, :]
    for x in range(SX):
        value = (skip[x].astype(F32) + 0.125 * up[x // 2]).astype(B16)
        grad[x] = value
    ends = ((grad, 0, 2), (grad, 1, 3), (pre, 0, SX - 1), (inp, 0, SX - 1))
    for at, (ref, bottom, top) in enumerate(ends):
        far[at], near[at] = far_near("gx", ref[bottom].astype(F32), ref[top].astype(F32))


def fields_of(grad, pre, inp, xlo, xhi):
    def own(ref):
        return [(ref, x) for x in range(SX)]

    return (
        [(xlo, 0), (xlo, 1)] + own(grad) + [(xhi, 0), (xhi, 1)],
        [(xlo, 2)] + own(pre) + [(xhi, 2)],
        [(xlo, 3)] + own(inp) + [(xhi, 3)],
    )


def ypack_kernel(grad, pre, inp, xfar, xnear, far, near, held):
    wide, acts, inputs = fields_of(grad, pre, inp, *below_above("gx", xfar, xnear))
    for at, (ref, x) in enumerate(wide):
        value = ref[x].astype(F32)
        far[at], near[at] = far_near("gy", value[0:2], value[SY - 2 : SY])
    for at, ((a, ax), (i, ix)) in enumerate(zip(acts, inputs)):
        v, w = a[ax].astype(F32), i[ix].astype(F32)
        held[0:1], held[1:2] = v[0:1], w[0:1]
        held[2:3], held[3:4] = v[SY - 1 :], w[SY - 1 :]
        far[8 + at], near[8 + at] = far_near("gy", held[0:2], held[2:4])


def zpack_kernel(grad, pre, inp, xfar, xnear, yfar, ynear, far, near, low, high):
    wide, acts, inputs = fields_of(grad, pre, inp, *below_above("gx", xfar, xnear))
    ylo, yhi = below_above("gy", yfar, ynear)
    for held, lane, half in ((low, 0, True), (high, LANES - 128, False)):
        held[...] = jnp.zeros_like(held)
        cut = slice(lane, lane + 128)
        for at, (ref, x) in enumerate(wide):
            row = 12 * at
            held[row : row + 2] = ylo[at, :, cut].astype(F32)
            held[row + 2 : row + 10] = ref[x, :, cut].astype(F32)
            held[row + 10 : row + 12] = yhi[at, :, cut].astype(F32)
        for j, ((a, ax), (i, ix)) in enumerate(zip(acts, inputs)):
            row = 12 * (8 + j)
            below, above = ylo[8 + j, :, cut].astype(F32), yhi[8 + j, :, cut].astype(F32)
            v, w = a[ax, :, cut].astype(F32), i[ix, :, cut].astype(F32)

            def joined(first, second):
                if half:
                    second = pltpu.roll(second, 64, 1)
                else:
                    first = pltpu.roll(first, 64, 1)
                return jnp.where(low_half(first.shape), first, second)

            held[row + 2 : row + 10] = joined(v, w)
            for at, pair in ((row + 1, below), (row + 10, above)):
                first, second = jnp.broadcast_to(pair[0:1], (8, 128)), jnp.broadcast_to(pair[1:2], (8, 128))
                held[at : at + 1] = joined(first, second)[0:1]
    far[...], near[...] = far_near("gz", low[...], high[...])


def bands_kernel(weights, one, two, flat, turned):
    count, rows = weights.shape[0], weights.shape[1] // 2
    block = lax.broadcasted_iota(jnp.int32, (CH, 128), 1) // CH
    for which, out in enumerate((one, two)):
        flat[...] = jnp.zeros_like(flat)
        for g in range(count):
            value = weights[g].astype(F32)[which * rows : (which + 1) * rows]
            flat[g * rows : (g + 1) * rows, 256 : 256 + 27 * CH] = value
        turned[...] = pltpu.roll(flat[...], flat.shape[1] - 64, 1)
        for m in range(9):
            for a in range(4):
                at = 4 + 3 * m + 2 - a
                source = turned if at % 2 else flat
                lane = at // 2 * 128
                valid = (block + 2 - a >= 0) & (block - a <= 0)
                value = jnp.where(valid, source[:, lane : lane + 128], 0.0)
                out[m * BAND + a * CH : m * BAND + (a + 1) * CH, :] = value.astype(B16)


def fill_wide(field, layers, ylo, yhi, zlo, zhi):
    field[...] = jnp.zeros_like(field)
    for at, (ref, x) in enumerate(layers):
        row = 16 * (at + 1)
        field[row : row + 8, 128 : 128 + LANES] = ref[x].astype(F32)
        field[row - 2 : row, 128 : 128 + LANES] = ylo[at].astype(F32)
        field[row + 8 : row + 10, 128 : 128 + LANES] = yhi[at].astype(F32)
        for side, lane in ((zlo, 0), (zhi, 128 + LANES)):
            field[row - 2 : row + 10, lane : lane + 128] = side[12 * at : 12 * at + 12]


def fill_thin(field, layers, second, ylo, yhi, zlo, zhi):
    field[...] = jnp.zeros_like(field)
    for j, (ref, x) in enumerate(layers):
        at, row = 8 + j, 16 * (j + 2)
        field[row : row + 8, 128 : 128 + LANES] = ref[x].astype(F32)
        field[row - 1 : row, 128 : 128 + LANES] = ylo[at].astype(F32)[second : second + 1]
        field[row + 8 : row + 9, 128 : 128 + LANES] = yhi[at].astype(F32)[second : second + 1]
        for side, lane, upper in ((zlo, 0, True), (zhi, 128 + LANES, False)):
            value = side[12 * at : 12 * at + 12]
            if upper != bool(second):
                value = pltpu.roll(value, 64, 1)
            value = jnp.where(low_half(value.shape) != upper, value, 0.0)
            field[row - 1 : row, lane : lane + 128] = value[1:2]
            field[row : row + 8, lane : lane + 128] = value[2:10]
            field[row + 8 : row + 9, lane : lane + 128] = value[10:11]


def spread(moved, evens, odds, sign, layers):
    for i, dy in enumerate((-1, 0, 1)):
        by = (-sign * dy) % ROWS
        value = pltpu.roll(moved, by, 0) if by else moved
        tiles = [value[16 * (x + 1) : 16 * (x + 1) + 8] for x in layers]
        evens[i, 0 : 8 * len(tiles)] = jnp.concatenate(tiles, 0).astype(B16)
        odds[i, 0 : 8 * len(tiles) - 16] = jnp.concatenate(tiles[1:-1], 0).astype(B16)


def stepped(evens, odds, dy, dx, rows, lane):
    ref, row = (odds, 0) if dx == 0 else (evens, 8 + 8 * dx)
    return ref[dy, row : row + rows, lane : lane + BAND]


def own_columns(evens, odds, columns, sign):
    for m in range(9):
        for h in range(OWN_GROUPS):
            columns[OWN_ROWS * h : OWN_ROWS * (h + 1), BAND * m : BAND * (m + 1)] = stepped(
                evens, odds, m % 3, sign * (m // 3 - 1), OWN_ROWS, 128 * h + 128
            )


def edge_rows(count):
    row = lax.broadcasted_iota(jnp.int32, (16 * count, ROWS), 0)
    column = lax.broadcasted_iota(jnp.int32, (16 * count, ROWS), 1)
    m, x = row // 16 + (4 if count == 1 else 0), row % 8
    source = 16 * (x - m // 3 + 2) + jnp.where(row % 16 < 8, -1, 8) - m % 3 + 1
    return jnp.where(column == source, 1.0, 0.0).astype(B16)


def slope(v):
    g = jax.nn.sigmoid(v)
    return g * (1.0 + v * (1.0 - g))


def main_kernel(scale, grad, pre, inp, xfar, xnear, yfar, ynear, znear, zfar, band,
                kept, sent, pre_out, fg, fa, fi, moved, picked, evens, odds, columns, many, left, left_f, grads_one, grads_two, held, zlo, zhi):
    wide, acts, inputs = fields_of(grad, pre, inp, *below_above("gx", xfar, xnear))
    ylo, yhi = below_above("gy", yfar, ynear)
    below, above = below_above("gz", zfar, znear)
    zlo[...] = below[...]
    zhi[...] = above[...]
    halos = (ylo, yhi, zlo, zhi)
    fill_wide(fg, wide, *halos)
    fill_thin(fa, acts, 0, *halos)
    fill_thin(fi, inputs, 1, *halos)
    contract = (((0,), (0,)), ((), ()))

    v = fa[...]
    act = (v * jax.nn.sigmoid(v)).astype(B16).astype(F32)
    spread(pltpu.roll(act, 64, 1), evens, odds, 1, range(1, SX + 3))
    own_columns(evens, odds, columns, 1)
    for h in range(OWN_GROUPS):
        for x in range(SX):
            row = OWN_ROWS * h + 8 * x
            left_f[row : row + 8, :] = grad[x, :, 128 * h : 128 * (h + 1)].astype(F32)
    left[...] = left_f[...].astype(B16)
    grads_two[...] = lax.dot_general(left[...], columns[...], contract, preferred_element_type=F32)

    moved[...] = pltpu.roll(fg[...], 64, 1)
    spread(moved[...], evens, odds, -1, range(SX + 4))
    for m in range(9):
        dx, dy = m // 3 - 1, m % 3
        for h in range(HALO_GROUPS):
            many[HALO_ROWS * h : HALO_ROWS * (h + 1), BAND * m : BAND * (m + 1)] = stepped(
                evens, odds, dy, -dx, HALO_ROWS, 128 * h
            )
    picked[...] = jnp.dot(edge_rows(9), moved[...].astype(B16), preferred_element_type=F32).astype(B16)
    for m in range(9):
        for h in range(HALO_GROUPS):
            row = EDGES + 16 * h
            many[row : row + 16, BAND * m : BAND * (m + 1)] = picked[
                16 * m : 16 * (m + 1), 128 * h : 128 * h + BAND
            ]
    held[...] = jnp.dot(many[...], band[...], preferred_element_type=F32)
    fg[:, 128 * HALO_GROUPS :] = jnp.zeros((ROWS, WIDE - 128 * HALO_GROUPS), F32)
    place = edge_rows(1)
    beside = slope(jnp.dot(place, fa[:, : 128 * HALO_GROUPS].astype(B16), preferred_element_type=F32))
    ends = jnp.concatenate(
        [held[EDGES + 16 * h : EDGES + 16 * (h + 1), :] for h in range(HALO_GROUPS)], 1
    )
    value = (ends * beside).astype(B16)
    fg[:, : 128 * HALO_GROUPS] = lax.dot_general(place, value, contract, preferred_element_type=F32)
    for h in range(HALO_GROUPS):
        lanes = slice(128 * h, 128 * (h + 1))
        for x in range(1, SX + 3):
            row, at = HALO_ROWS * h + 8 * (x - 1), slice(16 * (x + 1), 16 * (x + 1) + 8)
            value = held[row : row + 8, :] * slope(fa[at, lanes])
            fg[at, lanes] = value.astype(B16).astype(F32)
    pre_out[...] = pltpu.roll(fg[...], 64, 1).astype(B16)

    spread(pltpu.roll(fi[...], 64, 1), evens, odds, 1, range(1, SX + 3))
    own_columns(evens, odds, columns, 1)
    for h in range(OWN_GROUPS):
        for x in range(SX):
            row, at = OWN_ROWS * h + 8 * x, 16 * (x + 3)
            left_f[row : row + 8, :] = fg[at : at + 8, 128 * h + 128 : 128 * h + 256]
    left[...] = left_f[...].astype(B16)
    grads_one[...] = lax.dot_general(left[...], columns[...], contract, preferred_element_type=F32)

    count, rows = kept.shape[0], kept.shape[1]
    even = lax.rem(lax.axis_index("gz"), 2) == 0

    def block(source, k):
        m, t = k // 3, k % 3
        pieces = []
        for b in ((k + t) % 2, (k + t + 1) % 2):
            lane = (4 * m + b + t) // 2 * 128
            pieces.append(source[64 * b : 64 * (b + 1), lane : lane + 128])
        return pieces[0] + pltpu.roll(pieces[1], 64, 1)

    for j in range(14):
        pair = []
        for source in (grads_one, grads_two):
            value = block(source, 2 * j)
            if j < 13:
                value = jnp.where(low_half(value.shape), value, block(source, 2 * j + 1))
            pair.append(value * scale)
        width = 128 if j < 13 else 64
        keep = jnp.where(even, pair[0], pair[1])[:, :width]
        send = jnp.where(even, pair[1], pair[0])[:, :width]
        for g in range(count):
            kept[g, :, 128 * j : 128 * j + width] = keep[g * rows : (g + 1) * rows, :]
            sent[g, :, 128 * j : 128 * j + width] = send[g * rows : (g + 1) * rows, :].astype(B16)


def last_kernel(pre_grad, grad, band, out, evens, odds, columns, held):
    spread(pre_grad[...].astype(F32), evens, odds, -1, range(1, SX + 3))
    own_columns(evens, odds, columns, -1)
    held[...] = jnp.dot(columns[...], band[...], preferred_element_type=F32)
    for h in range(OWN_GROUPS):
        for x in range(SX):
            row, lanes = OWN_ROWS * h + 8 * x, slice(128 * h, 128 * (h + 1))
            out[x, :, lanes] = (held[row : row + 8, :] + grad[x, :, lanes].astype(F32)).astype(B16)


def swapped(far, near, axis):
    count = lax.axis_size(axis)
    steps = [1 if i % 2 else -1 for i in range(count)]
    return (
        lax.ppermute(far, axis, [(i, (i + step) % count) for i, step in enumerate(steps)]),
        lax.ppermute(near, axis, [(i, i - step) for i, step in enumerate(steps)]),
    )


def total_kernel(parts, out):
    value = parts[0].astype(F32)
    for i in range(1, parts.shape[0]):
        value += parts[i].astype(F32)
    value = value.astype(out.dtype)
    if out.ndim == value.ndim:
        out[...] = value
    else:
        for i in range(out.shape[0]):
            out[i] = value


def pair_kernel(kept, came, out):
    out[...] = (kept[...] + came[...].astype(F32)).astype(B16)


def last_total_kernel(parts, one, two):
    first, second = parts[0], parts[1]
    for i in range(2, parts.shape[0], 2):
        first += parts[i]
        second += parts[i + 1]
    one[...] = first
    two[...] = second


def reduced(kept, sent, other):
    rows, columns = kept.shape[1:]
    gy, gz = lax.axis_size("gy"), lax.axis_size("gz")
    came = lax.ppermute(sent, "gz", [(i, i + 1 - 2 * (i % 2)) for i in range(gz)])
    came, other = lax.optimization_barrier((came, other))
    (slots,) = call(pair_kernel, [(kept.shape, B16)], [], 1000, 500000, kept, came)
    parts = lax.all_to_all(slots, "gx", 0, 0, tiled=True)
    (copies,) = call(total_kernel, [((gy, rows, columns), B16)], [], 1000, 500000, parts)
    parts = lax.all_to_all(copies, "gy", 0, 0, tiled=True)
    (part,) = call(total_kernel, [((rows, columns), F32)], [], 1000, 500000, parts)
    parts = lax.all_gather(part, "gz", axis=0)
    grads = ((rows, columns), F32)
    one, two = call(last_total_kernel, [grads, grads], [], 1000, 500000, parts)
    return other, one, two


def body(block_input, pre_act, skip_grad, pool_grad, conv1_weight, conv2_weight):
    count = lax.axis_size("gx")
    rows = CH // count
    cells = SX * SY * SZ * count * lax.axis_size("gy") * lax.axis_size("gz")
    block, message = ((SX, SY, LANES), B16), ((4, SY, LANES), B16)
    weight = ((rows, 27 * CH), B16)
    grad, pre, inp, far, near, copies = call(
        prep_kernel,
        [block, block, block, message, message, ((count, 2 * rows, 27 * CH), B16)],
        [
            block, ((SX // 2, SY // 2, LANES // 2), B16), weight, weight,
            ((SX // 2, SY, LANES), F32), ((2 * rows, 27 * CH), F32), pltpu.SemaphoreType.DMA((6,)),
        ],
        100000, 400000,
        *(
            pltpu.with_memory_space_constraint(array, pltpu.HBM)
            for array in (skip_grad, pool_grad, pre_act, block_input, conv1_weight, conv2_weight)
        ),
        space=pltpu.HBM,
    )
    xfar, xnear = swapped(far, near, "gx")
    fields = (grad, pre, inp, xfar, xnear)
    message = ((LAYERS, 2, LANES), B16)
    yfar, ynear = swapped(
        *call(ypack_kernel, [message, message], [((4, LANES), F32)], 60000000000, 600000, *fields), "gy"
    )
    side = ((12 * LAYERS, 128), F32)
    gathered = lax.all_to_all(copies, "gx", 0, 0, tiled=True)
    message = ((12 * LAYERS, 128), B16)
    zfar, znear = swapped(
        *call(zpack_kernel, [message, message], [side, side], 100000, 700000, *fields, yfar, ynear), "gz"
    )
    matrix = ((DEPTH, 128), B16)
    flat = ((CH, 36 * CH), F32)
    band_one, band_two = call(bands_kernel, [matrix, matrix], [flat, flat], 1000000, 4000000, gathered)
    field = ((ROWS, WIDE), F32)
    evens, odds = ((3, 8 * (SX + 4), WIDE), B16), ((3, 8 * (SX + 2), WIDE), B16)
    columns = ((OWN_GROUPS * OWN_ROWS, DEPTH), B16)
    kept, sent, pre_grad = call(
        functools.partial(main_kernel, 1.0 / math.sqrt(cells)),
        [((count, rows, 27 * CH), F32), ((count, rows, 27 * CH), B16), ((ROWS, WIDE), B16)],
        [
            field, field, field, field, ((ROWS, WIDE), B16), evens, odds, columns,
            ((MANY, DEPTH), B16), ((OWN_GROUPS * OWN_ROWS, 128), B16), ((OWN_GROUPS * OWN_ROWS, 128), F32),
            ((128, DEPTH), F32), ((128, DEPTH), F32), ((MANY, 128), F32), side, side,
        ],
        2 * 900 * 1000 * 1000, 8000000,
        *fields, yfar, ynear, znear, zfar, band_two,
        grant=32,
    )
    (input_grad,) = call(
        last_kernel,
        [((SX, SY, LANES), B16)],
        [evens, odds, columns, ((OWN_GROUPS * OWN_ROWS, 128), F32)],
        500000000, 4000000,
        pre_grad, grad, band_one,
    )
    return reduced(kept, sent, input_grad)


def solution(mesh):
    in_specs = (
        P("gx", "gy", "gz"),
        P("gx", "gy", "gz"),
        P("gx", "gy", "gz"),
        P("gx", "gy", "gz"),
        P("gx", None),
        P("gx", None),
    )
    out_specs = (P("gx", "gy", "gz"), P("gx", None), P("gx", None))
    return jax.shard_map(body, mesh=mesh, in_specs=in_specs, out_specs=out_specs, check_vma=False)
```

```python
import functools
import math

import jax
import jax.numpy as jnp
from jax import lax
from jax.experimental import pallas as pl
from jax.experimental.pallas import tpu as pltpu
from jax.sharding import PartitionSpec as P

F32, B16 = jnp.float32, jnp.bfloat16
SX, SY, SZ, CH = 4, 8, 16, 64
LANES = SZ * CH
ROWS = 16 * (SX + 5)
WIDE = LANES + 6 * CH
BAND = 4 * CH
OWN_GROUPS, HALO_GROUPS = SZ // 2, SZ // 2 + 2
DEPTH = 9 * BAND
OWN_ROWS = 8 * SX
HALO_ROWS = 8 * (SX + 2)
EDGES = HALO_GROUPS * HALO_ROWS
MANY = EDGES + HALO_GROUPS * 16
LAYERS = 14


def call(kernel, outs, scratch, flops, moved, *args, space=pltpu.VMEM, grant=12):
    return pl.pallas_call(
        kernel,
        out_shape=[jax.ShapeDtypeStruct(shape, dtype) for shape, dtype in outs],
        in_specs=[pl.BlockSpec(memory_space=space)] * len(args),
        out_specs=[pl.BlockSpec(memory_space=pltpu.VMEM)] * len(outs),
        scratch_shapes=[pltpu.VMEM(*held) if isinstance(held, tuple) else held for held in scratch],
        compiler_params=pltpu.CompilerParams(vmem_limit_bytes=grant * 1024 * 1024),
        cost_estimate=pl.CostEstimate(flops=flops, bytes_accessed=moved, transcendentals=0),
    )(*args)


def low_half(shape):
    return lax.broadcasted_iota(jnp.int32, shape, len(shape) - 1) % 128 < 64


class Either:
    def __init__(self, axis, if_odd, if_even):
        self.odd = lax.rem(lax.axis_index(axis), 2) == 1
        self.refs = if_odd, if_even

    def __getitem__(self, at):
        first, second = (ref[at].astype(F32) for ref in self.refs)
        return jnp.where(self.odd, first, second)


def below_above(axis, far, near):
    return Either(axis, near, far), Either(axis, far, near)


def far_near(axis, low, high):
    odd = lax.rem(lax.axis_index(axis), 2) == 1
    return jnp.where(odd, high, low).astype(B16), jnp.where(odd, low, high).astype(B16)


def prep_kernel(skip_in, pool_in, pre_in, inp_in, one_in, two_in,
                grad, pre, inp, far, near, copies, skip, pool, one, two, up, rows, sems):
    moves = [
        pltpu.make_async_copy(source, target, sems.at[i])
        for i, (source, target) in enumerate(
            ((skip_in, skip), (pool_in, pool), (pre_in, pre), (inp_in, inp), (one_in, one), (two_in, two))
        )
    ]
    for move in moves:
        move.start()
    for move in moves:
        move.wait()
    each = one.shape[0]
    rows[0:each], rows[each : 2 * each] = one[...].astype(F32), two[...].astype(F32)
    both = rows[...].astype(B16)
    for g in range(copies.shape[0]):
        copies[g] = both
    for px in range(SX // 2):
        pieces = []
        for j in range(LANES // 256):
            v = pool[px, :, 128 * j : 128 * (j + 1)].astype(F32)
            turned = pltpu.roll(v, 64, 1)
            first = low_half(v.shape)
            pieces += [jnp.where(first, v, turned), jnp.where(first, turned, v)]
        for y in range(SY):
            for j, piece in enumerate(pieces):
                up[px, y : y + 1, 128 * j : 128 * (j + 1)] = piece[y // 2 : y // 2 + 1, :]
    for x in range(SX):
        value = (skip[x].astype(F32) + 0.125 * up[x // 2]).astype(B16)
        grad[x] = value
    ends = ((grad, 0, 2), (grad, 1, 3), (pre, 0, SX - 1), (inp, 0, SX - 1))
    for at, (ref, bottom, top) in enumerate(ends):
        far[at], near[at] = far_near("gx", ref[bottom].astype(F32), ref[top].astype(F32))


def fields_of(grad, pre, inp, xlo, xhi):
    def own(ref):
        return [(ref, x) for x in range(SX)]

    return (
        [(xlo, 0), (xlo, 1)] + own(grad) + [(xhi, 0), (xhi, 1)],
        [(xlo, 2)] + own(pre) + [(xhi, 2)],
        [(xlo, 3)] + own(inp) + [(xhi, 3)],
    )


def ypack_kernel(grad, pre, inp, xfar, xnear, far, near, held):
    wide, acts, inputs = fields_of(grad, pre, inp, *below_above("gx", xfar, xnear))
    for at, (ref, x) in enumerate(wide):
        value = ref[x].astype(F32)
        far[at], near[at] = far_near("gy", value[0:2], value[SY - 2 : SY])
    for at, ((a, ax), (i, ix)) in enumerate(zip(acts, inputs)):
        v, w = a[ax].astype(F32), i[ix].astype(F32)
        held[0:1], held[1:2] = v[0:1], w[0:1]
        held[2:3], held[3:4] = v[SY - 1 :], w[SY - 1 :]
        far[8 + at], near[8 + at] = far_near("gy", held[0:2], held[2:4])


def zpack_kernel(grad, pre, inp, xfar, xnear, yfar, ynear, far, near, low, high):
    wide, acts, inputs = fields_of(grad, pre, inp, *below_above("gx", xfar, xnear))
    ylo, yhi = below_above("gy", yfar, ynear)
    for held, lane, half in ((low, 0, True), (high, LANES - 128, False)):
        held[...] = jnp.zeros_like(held)
        cut = slice(lane, lane + 128)
        for at, (ref, x) in enumerate(wide):
            row = 12 * at
            held[row : row + 2] = ylo[at, :, cut].astype(F32)
            held[row + 2 : row + 10] = ref[x, :, cut].astype(F32)
            held[row + 10 : row + 12] = yhi[at, :, cut].astype(F32)
        for j, ((a, ax), (i, ix)) in enumerate(zip(acts, inputs)):
            row = 12 * (8 + j)
            below, above = ylo[8 + j, :, cut].astype(F32), yhi[8 + j, :, cut].astype(F32)
            v, w = a[ax, :, cut].astype(F32), i[ix, :, cut].astype(F32)

            def joined(first, second):
                if half:
                    second = pltpu.roll(second, 64, 1)
                else:
                    first = pltpu.roll(first, 64, 1)
                return jnp.where(low_half(first.shape), first, second)

            held[row + 2 : row + 10] = joined(v, w)
            for at, pair in ((row + 1, below), (row + 10, above)):
                first, second = jnp.broadcast_to(pair[0:1], (8, 128)), jnp.broadcast_to(pair[1:2], (8, 128))
                held[at : at + 1] = joined(first, second)[0:1]
    far[...], near[...] = far_near("gz", low[...], high[...])


def bands_kernel(weights, one, two, flat, turned):
    count, rows = weights.shape[0], weights.shape[1] // 2
    block = lax.broadcasted_iota(jnp.int32, (CH, 128), 1) // CH
    for which, out in enumerate((one, two)):
        flat[...] = jnp.zeros_like(flat)
        for g in range(count):
            value = weights[g].astype(F32)[which * rows : (which + 1) * rows]
            flat[g * rows : (g + 1) * rows, 256 : 256 + 27 * CH] = value
        turned[...] = pltpu.roll(flat[...], flat.shape[1] - 64, 1)
        for m in range(9):
            for a in range(4):
                at = 4 + 3 * m + 2 - a
                source = turned if at % 2 else flat
                lane = at // 2 * 128
                valid = (block + 2 - a >= 0) & (block - a <= 0)
                value = jnp.where(valid, source[:, lane : lane + 128], 0.0)
                out[m * BAND + a * CH : m * BAND + (a + 1) * CH, :] = value.astype(B16)


def fill_wide(field, layers, ylo, yhi, zlo, zhi):
    field[...] = jnp.zeros_like(field)
    for at, (ref, x) in enumerate(layers):
        row = 16 * (at + 1)
        field[row : row + 8, 128 : 128 + LANES] = ref[x].astype(F32)
        field[row - 2 : row, 128 : 128 + LANES] = ylo[at].astype(F32)
        field[row + 8 : row + 10, 128 : 128 + LANES] = yhi[at].astype(F32)
        for side, lane in ((zlo, 0), (zhi, 128 + LANES)):
            field[row - 2 : row + 10, lane : lane + 128] = side[12 * at : 12 * at + 12]


def fill_thin(field, layers, second, ylo, yhi, zlo, zhi):
    field[...] = jnp.zeros_like(field)
    for j, (ref, x) in enumerate(layers):
        at, row = 8 + j, 16 * (j + 2)
        field[row : row + 8, 128 : 128 + LANES] = ref[x].astype(F32)
        field[row - 1 : row, 128 : 128 + LANES] = ylo[at].astype(F32)[second : second + 1]
        field[row + 8 : row + 9, 128 : 128 + LANES] = yhi[at].astype(F32)[second : second + 1]
        for side, lane, upper in ((zlo, 0, True), (zhi, 128 + LANES, False)):
            value = side[12 * at : 12 * at + 12]
            if upper != bool(second):
                value = pltpu.roll(value, 64, 1)
            value = jnp.where(low_half(value.shape) != upper, value, 0.0)
            field[row - 1 : row, lane : lane + 128] = value[1:2]
            field[row : row + 8, lane : lane + 128] = value[2:10]
            field[row + 8 : row + 9, lane : lane + 128] = value[10:11]


def spread(moved, evens, odds, sign, layers):
    for i, dy in enumerate((-1, 0, 1)):
        by = (-sign * dy) % ROWS
        value = pltpu.roll(moved, by, 0) if by else moved
        tiles = [value[16 * (x + 1) : 16 * (x + 1) + 8] for x in layers]
        evens[i, 0 : 8 * len(tiles)] = jnp.concatenate(tiles, 0).astype(B16)
        odds[i, 0 : 8 * len(tiles) - 16] = jnp.concatenate(tiles[1:-1], 0).astype(B16)


def stepped(evens, odds, dy, dx, rows, lane):
    ref, row = (odds, 0) if dx == 0 else (evens, 8 + 8 * dx)
    return ref[dy, row : row + rows, lane : lane + BAND]


def own_columns(evens, odds, columns, sign):
    for m in range(9):
        for h in range(OWN_GROUPS):
            columns[OWN_ROWS * h : OWN_ROWS * (h + 1), BAND * m : BAND * (m + 1)] = stepped(
                evens, odds, m % 3, sign * (m // 3 - 1), OWN_ROWS, 128 * h + 128
            )


def edge_rows(count):
    row = lax.broadcasted_iota(jnp.int32, (16 * count, ROWS), 0)
    column = lax.broadcasted_iota(jnp.int32, (16 * count, ROWS), 1)
    m, x = row // 16 + (4 if count == 1 else 0), row % 8
    source = 16 * (x - m // 3 + 2) + jnp.where(row % 16 < 8, -1, 8) - m % 3 + 1
    return jnp.where(column == source, 1.0, 0.0).astype(B16)


def slope(v):
    g = jax.nn.sigmoid(v)
    return g * (1.0 + v * (1.0 - g))


def main_kernel(scale, grad, pre, inp, xfar, xnear, yfar, ynear, zfar, znear, band,
                kept, sent, pre_out, fg, fa, fi, moved, picked, evens, odds, columns, many, left, left_f, grads_one, grads_two, held, zlo, zhi):
    wide, acts, inputs = fields_of(grad, pre, inp, *below_above("gx", xfar, xnear))
    ylo, yhi = below_above("gy", yfar, ynear)
    below, above = below_above("gz", zfar, znear)
    zlo[...] = below[...]
    zhi[...] = above[...]
    halos = (ylo, yhi, zlo, zhi)
    fill_wide(fg, wide, *halos)
    fill_thin(fa, acts, 0, *halos)
    fill_thin(fi, inputs, 1, *halos)
    contract = (((0,), (0,)), ((), ()))

    v = fa[...]
    act = (v * jax.nn.sigmoid(v)).astype(B16).astype(F32)
    spread(pltpu.roll(act, 64, 1), evens, odds, 1, range(1, SX + 3))
    own_columns(evens, odds, columns, 1)
    for h in range(OWN_GROUPS):
        for x in range(SX):
            row = OWN_ROWS * h + 8 * x
            left_f[row : row + 8, :] = grad[x, :, 128 * h : 128 * (h + 1)].astype(F32)
    left[...] = left_f[...].astype(B16)
    grads_two[...] = lax.dot_general(left[...], columns[...], contract, preferred_element_type=F32)

    moved[...] = pltpu.roll(fg[...], 64, 1)
    spread(moved[...], evens, odds, -1, range(SX + 4))
    for m in range(9):
        dx, dy = m // 3 - 1, m % 3
        for h in range(HALO_GROUPS):
            many[HALO_ROWS * h : HALO_ROWS * (h + 1), BAND * m : BAND * (m + 1)] = stepped(
                evens, odds, dy, -dx, HALO_ROWS, 128 * h
            )
    picked[...] = jnp.dot(edge_rows(9), moved[...].astype(B16), preferred_element_type=F32).astype(B16)
    for m in range(9):
        for h in range(HALO_GROUPS):
            row = EDGES + 16 * h
            many[row : row + 16, BAND * m : BAND * (m + 1)] = picked[
                16 * m : 16 * (m + 1), 128 * h : 128 * h + BAND
            ]
    held[...] = jnp.dot(many[...], band[...], preferred_element_type=F32)
    fg[:, 128 * HALO_GROUPS :] = jnp.zeros((ROWS, WIDE - 128 * HALO_GROUPS), F32)
    place = edge_rows(1)
    beside = slope(jnp.dot(place, fa[:, : 128 * HALO_GROUPS].astype(B16), preferred_element_type=F32))
    ends = jnp.concatenate(
        [held[EDGES + 16 * h : EDGES + 16 * (h + 1), :] for h in range(HALO_GROUPS)], 1
    )
    value = (ends * beside).astype(B16)
    fg[:, : 128 * HALO_GROUPS] = lax.dot_general(place, value, contract, preferred_element_type=F32)
    for h in range(HALO_GROUPS):
        lanes = slice(128 * h, 128 * (h + 1))
        for x in range(1, SX + 3):
            row, at = HALO_ROWS * h + 8 * (x - 1), slice(16 * (x + 1), 16 * (x + 1) + 8)
            value = held[row : row + 8, :] * slope(fa[at, lanes])
            fg[at, lanes] = value.astype(B16).astype(F32)
    pre_out[...] = pltpu.roll(fg[...], 64, 1).astype(B16)

    spread(pltpu.roll(fi[...], 64, 1), evens, odds, 1, range(1, SX + 3))
    own_columns(evens, odds, columns, 1)
    for h in range(OWN_GROUPS):
        for x in range(SX):
            row, at = OWN_ROWS * h + 8 * x, 16 * (x + 3)
            left_f[row : row + 8, :] = fg[at : at + 8, 128 * h + 128 : 128 * h + 256]
    left[...] = left_f[...].astype(B16)
    grads_one[...] = lax.dot_general(left[...], columns[...], contract, preferred_element_type=F32)

    count, rows = kept.shape[0], kept.shape[1]
    even = lax.rem(lax.axis_index("gz"), 2) == 0

    def block(source, k):
        m, t = k // 3, k % 3
        pieces = []
        for b in ((k + t) % 2, (k + t + 1) % 2):
            lane = (4 * m + b + t) // 2 * 128
            pieces.append(source[64 * b : 64 * (b + 1), lane : lane + 128])
        return pieces[0] + pltpu.roll(pieces[1], 64, 1)

    for j in range(14):
        pair = []
        for source in (grads_one, grads_two):
            value = block(source, 2 * j)
            if j < 13:
                value = jnp.where(low_half(value.shape), value, block(source, 2 * j + 1))
            pair.append(value * scale)
        width = 128 if j < 13 else 64
        keep = jnp.where(even, pair[0], pair[1])[:, :width]
        send = jnp.where(even, pair[1], pair[0])[:, :width]
        for g in range(count):
            kept[g, :, 128 * j : 128 * j + width] = keep[g * rows : (g + 1) * rows, :]
            sent[g, :, 128 * j : 128 * j + width] = send[g * rows : (g + 1) * rows, :].astype(B16)


def last_kernel(pre_grad, grad, band, out, evens, odds, columns, held):
    spread(pre_grad[...].astype(F32), evens, odds, -1, range(1, SX + 3))
    own_columns(evens, odds, columns, -1)
    held[...] = jnp.dot(columns[...], band[...], preferred_element_type=F32)
    for h in range(OWN_GROUPS):
        for x in range(SX):
            row, lanes = OWN_ROWS * h + 8 * x, slice(128 * h, 128 * (h + 1))
            out[x, :, lanes] = (held[row : row + 8, :] + grad[x, :, lanes].astype(F32)).astype(B16)


def swapped(far, near, axis):
    count = lax.axis_size(axis)
    steps = [1 if i % 2 else -1 for i in range(count)]
    return (
        lax.ppermute(far, axis, [(i, (i + step) % count) for i, step in enumerate(steps)]),
        lax.ppermute(near, axis, [(i, i - step) for i, step in enumerate(steps)]),
    )


def total_kernel(parts, out):
    value = parts[0].astype(F32)
    for i in range(1, parts.shape[0]):
        value += parts[i].astype(F32)
    value = value.astype(out.dtype)
    if out.ndim == value.ndim:
        out[...] = value
    else:
        for i in range(out.shape[0]):
            out[i] = value


def pair_kernel(kept, came, out):
    out[...] = (kept[...] + came[...].astype(F32)).astype(B16)


def last_total_kernel(parts, one, two):
    first, second = parts[0], parts[1]
    for i in range(2, parts.shape[0], 2):
        first += parts[i]
        second += parts[i + 1]
    one[...] = first
    two[...] = second


def reduced(kept, sent, other):
    rows, columns = kept.shape[1:]
    gy, gz = lax.axis_size("gy"), lax.axis_size("gz")
    came = lax.ppermute(sent, "gz", [(i, i + 1 - 2 * (i % 2)) for i in range(gz)])
    came, other = lax.optimization_barrier((came, other))
    (slots,) = call(pair_kernel, [(kept.shape, B16)], [], 1000, 500000, kept, came)
    parts = lax.all_to_all(slots, "gx", 0, 0, tiled=True)
    (copies,) = call(total_kernel, [((gy, rows, columns), B16)], [], 1000, 500000, parts)
    parts = lax.all_to_all(copies, "gy", 0, 0, tiled=True)
    (copies,) = call(total_kernel, [((gz, rows, columns), F32)], [], 1000, 500000, parts)
    parts = lax.all_to_all(copies, "gz", 0, 0, tiled=True)
    grads = ((rows, columns), F32)
    one, two = call(last_total_kernel, [grads, grads], [], 1000, 500000, parts)
    return other, one, two


def body(block_input, pre_act, skip_grad, pool_grad, conv1_weight, conv2_weight):
    count = lax.axis_size("gx")
    rows = CH // count
    cells = SX * SY * SZ * count * lax.axis_size("gy") * lax.axis_size("gz")
    block, message = ((SX, SY, LANES), B16), ((4, SY, LANES), B16)
    weight = ((rows, 27 * CH), B16)
    grad, pre, inp, far, near, copies = call(
        prep_kernel,
        [block, block, block, message, message, ((count, 2 * rows, 27 * CH), B16)],
        [
            block, ((SX // 2, SY // 2, LANES // 2), B16), weight, weight,
            ((SX // 2, SY, LANES), F32), ((2 * rows, 27 * CH), F32), pltpu.SemaphoreType.DMA((6,)),
        ],
        100000, 400000,
        *(
            pltpu.with_memory_space_constraint(array, pltpu.HBM)
            for array in (skip_grad, pool_grad, pre_act, block_input, conv1_weight, conv2_weight)
        ),
        space=pltpu.HBM,
    )
    xfar, xnear = swapped(far, near, "gx")
    fields = (grad, pre, inp, xfar, xnear)
    message = ((LAYERS, 2, LANES), B16)
    yfar, ynear = swapped(
        *call(ypack_kernel, [message, message], [((4, LANES), F32)], 60000000000, 600000, *fields), "gy"
    )
    side = ((12 * LAYERS, 128), F32)
    gathered = lax.all_to_all(copies, "gx", 0, 0, tiled=True)
    message = ((12 * LAYERS, 128), B16)
    zfar, znear = swapped(
        *call(zpack_kernel, [message, message], [side, side], 100000, 700000, *fields, yfar, ynear), "gz"
    )
    matrix = ((DEPTH, 128), B16)
    flat = ((CH, 36 * CH), F32)
    band_one, band_two = call(bands_kernel, [matrix, matrix], [flat, flat], 1000000, 4000000, gathered)
    field = ((ROWS, WIDE), F32)
    evens, odds = ((3, 8 * (SX + 4), WIDE), B16), ((3, 8 * (SX + 2), WIDE), B16)
    columns = ((OWN_GROUPS * OWN_ROWS, DEPTH), B16)
    kept, sent, pre_grad = call(
        functools.partial(main_kernel, 1.0 / math.sqrt(cells)),
        [((count, rows, 27 * CH), F32), ((count, rows, 27 * CH), B16), ((ROWS, WIDE), B16)],
        [
            field, field, field, field, ((ROWS, WIDE), B16), evens, odds, columns,
            ((MANY, DEPTH), B16), ((OWN_GROUPS * OWN_ROWS, 128), B16), ((OWN_GROUPS * OWN_ROWS, 128), F32),
            ((128, DEPTH), F32), ((128, DEPTH), F32), ((MANY, 128), F32), side, side,
        ],
        2 * 900 * 1000 * 1000, 8000000,
        *fields, yfar, ynear, zfar, znear, band_two,
        grant=32,
    )
    (input_grad,) = call(
        last_kernel,
        [((SX, SY, LANES), B16)],
        [evens, odds, columns, ((OWN_GROUPS * OWN_ROWS, 128), F32)],
        500000000, 4000000,
        pre_grad, grad, band_one,
    )
    return reduced(kept, sent, input_grad)


def solution(mesh):
    in_specs = (
        P("gx", "gy", "gz"),
        P("gx", "gy", "gz"),
        P("gx", "gy", "gz"),
        P("gx", "gy", "gz"),
        P("gx", None),
        P("gx", None),
    )
    out_specs = (P("gx", "gy", "gz"), P("gx", None), P("gx", None))
    return jax.shard_map(body, mesh=mesh, in_specs=in_specs, out_specs=out_specs, check_vma=False)
```

```python
import functools
import math

import jax
import jax.numpy as jnp
from jax import lax
from jax.experimental import pallas as pl
from jax.experimental.pallas import tpu as pltpu
from jax.sharding import PartitionSpec as P

F32, B16 = jnp.float32, jnp.bfloat16
SX, SY, SZ, CH = 4, 8, 16, 64
LANES = SZ * CH
ROWS = 16 * (SX + 5)
WIDE = LANES + 6 * CH
BAND = 4 * CH
OWN_GROUPS, HALO_GROUPS = SZ // 2, SZ // 2 + 2
DEPTH = 9 * BAND
OWN_ROWS = 8 * SX
HALO_ROWS = 8 * (SX + 2)
EDGES = HALO_GROUPS * HALO_ROWS
MANY = EDGES + HALO_GROUPS * 16
LAYERS = 14


def call(kernel, outs, scratch, flops, moved, *args, space=pltpu.VMEM, grant=12):
    return pl.pallas_call(
        kernel,
        out_shape=[jax.ShapeDtypeStruct(shape, dtype) for shape, dtype in outs],
        in_specs=[pl.BlockSpec(memory_space=space)] * len(args),
        out_specs=[pl.BlockSpec(memory_space=pltpu.VMEM)] * len(outs),
        scratch_shapes=[pltpu.VMEM(*held) if isinstance(held, tuple) else held for held in scratch],
        compiler_params=pltpu.CompilerParams(vmem_limit_bytes=grant * 1024 * 1024),
        cost_estimate=pl.CostEstimate(flops=flops, bytes_accessed=moved, transcendentals=0),
    )(*args)


def low_half(shape):
    return lax.broadcasted_iota(jnp.int32, shape, len(shape) - 1) % 128 < 64


class Either:
    def __init__(self, axis, if_odd, if_even):
        self.odd = lax.rem(lax.axis_index(axis), 2) == 1
        self.refs = if_odd, if_even

    def __getitem__(self, at):
        first, second = (ref[at].astype(F32) for ref in self.refs)
        return jnp.where(self.odd, first, second)


def below_above(axis, far, near):
    return Either(axis, near, far), Either(axis, far, near)


def far_near(axis, low, high):
    odd = lax.rem(lax.axis_index(axis), 2) == 1
    return jnp.where(odd, high, low).astype(B16), jnp.where(odd, low, high).astype(B16)


def prep_kernel(skip_in, pool_in, pre_in, inp_in, one_in, two_in,
                grad, pre, inp, far, near, copies, skip, pool, one, two, up, rows, sems):
    moves = [
        pltpu.make_async_copy(source, target, sems.at[i])
        for i, (source, target) in enumerate(
            ((skip_in, skip), (pool_in, pool), (pre_in, pre), (inp_in, inp), (one_in, one), (two_in, two))
        )
    ]
    for move in moves:
        move.start()
    for move in moves:
        move.wait()
    each = one.shape[0]
    rows[0:each], rows[each : 2 * each] = one[...].astype(F32), two[...].astype(F32)
    both = rows[...].astype(B16)
    for g in range(copies.shape[0]):
        copies[g] = both
    for px in range(SX // 2):
        pieces = []
        for j in range(LANES // 256):
            v = pool[px, :, 128 * j : 128 * (j + 1)].astype(F32)
            turned = pltpu.roll(v, 64, 1)
            first = low_half(v.shape)
            pieces += [jnp.where(first, v, turned), jnp.where(first, turned, v)]
        for y in range(SY):
            for j, piece in enumerate(pieces):
                up[px, y : y + 1, 128 * j : 128 * (j + 1)] = piece[y // 2 : y // 2 + 1, :]
    for x in range(SX):
        value = (skip[x].astype(F32) + 0.125 * up[x // 2]).astype(B16)
        grad[x] = value
    ends = ((grad, 0, 2), (grad, 1, 3), (pre, 0, SX - 1), (inp, 0, SX - 1))
    for at, (ref, bottom, top) in enumerate(ends):
        far[at], near[at] = far_near("gx", ref[bottom].astype(F32), ref[top].astype(F32))


def fields_of(grad, pre, inp, xlo, xhi):
    def own(ref):
        return [(ref, x) for x in range(SX)]

    return (
        [(xlo, 0), (xlo, 1)] + own(grad) + [(xhi, 0), (xhi, 1)],
        [(xlo, 2)] + own(pre) + [(xhi, 2)],
        [(xlo, 3)] + own(inp) + [(xhi, 3)],
    )


def ypack_kernel(grad, pre, inp, xnear, xfar, far, near, held):
    wide, acts, inputs = fields_of(grad, pre, inp, *below_above("gx", xfar, xnear))
    for at, (ref, x) in enumerate(wide):
        value = ref[x].astype(F32)
        far[at], near[at] = far_near("gy", value[0:2], value[SY - 2 : SY])
    for at, ((a, ax), (i, ix)) in enumerate(zip(acts, inputs)):
        v, w = a[ax].astype(F32), i[ix].astype(F32)
        held[0:1], held[1:2] = v[0:1], w[0:1]
        held[2:3], held[3:4] = v[SY - 1 :], w[SY - 1 :]
        far[8 + at], near[8 + at] = far_near("gy", held[0:2], held[2:4])


def zpack_kernel(grad, pre, inp, xnear, xfar, yfar, ynear, far, near, low, high):
    wide, acts, inputs = fields_of(grad, pre, inp, *below_above("gx", xfar, xnear))
    ylo, yhi = below_above("gy", yfar, ynear)
    for held, lane, half in ((low, 0, True), (high, LANES - 128, False)):
        held[...] = jnp.zeros_like(held)
        cut = slice(lane, lane + 128)
        for at, (ref, x) in enumerate(wide):
            row = 12 * at
            held[row : row + 2] = ylo[at, :, cut].astype(F32)
            held[row + 2 : row + 10] = ref[x, :, cut].astype(F32)
            held[row + 10 : row + 12] = yhi[at, :, cut].astype(F32)
        for j, ((a, ax), (i, ix)) in enumerate(zip(acts, inputs)):
            row = 12 * (8 + j)
            below, above = ylo[8 + j, :, cut].astype(F32), yhi[8 + j, :, cut].astype(F32)
            v, w = a[ax, :, cut].astype(F32), i[ix, :, cut].astype(F32)

            def joined(first, second):
                if half:
                    second = pltpu.roll(second, 64, 1)
                else:
                    first = pltpu.roll(first, 64, 1)
                return jnp.where(low_half(first.shape), first, second)

            held[row + 2 : row + 10] = joined(v, w)
            for at, pair in ((row + 1, below), (row + 10, above)):
                first, second = jnp.broadcast_to(pair[0:1], (8, 128)), jnp.broadcast_to(pair[1:2], (8, 128))
                held[at : at + 1] = joined(first, second)[0:1]
    far[...], near[...] = far_near("gz", low[...], high[...])


def bands_kernel(weights, one, two, flat, turned):
    count, rows = weights.shape[0], weights.shape[1] // 2
    block = lax.broadcasted_iota(jnp.int32, (CH, 128), 1) // CH
    for which, out in enumerate((one, two)):
        flat[...] = jnp.zeros_like(flat)
        for g in range(count):
            value = weights[g].astype(F32)[which * rows : (which + 1) * rows]
            flat[g * rows : (g + 1) * rows, 256 : 256 + 27 * CH] = value
        turned[...] = pltpu.roll(flat[...], flat.shape[1] - 64, 1)
        for m in range(9):
            for a in range(4):
                at = 4 + 3 * m + 2 - a
                source = turned if at % 2 else flat
                lane = at // 2 * 128
                valid = (block + 2 - a >= 0) & (block - a <= 0)
                value = jnp.where(valid, source[:, lane : lane + 128], 0.0)
                out[m * BAND + a * CH : m * BAND + (a + 1) * CH, :] = value.astype(B16)


def fill_wide(field, layers, ylo, yhi, zlo, zhi):
    field[...] = jnp.zeros_like(field)
    for at, (ref, x) in enumerate(layers):
        row = 16 * (at + 1)
        field[row : row + 8, 128 : 128 + LANES] = ref[x].astype(F32)
        field[row - 2 : row, 128 : 128 + LANES] = ylo[at].astype(F32)
        field[row + 8 : row + 10, 128 : 128 + LANES] = yhi[at].astype(F32)
        for side, lane in ((zlo, 0), (zhi, 128 + LANES)):
            field[row - 2 : row + 10, lane : lane + 128] = side[12 * at : 12 * at + 12]


def fill_thin(field, layers, second, ylo, yhi, zlo, zhi):
    field[...] = jnp.zeros_like(field)
    for j, (ref, x) in enumerate(layers):
        at, row = 8 + j, 16 * (j + 2)
        field[row : row + 8, 128 : 128 + LANES] = ref[x].astype(F32)
        field[row - 1 : row, 128 : 128 + LANES] = ylo[at].astype(F32)[second : second + 1]
        field[row + 8 : row + 9, 128 : 128 + LANES] = yhi[at].astype(F32)[second : second + 1]
        for side, lane, upper in ((zlo, 0, True), (zhi, 128 + LANES, False)):
            value = side[12 * at : 12 * at + 12]
            if upper != bool(second):
                value = pltpu.roll(value, 64, 1)
            value = jnp.where(low_half(value.shape) != upper, value, 0.0)
            field[row - 1 : row, lane : lane + 128] = value[1:2]
            field[row : row + 8, lane : lane + 128] = value[2:10]
            field[row + 8 : row + 9, lane : lane + 128] = value[10:11]


def spread(moved, evens, odds, sign, layers):
    for i, dy in enumerate((-1, 0, 1)):
        by = (-sign * dy) % ROWS
        value = pltpu.roll(moved, by, 0) if by else moved
        tiles = [value[16 * (x + 1) : 16 * (x + 1) + 8] for x in layers]
        evens[i, 0 : 8 * len(tiles)] = jnp.concatenate(tiles, 0).astype(B16)
        odds[i, 0 : 8 * len(tiles) - 16] = jnp.concatenate(tiles[1:-1], 0).astype(B16)


def stepped(evens, odds, dy, dx, rows, lane):
    ref, row = (odds, 0) if dx == 0 else (evens, 8 + 8 * dx)
    return ref[dy, row : row + rows, lane : lane + BAND]


def own_columns(evens, odds, columns, sign):
    for m in range(9):
        for h in range(OWN_GROUPS):
            columns[OWN_ROWS * h : OWN_ROWS * (h + 1), BAND * m : BAND * (m + 1)] = stepped(
                evens, odds, m % 3, sign * (m // 3 - 1), OWN_ROWS, 128 * h + 128
            )


def edge_rows(count):
    row = lax.broadcasted_iota(jnp.int32, (16 * count, ROWS), 0)
    column = lax.broadcasted_iota(jnp.int32, (16 * count, ROWS), 1)
    m, x = row // 16 + (4 if count == 1 else 0), row % 8
    source = 16 * (x - m // 3 + 2) + jnp.where(row % 16 < 8, -1, 8) - m % 3 + 1
    return jnp.where(column == source, 1.0, 0.0).astype(B16)


def slope(v):
    g = jax.nn.sigmoid(v)
    return g * (1.0 + v * (1.0 - g))


def main_kernel(scale, grad, pre, inp, xnear, xfar, yfar, ynear, zfar, znear, band,
                kept, sent, pre_out, fg, fa, fi, moved, picked, evens, odds, columns, many, left, left_f, grads_one, grads_two, held, zlo, zhi):
    wide, acts, inputs = fields_of(grad, pre, inp, *below_above("gx", xfar, xnear))
    ylo, yhi = below_above("gy", yfar, ynear)
    below, above = below_above("gz", zfar, znear)
    zlo[...] = below[...]
    zhi[...] = above[...]
    halos = (ylo, yhi, zlo, zhi)
    fill_wide(fg, wide, *halos)
    fill_thin(fa, acts, 0, *halos)
    fill_thin(fi, inputs, 1, *halos)
    contract = (((0,), (0,)), ((), ()))

    v = fa[...]
    act = (v * jax.nn.sigmoid(v)).astype(B16).astype(F32)
    spread(pltpu.roll(act, 64, 1), evens, odds, 1, range(1, SX + 3))
    own_columns(evens, odds, columns, 1)
    for h in range(OWN_GROUPS):
        for x in range(SX):
            row = OWN_ROWS * h + 8 * x
            left_f[row : row + 8, :] = grad[x, :, 128 * h : 128 * (h + 1)].astype(F32)
    left[...] = left_f[...].astype(B16)
    grads_two[...] = lax.dot_general(left[...], columns[...], contract, preferred_element_type=F32)

    moved[...] = pltpu.roll(fg[...], 64, 1)
    spread(moved[...], evens, odds, -1, range(SX + 4))
    for m in range(9):
        dx, dy = m // 3 - 1, m % 3
        for h in range(HALO_GROUPS):
            many[HALO_ROWS * h : HALO_ROWS * (h + 1), BAND * m : BAND * (m + 1)] = stepped(
                evens, odds, dy, -dx, HALO_ROWS, 128 * h
            )
    picked[...] = jnp.dot(edge_rows(9), moved[...].astype(B16), preferred_element_type=F32).astype(B16)
    for m in range(9):
        for h in range(HALO_GROUPS):
            row = EDGES + 16 * h
            many[row : row + 16, BAND * m : BAND * (m + 1)] = picked[
                16 * m : 16 * (m + 1), 128 * h : 128 * h + BAND
            ]
    held[...] = jnp.dot(many[...], band[...], preferred_element_type=F32)
    fg[:, 128 * HALO_GROUPS :] = jnp.zeros((ROWS, WIDE - 128 * HALO_GROUPS), F32)
    place = edge_rows(1)
    beside = slope(jnp.dot(place, fa[:, : 128 * HALO_GROUPS].astype(B16), preferred_element_type=F32))
    ends = jnp.concatenate(
        [held[EDGES + 16 * h : EDGES + 16 * (h + 1), :] for h in range(HALO_GROUPS)], 1
    )
    value = (ends * beside).astype(B16)
    fg[:, : 128 * HALO_GROUPS] = lax.dot_general(place, value, contract, preferred_element_type=F32)
    for h in range(HALO_GROUPS):
        lanes = slice(128 * h, 128 * (h + 1))
        for x in range(1, SX + 3):
            row, at = HALO_ROWS * h + 8 * (x - 1), slice(16 * (x + 1), 16 * (x + 1) + 8)
            value = held[row : row + 8, :] * slope(fa[at, lanes])
            fg[at, lanes] = value.astype(B16).astype(F32)
    pre_out[...] = pltpu.roll(fg[...], 64, 1).astype(B16)

    spread(pltpu.roll(fi[...], 64, 1), evens, odds, 1, range(1, SX + 3))
    own_columns(evens, odds, columns, 1)
    for h in range(OWN_GROUPS):
        for x in range(SX):
            row, at = OWN_ROWS * h + 8 * x, 16 * (x + 3)
            left_f[row : row + 8, :] = fg[at : at + 8, 128 * h + 128 : 128 * h + 256]
    left[...] = left_f[...].astype(B16)
    grads_one[...] = lax.dot_general(left[...], columns[...], contract, preferred_element_type=F32)

    count, rows = kept.shape[0], kept.shape[1]
    even = lax.rem(lax.axis_index("gz"), 2) == 0

    def block(source, k):
        m, t = k // 3, k % 3
        pieces = []
        for b in ((k + t) % 2, (k + t + 1) % 2):
            lane = (4 * m + b + t) // 2 * 128
            pieces.append(source[64 * b : 64 * (b + 1), lane : lane + 128])
        return pieces[0] + pltpu.roll(pieces[1], 64, 1)

    for j in range(14):
        pair = []
        for source in (grads_one, grads_two):
            value = block(source, 2 * j)
            if j < 13:
                value = jnp.where(low_half(value.shape), value, block(source, 2 * j + 1))
            pair.append(value * scale)
        width = 128 if j < 13 else 64
        keep = jnp.where(even, pair[0], pair[1])[:, :width]
        send = jnp.where(even, pair[1], pair[0])[:, :width]
        for g in range(count):
            kept[g, :, 128 * j : 128 * j + width] = keep[g * rows : (g + 1) * rows, :]
            sent[g, :, 128 * j : 128 * j + width] = send[g * rows : (g + 1) * rows, :].astype(B16)


def last_kernel(pre_grad, grad, band, out, evens, odds, columns, held):
    spread(pre_grad[...].astype(F32), evens, odds, -1, range(1, SX + 3))
    own_columns(evens, odds, columns, -1)
    held[...] = jnp.dot(columns[...], band[...], preferred_element_type=F32)
    for h in range(OWN_GROUPS):
        for x in range(SX):
            row, lanes = OWN_ROWS * h + 8 * x, slice(128 * h, 128 * (h + 1))
            out[x, :, lanes] = (held[row : row + 8, :] + grad[x, :, lanes].astype(F32)).astype(B16)


def swapped(far, near, axis):
    count = lax.axis_size(axis)
    steps = [1 if i % 2 else -1 for i in range(count)]
    return (
        lax.ppermute(far, axis, [(i, (i + step) % count) for i, step in enumerate(steps)]),
        lax.ppermute(near, axis, [(i, i - step) for i, step in enumerate(steps)]),
    )


def total_kernel(parts, out):
    value = parts[0].astype(F32)
    for i in range(1, parts.shape[0]):
        value += parts[i].astype(F32)
    value = value.astype(out.dtype)
    if out.ndim == value.ndim:
        out[...] = value
    else:
        for i in range(out.shape[0]):
            out[i] = value


def pair_kernel(kept, came, out):
    out[...] = (kept[...] + came[...].astype(F32)).astype(B16)


def last_total_kernel(parts, one, two):
    first, second = parts[0], parts[1]
    for i in range(2, parts.shape[0], 2):
        first += parts[i]
        second += parts[i + 1]
    one[...] = first
    two[...] = second


def reduced(kept, sent, other):
    rows, columns = kept.shape[1:]
    gy, gz = lax.axis_size("gy"), lax.axis_size("gz")
    came = lax.ppermute(sent, "gz", [(i, i + 1 - 2 * (i % 2)) for i in range(gz)])
    came, other = lax.optimization_barrier((came, other))
    (slots,) = call(pair_kernel, [(kept.shape, B16)], [], 1000, 500000, kept, came)
    parts = lax.all_to_all(slots, "gx", 0, 0, tiled=True)
    (copies,) = call(total_kernel, [((gy, rows, columns), B16)], [], 1000, 500000, parts)
    parts = lax.all_to_all(copies, "gy", 0, 0, tiled=True)
    (part,) = call(total_kernel, [((rows, columns), F32)], [], 1000, 500000, parts)
    parts = lax.all_gather(part, "gz", axis=0)
    grads = ((rows, columns), F32)
    one, two = call(last_total_kernel, [grads, grads], [], 1000, 500000, parts)
    return other, one, two


def body(block_input, pre_act, skip_grad, pool_grad, conv1_weight, conv2_weight):
    count = lax.axis_size("gx")
    rows = CH // count
    cells = SX * SY * SZ * count * lax.axis_size("gy") * lax.axis_size("gz")
    block, message = ((SX, SY, LANES), B16), ((4, SY, LANES), B16)
    weight = ((rows, 27 * CH), B16)
    grad, pre, inp, far, near, copies = call(
        prep_kernel,
        [block, block, block, message, message, ((count, 2 * rows, 27 * CH), B16)],
        [
            block, ((SX // 2, SY // 2, LANES // 2), B16), weight, weight,
            ((SX // 2, SY, LANES), F32), ((2 * rows, 27 * CH), F32), pltpu.SemaphoreType.DMA((6,)),
        ],
        100000, 400000,
        *(
            pltpu.with_memory_space_constraint(array, pltpu.HBM)
            for array in (skip_grad, pool_grad, pre_act, block_input, conv1_weight, conv2_weight)
        ),
        space=pltpu.HBM,
    )
    xfar, xnear = swapped(far, near, "gx")
    fields = (grad, pre, inp, xnear, xfar)
    message = ((LAYERS, 2, LANES), B16)
    yfar, ynear = swapped(
        *call(ypack_kernel, [message, message], [((4, LANES), F32)], 60000000000, 600000, *fields), "gy"
    )
    side = ((12 * LAYERS, 128), F32)
    gathered = lax.all_to_all(copies, "gx", 0, 0, tiled=True)
    message = ((12 * LAYERS, 128), B16)
    zfar, znear = swapped(
        *call(zpack_kernel, [message, message], [side, side], 100000, 700000, *fields, yfar, ynear), "gz"
    )
    matrix = ((DEPTH, 128), B16)
    flat = ((CH, 36 * CH), F32)
    band_one, band_two = call(bands_kernel, [matrix, matrix], [flat, flat], 1000000, 4000000, gathered)
    field = ((ROWS, WIDE), F32)
    evens, odds = ((3, 8 * (SX + 4), WIDE), B16), ((3, 8 * (SX + 2), WIDE), B16)
    columns = ((OWN_GROUPS * OWN_ROWS, DEPTH), B16)
    kept, sent, pre_grad = call(
        functools.partial(main_kernel, 1.0 / math.sqrt(cells)),
        [((count, rows, 27 * CH), F32), ((count, rows, 27 * CH), B16), ((ROWS, WIDE), B16)],
        [
            field, field, field, field, ((ROWS, WIDE), B16), evens, odds, columns,
            ((MANY, DEPTH), B16), ((OWN_GROUPS * OWN_ROWS, 128), B16), ((OWN_GROUPS * OWN_ROWS, 128), F32),
            ((128, DEPTH), F32), ((128, DEPTH), F32), ((MANY, 128), F32), side, side,
        ],
        2 * 900 * 1000 * 1000, 8000000,
        *fields, yfar, ynear, zfar, znear, band_two,
        grant=32,
    )
    (input_grad,) = call(
        last_kernel,
        [((SX, SY, LANES), B16)],
        [evens, odds, columns, ((OWN_GROUPS * OWN_ROWS, 128), F32)],
        500000000, 4000000,
        pre_grad, grad, band_one,
    )
    return reduced(kept, sent, input_grad)


def solution(mesh):
    in_specs = (
        P("gx", "gy", "gz"),
        P("gx", "gy", "gz"),
        P("gx", "gy", "gz"),
        P("gx", "gy", "gz"),
        P("gx", None),
        P("gx", None),
    )
    out_specs = (P("gx", "gy", "gz"), P("gx", None), P("gx", None))
    return jax.shard_map(body, mesh=mesh, in_specs=in_specs, out_specs=out_specs, check_vma=False)
```
